32 devices in a mesh: dp: 4 (over z), row: 4 (over x, core), col: 2 (over y).
Axes of the slice: x: 2, y: 2, z: 4, core: 2. Of those that a mesh axis runs over, the one named last changes fastest.
Arguments:
- tokens: bfloat16 [11664, 1152], P(('dp', 'col'), 'row'), may hold values from -6 to 6
- ln_gain: bfloat16 [2, 1152], P(None, 'row'), may hold values from 0.5 to 1.5
- ln_bias: bfloat16 [2, 1152], P(None, 'row'), may hold values from -3 to 3
- w_qkv: bfloat16 [1152, 3, 1152], P('row', None, 'col'), may hold values from -0.1875 to 0.1875
- b_qv: bfloat16 [2, 1152], P(None, 'col'), may hold values from -3 to 3
- w_out: bfloat16 [1152, 1152], P('col', 'row'), may hold values from -3 to 3
- b_out: bfloat16 [1152], P('row'), may hold values from -3 to 3
- w_up: bfloat16 [1152, 4304], P('row', 'col'), may hold values from -0.1875 to 0.1875
- b_up: bfloat16 [4304], P('col'), may hold values from -3 to 3
- w_down: bfloat16 [4304, 1152], P('col', 'row'), may hold values from -0.09375 to 0.09375
- b_down: bfloat16 [1152], P('row'), may hold values from -3 to 3
- cotangent: bfloat16 [11664, 1152], P(('dp', 'col'), 'row'), may hold values from -6 to 6
Outputs:
- output: bfloat16 [11664, 1152], P(('dp', 'col'), 'row')
- input_grad: bfloat16 [11664, 1152], P(('dp', 'col'), 'row')
- d_ln_gain: float32 [2, 1152], P(None, 'row')
- d_ln_bias: float32 [2, 1152], P(None, 'row')
- d_w_qkv: float32 [1152, 3, 1152], P(('row', 'dp'), None, 'col')
- d_b_qv: float32 [2, 1152], P(None, 'col')
- d_w_out: float32 [1152, 1152], P(('col', 'dp'), 'row')
- d_b_out: float32 [1152], P('row')
- d_w_up: float32 [1152, 4304], P(('row', 'dp'), 'col')
- d_b_up: float32 [4304], P('col')
- d_w_down: float32 [4304, 1152], P('col', ('row', 'dp'))
- d_b_down: float32 [1152], P('row')
The draws below stay inside these ranges and needn't reach their ends.
All inputs are finite; a program needn't handle non-finite values.
Results may differ from the reference program's by a relative error of at most 0.018.
Values may be sent and summed in bfloat16 or wider, within the bound.
A program may use at most 192 MiB of HBM per device.

```python
import jax
import jax.numpy as jnp
from jax import lax

D = 1152
HD = 72
FF = 4304
SEQ = 729
HEADS = 16
GRID_TOK = 2916
TOKENS = 11664
N_DP = 4


def steps_of(own_key, dims, cuts, least, high):
    level, own = 1.0, jax.random.fold_in(own_key, 6)
    for dim, blocks in cuts:
        steps = jnp.exp(jax.random.uniform(jax.random.fold_in(own, dim), (blocks,), jnp.float32, least / len(cuts), high / len(cuts)))
        level = level * jnp.repeat(steps, dims[dim] // blocks).reshape([-1 if axis == dim else 1 for axis in range(len(dims))])
    return level


def gaussian(key, shape, spread, most, cuts=(), held_as=jnp.bfloat16):
    values = jax.random.normal(key, shape, jnp.float32) * spread
    if len(cuts) > 0:
        values = steps_of(key, shape, cuts, -0.22, 0.18) * values
    return jnp.clip(values, min=-most, max=most).astype(held_as)


def setup_inputs(seed: int = 0) -> dict:
    arg_keys = jax.random.split(jax.random.key(seed), 13)
    return {
        "tokens": gaussian(arg_keys[0], (TOKENS, D), 1.0, 6.0, ((0, 8), (1, 4))),
        "ln_gain": jnp.clip(1.0 + 0.1 * jax.random.normal(arg_keys[1], (2, D), jnp.float32), 0.5, 1.5).astype(jnp.bfloat16),
        "ln_bias": gaussian(arg_keys[2], (2, D), 0.5, 3.0, ((1, 4),)),
        "w_qkv": gaussian(arg_keys[3], (D, 3, D), D ** -0.5, 0.1875, ((0, 4), (2, 2))),
        "b_qv": gaussian(arg_keys[4], (2, D), 0.5, 3.0, ((1, 2),)),
        "w_out": gaussian(arg_keys[5], (D, D), (max(D // 256, 1)) ** -0.5, 3.0, ((0, 2), (1, 4))),
        "b_out": gaussian(arg_keys[6], (D,), 0.5, 3.0, ((0, 4),)),
        "w_up": gaussian(arg_keys[7], (D, FF), D ** -0.5, 0.1875, ((0, 4), (1, 2))),
        "b_up": gaussian(arg_keys[8], (FF,), 0.5, 3.0, ((0, 2),)),
        "w_down": gaussian(arg_keys[9], (FF, D), FF ** -0.5, 0.09375, ((0, 2), (1, 4))),
        "b_down": gaussian(arg_keys[10], (D,), 0.5, 3.0, ((0, 4),)),
        "cotangent": gaussian(arg_keys[11], (TOKENS, D), 1.0, 6.0, ((0, 8), (1, 4))),
    }


@jax.custom_vjp
def low(v):
    return lax.optimization_barrier(v.astype(jnp.bfloat16)).astype(jnp.float32)

@jax.custom_vjp
def low_back(v):
    return v

def low_keep(v):
    return (low(v), None)

def low_pass(kept, grad):
    return (grad,)

def back_keep(v):
    return (v, None)

def back_low(kept, grad):
    return (low(grad),)
low.defvjp(low_keep, low_pass)
low_back.defvjp(back_keep, back_low)

def matmul(left, right):
    return jnp.dot(left, right, precision=lax.Precision.HIGHEST, preferred_element_type=jnp.float32)

def layer_norm(values, gain, shift):
    row_mean = lax.optimization_barrier(jnp.mean(values, axis=-1, keepdims=True))
    center = values - row_mean
    variance = lax.optimization_barrier(jnp.mean(center * center, axis=-1, keepdims=True))
    return center * lax.rsqrt(variance + 1e-06) * gain + shift

def gelu_tanh(values):
    return 0.5 * values * (1.0 + jnp.tanh(0.7978845608028654 * (values + 0.044715 * values * values * values)))

def attend_image(image_block):
    queries, keys_in, values = image_block
    query_heads = queries.reshape(SEQ, HEADS, HD)
    key_heads = keys_in.reshape(SEQ, HEADS, HD)
    value_heads = values.reshape(SEQ, HEADS, HD)
    scores = low_back(jnp.einsum('qhd,khd->hqk', query_heads, key_heads, precision=lax.Precision.HIGHEST) * HD ** (-0.5))
    weights = low(jax.nn.softmax(scores, axis=-1))
    heads_out = jnp.einsum('hqk,khd->qhd', weights, value_heads, precision=lax.Precision.HIGHEST)
    return heads_out.reshape(SEQ, D)

def encoder_layer(tokens, ln_gain, ln_bias, w_qkv, b_qv, w_out, b_out, w_up, b_up, w_down, b_down):
    first_norm = low(layer_norm(tokens, ln_gain[0], ln_bias[0]))
    bias_rows = jnp.stack([b_qv[0], jnp.zeros((D,), jnp.float32), b_qv[1]])
    triple = low(low_back(matmul(first_norm, w_qkv.reshape(D, 3 * D)).reshape(-1, 3, D) + bias_rows))
    images = tokens.shape[0] // SEQ
    heads_out = lax.map(jax.checkpoint(attend_image), (triple[:, 0].reshape(images, SEQ, D), triple[:, 1].reshape(images, SEQ, D), triple[:, 2].reshape(images, SEQ, D)))
    heads_out = low(low_back(heads_out.reshape(-1, D)))
    residual = tokens + low_back(matmul(heads_out, w_out) + b_out)
    second_norm = low(layer_norm(residual, ln_gain[1], ln_bias[1]))
    up_value = low_back(matmul(second_norm, w_up) + b_up)
    hidden_act = low(gelu_tanh(up_value))
    return residual + low_back(matmul(hidden_act, w_down) + b_down)

def reference(tokens, ln_gain, ln_bias, w_qkv, b_qv, w_out, b_out, w_up, b_up, w_down, b_down, cotangent):
    params = tuple((argument.astype(jnp.float32) for argument in (ln_gain, ln_bias, w_qkv, b_qv, w_out, b_out, w_up, b_up, w_down, b_down)))
    token_groups = tokens.astype(jnp.float32).reshape(N_DP, GRID_TOK, D)
    grad_groups = cotangent.astype(jnp.float32).reshape(N_DP, GRID_TOK, D)

    def one_group(running, group_pair):
        token_block, grad_block = group_pair
        layer_out, pullback = jax.vjp(encoder_layer, token_block, *params)
        gradient_set = pullback(grad_block)
        running = tuple((summed + latest for summed, latest in zip(running, gradient_set[1:])))
        return (running, (layer_out.astype(jnp.bfloat16), gradient_set[0].astype(jnp.bfloat16)))
    start_sums = tuple((jnp.zeros_like(argument) for argument in params))
    param_grads, (outputs, input_grads) = lax.scan(one_group, start_sums, (token_groups, grad_groups))
    return (outputs.reshape(TOKENS, D), input_grads.reshape(TOKENS, D), param_grads[0], param_grads[1], param_grads[2], param_grads[3], param_grads[4], param_grads[5], param_grads[6], param_grads[7], param_grads[8], param_grads[9])
```

```python
import jax
import jax.numpy as jnp
from jax import lax
from jax.sharding import PartitionSpec as P

HD = 72
SEQ = 729
EPS = 1e-06
BF = jnp.bfloat16
F32 = jnp.float32
AX = ("row", "col")


def pairs(rule):
    out = []
    for row in range(4):
        for col in range(2):
            dest = rule(row // 2, row % 2, col)
            if dest is not None:
                out.append((row * 2 + col, (2 * dest[0] + dest[1]) * 2 + dest[2]))
    return out


TO_X = pairs(lambda x, k, y: (1 - x, k, y))
TO_CORE = pairs(lambda x, k, y: (x, 1 - k, y))
ALPHA = pairs(lambda x, k, y: (1 - x, y, y) if k == y else (x, y, 1 - y))
BETA = pairs(lambda x, k, y: (x, y, 1 - y) if k == y else (1 - x, y, y))
GAMMA = pairs(lambda x, k, y: None if k == y else (x, y, y))
RELAY_Y = pairs(lambda x, k, y: (x, k, 1 - y) if k == y else None)
RELAY_X = pairs(lambda x, k, y: None if k == y else (1 - x, k, y))
B_TO_A = pairs(lambda x, k, y: None if k == y else (x, k, 1 - y))
A_TO_A = pairs(lambda x, k, y: (1 - x, k, y) if k == y else None)
A_TO_CORE = pairs(lambda x, k, y: (x, 1 - k, y) if k == y else None)


def send(value, route):
    return lax.ppermute(value, AX, route)


def nn(a, b):
    return jnp.dot(a, b, preferred_element_type=F32)


def nt(a, b):
    return lax.dot_general(a, b, (((1,), (1,)), ((), ())), preferred_element_type=F32)


def tn(a, b):
    return lax.dot_general(a, b, (((0,), (0,)), ((), ())), preferred_element_type=F32)


def gather_weight(block, is_a, k, rows):
    alpha = send(block, ALPHA)
    beta = send(block, BETA)
    gamma = send(block, GAMMA)
    via_y = send(alpha, RELAY_Y)
    via_x = send(alpha, RELAY_X)
    bias = jnp.where(is_a, block[rows:], alpha[rows:])
    u0 = jnp.where(is_a, block[:rows], beta[:rows])
    u1 = jnp.where(is_a, gamma[:rows], alpha[:rows])
    u2 = jnp.where(is_a, alpha[:rows], via_y[:rows])
    u3 = jnp.where(is_a, beta[:rows], via_x[:rows])
    low = k == 0
    whole = jnp.concatenate(
        [jnp.where(low, u0, u1), jnp.where(low, u1, u0), jnp.where(low, u2, u3), jnp.where(low, u3, u2)], axis=0
    )
    return whole, bias


def reduce_grad(grad, is_a, k):
    grad = grad.astype(BF)
    rows = grad.shape[0] // 4
    own0, own1 = grad[:rows], grad[rows : 2 * rows]
    oth0, oth1 = grad[2 * rows : 3 * rows], grad[3 * rows :]
    rx1 = send(oth0, TO_X).astype(F32)
    ryo = send(oth1, B_TO_A).astype(F32)
    ryw = send(own1, B_TO_A).astype(F32)
    rx2 = send((oth1.astype(F32) + ryo).astype(BF), A_TO_A).astype(F32)
    mid0 = own0.astype(F32) + rx1
    ry2 = send(mid0.astype(BF), B_TO_A).astype(F32)
    f0 = mid0 + ry2
    f1 = own1.astype(F32) + ryw + rx2
    low = k == 0
    away = jnp.where(low, f1, f0).astype(BF)
    stay = jnp.where(low, f0, f1).astype(BF)
    back = send(away, A_TO_CORE)
    return jnp.where(is_a, stay, back)


def spread(block, x, k, y_unused=None):
    first, second = block[: block.shape[0] // 2], block[block.shape[0] // 2 :]
    mine = jnp.where(x == 0, first, second)
    other = jnp.where(x == 0, second, first)
    return mine, other


def whole_rows(mine, got, k):
    pm = send(mine, TO_CORE)
    pg = send(got, TO_CORE)
    low = k == 0
    return jnp.concatenate(
        [jnp.where(low, mine, pm), jnp.where(low, pm, mine), jnp.where(low, got, pg), jnp.where(low, pg, got)], axis=1
    )


def norm_forward(values, gain, shift):
    mean = jnp.mean(values, axis=1, keepdims=True)
    center = values - mean
    scale = lax.rsqrt(jnp.mean(center * center, axis=1, keepdims=True) + EPS)
    normed = center * scale
    return normed, scale, normed * gain + shift


def norm_backward(incoming, normed, scale, gain):
    e = incoming * gain
    back = scale * (
        e - jnp.mean(e, axis=1, keepdims=True) - normed * jnp.mean(e * normed, axis=1, keepdims=True)
    )
    return back, jnp.sum(incoming * normed, axis=0), jnp.sum(incoming, axis=0)


def gelu_parts(u):
    t = jnp.tanh(0.7978845608028654 * (u + 0.044715 * u * u * u))
    value = 0.5 * u * (1.0 + t)
    slope = 0.5 * (1.0 + t) + 0.5 * u * (1.0 - t * t) * 0.7978845608028654 * (1.0 + 3 * 0.044715 * u * u)
    return value, slope


def home(partial, base, x, k):
    w = partial.shape[1] // 4
    low = k == 0
    part = partial.astype(BF)
    c0, c1, c2, c3 = (part[:, j * w : (j + 1) * w] for j in range(4))
    away = send(jnp.concatenate([jnp.where(low, c1, c0), jnp.where(low, c3, c2)], axis=0), TO_CORE).astype(F32)

    def keep(a, j):
        return jnp.where(low, a[:, j * w : (j + 1) * w], a[:, (j + 1) * w : (j + 2) * w])

    rows = partial.shape[0]
    mine = (keep(base, 0) + keep(partial, 0) + away[:rows]).astype(BF)
    theirs = (keep(base, 2) + keep(partial, 2) + away[rows:]).astype(BF)
    got = send(theirs, TO_X)
    return jnp.concatenate([jnp.where(x == 0, mine, got), jnp.where(x == 0, got, mine)], axis=0)


def shards(tokens, ln_gain, ln_bias, w_qkv, b_qv, w_out, b_out, w_up, b_up, w_down, b_down, cotangent):
    row, y = lax.axis_index("row"), lax.axis_index("col")
    x, k = row // 2, row % 2
    is_a = k == y
    width = tokens.shape[1]
    hw = b_qv.shape[1]
    heads = hw // HD

    extra = jnp.concatenate(
        [ln_gain, ln_bias, b_out[None], b_down[None], jnp.zeros((1, width), BF)], axis=0
    )
    mine, other = spread(tokens, x, k)
    got = send(other, TO_X)
    ex_got = send(extra, TO_X)
    tok = whole_rows(jnp.concatenate([mine, extra], axis=0), jnp.concatenate([got, ex_got], axis=0), k)
    vec = tok[SEQ:].astype(F32)
    xin = tok[:SEQ].astype(F32)
    g1, g2, s1, s2, bo, bd = (vec[j] for j in range(6))

    qblock = jnp.concatenate(
        [
            w_qkv.reshape(width, 3 * hw),
            jnp.concatenate([b_qv[0], jnp.zeros_like(b_qv[0]), b_qv[1]])[None],
            jnp.zeros((15, 3 * hw), BF),
        ],
        axis=0,
    )
    gq, bq = gather_weight(qblock, is_a, k, width)
    go, _ = gather_weight(w_out.T, is_a, k, width)
    ublock = jnp.concatenate([w_up, b_up[None], jnp.zeros((15, w_up.shape[1]), BF)], axis=0)
    gu, bu = gather_weight(ublock, is_a, k, width)
    gd, _ = gather_weight(w_down.T, is_a, k, width)

    cm, co = spread(cotangent, x, k)
    dy = whole_rows(cm, send(co, TO_X), k)

    n1, sc1, f1 = norm_forward(xin, g1, s1)
    f1 = f1.astype(BF)
    qkv = (nn(f1, gq) + bq[0].astype(F32)).astype(BF)
    q, kk, v = (qkv[:, j * hw : (j + 1) * hw].reshape(SEQ, heads, HD).transpose(1, 0, 2) for j in range(3))
    scores = jnp.einsum("hqd,hkd->hqk", q, kk, preferred_element_type=F32) * HD ** (-0.5)
    top = jnp.max(scores, axis=-1, keepdims=True)
    ex = jnp.exp(scores - top)
    tot = jnp.sum(ex, axis=-1, keepdims=True)
    lse = top + jnp.log(tot)
    ho = jnp.einsum("hqk,hkd->hqd", (ex / tot).astype(BF), v, preferred_element_type=F32).astype(BF)
    hflat = ho.transpose(1, 0, 2).reshape(SEQ, hw)
    part = nt(hflat, go)
    residual = xin + bo + part + send(part.astype(BF), TO_CORE).astype(F32)
    n2, sc2, f2 = norm_forward(residual, g2, s2)
    f2 = f2.astype(BF)
    up = nn(f2, gu) + bu[0].astype(F32)
    hidden, slope = gelu_parts(up)
    hidden = hidden.astype(BF)
    gdown = reduce_grad(tn(dy, hidden), is_a, k)
    output = home(nt(hidden, gd), residual + bd, x, k)

    dyf = dy.astype(F32)
    dup = (nn(dy, gd) * slope).astype(BF)
    gup = reduce_grad(tn(f2, dup), is_a, k)
    dpart = nt(dup, gu)
    dsec = dpart + send(dpart.astype(BF), TO_CORE).astype(F32)
    back2, dg2, ds2 = norm_backward(dsec, n2, sc2, g2)
    dres = dyf + back2
    dbr = dres.astype(BF)
    gout = reduce_grad(tn(dbr, hflat), is_a, k)
    dh = nn(dbr, go).astype(BF).reshape(SEQ, heads, HD).transpose(1, 0, 2)
    p = jnp.exp(scores - lse)
    dv = jnp.einsum("hqk,hqd->hkd", p.astype(BF), dh, preferred_element_type=F32)
    dp = jnp.einsum("hqd,hkd->hqk", dh, v, preferred_element_type=F32)
    dsc = (p * (dp - jnp.sum(p * dp, axis=-1, keepdims=True))).astype(BF)
    dq = jnp.einsum("hqk,hkd->hqd", dsc, kk, preferred_element_type=F32) * HD ** (-0.5)
    dk = jnp.einsum("hqk,hqd->hkd", dsc, q, preferred_element_type=F32) * HD ** (-0.5)
    dqkv = jnp.concatenate([a.astype(BF).transpose(1, 0, 2).reshape(SEQ, hw) for a in (dq, dk, dv)], axis=1)
    gqkv = reduce_grad(tn(f1, dqkv), is_a, k)
    fpart = nt(dqkv, gq)
    dfirst = fpart + send(fpart.astype(BF), TO_CORE).astype(F32)
    back1, dg1, ds1 = norm_backward(dfirst, n1, sc1, g1)
    gin = (dres + back1).astype(BF)
    w = width
    low = k == 0

    def pick(a, j):
        return jnp.where(low, a[:, j * w : (j + 1) * w], a[:, (j + 1) * w : (j + 2) * w])

    gmine, gtheirs = pick(gin, 0), pick(gin, 2)
    ggot = send(gtheirs, TO_X)
    input_grad = jnp.concatenate([jnp.where(x == 0, gmine, ggot), jnp.where(x == 0, ggot, gmine)], axis=0)

    dbo = jnp.sum(dbr.astype(F32), axis=0)
    dbd = jnp.sum(dyf, axis=0)
    rowvec = jnp.stack([dg1, dg2, ds1, ds2, dbo, dbd])
    rowvec = jnp.where(x == 0, rowvec, jnp.roll(rowvec, 2 * w, axis=1)) * jnp.where(k == 0, 1.0, 0.0)
    colvec = jnp.concatenate(
        [jnp.sum(dqkv[:, :hw].astype(F32), axis=0), jnp.sum(dqkv[:, 2 * hw :].astype(F32), axis=0),
         jnp.sum(dup.astype(F32), axis=0)]
    )
    colvec = jnp.concatenate([jnp.where(low, colvec, 0.0), jnp.where(low, 0.0, colvec)])
    total = lax.psum(jnp.concatenate([rowvec.reshape(-1), colvec]), ("dp", "row", "col"))
    rv = lax.dynamic_slice_in_dim(total[: 24 * w].reshape(6, 4 * w), row * w, w, 1)
    cv = lax.dynamic_slice_in_dim(total[24 * w :], y * colvec.shape[0] // 2, colvec.shape[0] // 2, 0)

    def over_dp(a, dim):
        return lax.psum_scatter(a, "dp", scatter_dimension=dim, tiled=True).astype(F32)

    t_qkv = over_dp(gqkv, 0)
    return (
        output,
        input_grad,
        rv[0:2],
        rv[2:4],
        t_qkv.reshape(-1, 3, hw),
        cv[: 2 * hw].reshape(2, hw),
        over_dp(gout, 1).T,
        rv[4],
        over_dp(gup, 0),
        cv[2 * hw :],
        over_dp(gdown, 0).T,
        rv[5],
    )


def solution(mesh):
    placed = (
        P(("dp", "col"), "row"),
        P(None, "row"),
        P(None, "row"),
        P("row", None, "col"),
        P(None, "col"),
        P("col", "row"),
        P("row"),
        P("row", "col"),
        P("col"),
        P("col", "row"),
        P("row"),
        P(("dp", "col"), "row"),
    )
    return jax.shard_map(
        shards,
        mesh=mesh,
        in_specs=placed,
        out_specs=(
            P(("dp", "col"), "row"),
            P(("dp", "col"), "row"),
            P(None, "row"),
            P(None, "row"),
            P(("row", "dp"), None, "col"),
            P(None, "col"),
            P(("col", "dp"), "row"),
            P("row"),
            P(("row", "dp"), "col"),
            P("col"),
            P("col", ("row", "dp")),
            P("row"),
        ),
        check_vma=False,
    )
```

```python
import jax
import jax.numpy as jnp
from jax import lax
from jax.experimental import pallas as pl
from jax.experimental.pallas import tpu as pltpu
from jax.sharding import PartitionSpec as P

HD = 72
SEQ = 729
EPS = 1e-06
BF = jnp.bfloat16
F32 = jnp.float32
AX = ("row", "col")


def pairs(rule):
    out = []
    for row in range(4):
        for col in range(2):
            dest = rule(row // 2, row % 2, col)
            if dest is not None:
                out.append((row * 2 + col, (2 * dest[0] + dest[1]) * 2 + dest[2]))
    return out


TO_X = pairs(lambda x, k, y: (1 - x, k, y))
TO_CORE = pairs(lambda x, k, y: (x, 1 - k, y))
ALPHA = pairs(lambda x, k, y: (1 - x, y, y) if k == y else (x, y, 1 - y))
BETA = pairs(lambda x, k, y: (x, y, 1 - y) if k == y else (1 - x, y, y))
GAMMA = pairs(lambda x, k, y: None if k == y else (x, y, y))
RELAY_Y = pairs(lambda x, k, y: (x, k, 1 - y) if k == y else None)
RELAY_X = pairs(lambda x, k, y: None if k == y else (1 - x, k, y))
B_TO_A = pairs(lambda x, k, y: None if k == y else (x, k, 1 - y))
A_TO_A = pairs(lambda x, k, y: (1 - x, k, y) if k == y else None)
A_TO_CORE = pairs(lambda x, k, y: (x, 1 - k, y) if k == y else None)


def send(value, route):
    return lax.ppermute(value, AX, route)


def nn(a, b):
    return jnp.dot(a, b, preferred_element_type=F32)


def nt(a, b):
    return lax.dot_general(a, b, (((1,), (1,)), ((), ())), preferred_element_type=F32)


def tn(a, b):
    return lax.dot_general(a, b, (((0,), (0,)), ((), ())), preferred_element_type=F32)


def gather_weight(block, is_a, k, rows):
    alpha = send(block, ALPHA)
    beta = send(block, BETA)
    gamma = send(block, GAMMA)
    via_y = send(alpha, RELAY_Y)
    via_x = send(alpha, RELAY_X)
    bias = jnp.where(is_a, block[rows:], alpha[rows:])
    u0 = jnp.where(is_a, block[:rows], beta[:rows])
    u1 = jnp.where(is_a, gamma[:rows], alpha[:rows])
    u2 = jnp.where(is_a, alpha[:rows], via_y[:rows])
    u3 = jnp.where(is_a, beta[:rows], via_x[:rows])
    low = k == 0
    whole = jnp.concatenate(
        [jnp.where(low, u0, u1), jnp.where(low, u1, u0), jnp.where(low, u2, u3), jnp.where(low, u3, u2)], axis=0
    )
    return whole, bias


def reduce_grad(grad, is_a, k):
    grad = grad.astype(BF)
    rows = grad.shape[0] // 4
    own0, own1 = grad[:rows], grad[rows : 2 * rows]
    oth0, oth1 = grad[2 * rows : 3 * rows], grad[3 * rows :]
    rx1 = send(oth0, TO_X).astype(F32)
    ryo = send(oth1, B_TO_A).astype(F32)
    ryw = send(own1, B_TO_A).astype(F32)
    rx2 = send((oth1.astype(F32) + ryo).astype(BF), A_TO_A).astype(F32)
    mid0 = own0.astype(F32) + rx1
    ry2 = send(mid0.astype(BF), B_TO_A).astype(F32)
    f0 = mid0 + ry2
    f1 = own1.astype(F32) + ryw + rx2
    low = k == 0
    away = jnp.where(low, f1, f0).astype(BF)
    stay = jnp.where(low, f0, f1).astype(BF)
    back = send(away, A_TO_CORE)
    return jnp.where(is_a, stay, back)


def spread(block, x, k, y_unused=None):
    first, second = block[: block.shape[0] // 2], block[block.shape[0] // 2 :]
    mine = jnp.where(x == 0, first, second)
    other = jnp.where(x == 0, second, first)
    return mine, other


def whole_rows(mine, got, k):
    pm = send(mine, TO_CORE)
    pg = send(got, TO_CORE)
    low = k == 0
    return jnp.concatenate(
        [jnp.where(low, mine, pm), jnp.where(low, pm, mine), jnp.where(low, got, pg), jnp.where(low, pg, got)], axis=1
    )


def norm_forward(values, gain, shift):
    mean = jnp.mean(values, axis=1, keepdims=True)
    center = values - mean
    scale = lax.rsqrt(jnp.mean(center * center, axis=1, keepdims=True) + EPS)
    normed = center * scale
    return normed, scale, normed * gain + shift


def norm_backward(incoming, normed, scale, gain):
    e = incoming * gain
    back = scale * (
        e - jnp.mean(e, axis=1, keepdims=True) - normed * jnp.mean(e * normed, axis=1, keepdims=True)
    )
    return back, jnp.sum(incoming * normed, axis=0), jnp.sum(incoming, axis=0)


def gelu_parts(u):
    t = jnp.tanh(0.7978845608028654 * (u + 0.044715 * u * u * u))
    value = 0.5 * u * (1.0 + t)
    slope = 0.5 * (1.0 + t) + 0.5 * u * (1.0 - t * t) * 0.7978845608028654 * (1.0 + 3 * 0.044715 * u * u)
    return value, slope


def home(partial, base, x, k):
    w = partial.shape[1] // 4
    low = k == 0
    part = partial.astype(BF)
    c0, c1, c2, c3 = (part[:, j * w : (j + 1) * w] for j in range(4))
    away = send(jnp.concatenate([jnp.where(low, c1, c0), jnp.where(low, c3, c2)], axis=0), TO_CORE).astype(F32)

    def keep(a, j):
        return jnp.where(low, a[:, j * w : (j + 1) * w], a[:, (j + 1) * w : (j + 2) * w])

    rows = partial.shape[0]
    mine = (keep(base, 0) + keep(partial, 0) + away[:rows]).astype(BF)
    theirs = (keep(base, 2) + keep(partial, 2) + away[rows:]).astype(BF)
    got = send(theirs, TO_X)
    return jnp.concatenate([jnp.where(x == 0, mine, got), jnp.where(x == 0, got, mine)], axis=0)


MESH = pl.DeviceIdType.MESH
PADS = 736
VMEM_CAP = 66_000_000


def place():
    row, col = lax.axis_index("row"), lax.axis_index("col")
    return row // 2, lax.rem(row, 2), col


def at(x, k, y):
    return {"row": 2 * x + k, "col": y}


def greet(peers):
    barrier = pltpu.get_barrier_semaphore()
    for peer in peers:
        pl.semaphore_signal(barrier, inc=1, device_id=peer, device_id_type=MESH)
    pl.semaphore_wait(barrier, len(peers))


def chunks(total, step, body):
    whole = total // step
    if whole > 0:
        lax.fori_loop(0, whole, lambda i, c: (body(pl.multiple_of(i * step, step), step), c)[1], 0)
    if total % step:
        body(whole * step, total % step)


def forward_kernel(
    tok, cot, bias, wq, wo, wu, wd,
    gq, go, gu, gd, xb, dyb, bv, f1, qkv, hflat, lse, residual, f2, hidden, slope,
    tbuf, cbuf, gqv, gov, guv, qh, psend, precv,
    ssem, rsem, csem, lsem, wsend, wrecv,
):
    x, k, y = place()
    is_a, is_b = k == y, k != y
    heads = hflat.shape[1] // HD
    hw = hflat.shape[1]
    width = tok.shape[2]
    greet([at(x, 1 - k, y), at(1 - x, k, y), at(1 - x, 1 - k, y), at(x, k, 1 - y), at(x, 1 - k, 1 - y)])

    def remote(src, dst, s, r, dest):
        return pltpu.make_async_remote_copy(
            src_ref=src, dst_ref=dst, send_sem=s, recv_sem=r, device_id=dest, device_id_type=MESH
        )

    blocks, wholes = (wq, wo, wu, wd), (gq, go, gu, gd)

    def own_sends(w):
        b, g = blocks[w], wholes[w]
        a = [
            remote(b, g.at[2 + k], wsend.at[w, 0], wrecv.at[w, 2 + k], at(1 - x, k, y)),
            remote(b, g.at[k], wsend.at[w, 1], wrecv.at[w, k], at(x, k, 1 - y)),
        ]
        bb = [
            remote(b, g.at[2 + k], wsend.at[w, 0], wrecv.at[w, 2 + k], at(1 - x, 1 - k, y)),
            remote(b, g.at[k], wsend.at[w, 1], wrecv.at[w, k], at(x, 1 - k, 1 - y)),
            remote(b, g.at[k], wsend.at[w, 2], wrecv.at[w, k], at(x, 1 - k, y)),
        ]
        return a, bb

    def relays(w):
        g = wholes[w]
        return (
            remote(g.at[2], g.at[2], wsend.at[w, 3], wrecv.at[w, 2], at(x, k, 1 - y)),
            remote(g.at[1], g.at[3], wsend.at[w, 3], wrecv.at[w, 3], at(1 - x, k, y)),
        )

    def both(fa, fb):
        pl.when(is_a)(fa)
        pl.when(is_b)(fb)

    def start_own(w):
        a, b = own_sends(w)
        both(lambda: [c.start() for c in a] and None, lambda: [c.start() for c in b] and None)

    def arrived(w, j):
        remote(blocks[w], wholes[w].at[j], wsend.at[w, 0], wrecv.at[w, j], at(x, 1 - k, y)).wait_recv()

    def start_relay(w):
        ra, rb = relays(w)

        def fa():
            arrived(w, 2)
            ra.start()

        def fb():
            arrived(w, 1)
            rb.start()

        both(fa, fb)

    def wait_rest(w):
        pl.when(is_b | (k == 1))(lambda: arrived(w, 0))
        pl.when(is_a & (k == 0))(lambda: arrived(w, 1))
        pl.when(is_b)(lambda: arrived(w, 2))
        arrived(w, 3)

    def finish_sends(w):
        a, b = own_sends(w)
        ra, rb = relays(w)
        both(
            lambda: [c.wait_send() for c in a + [ra]] and None,
            lambda: [c.wait_send() for c in b + [rb]] and None,
        )

    def load(w, dst):
        b, g = blocks[w], wholes[w]
        for j in range(4):
            rows = pl.ds(j * width, width)
            local = is_a & (k == j) if j < 2 else None
            if local is None:
                pltpu.make_async_copy(g.at[j], dst.at[rows], lsem.at[j]).start()
            else:
                pl.when(local)(lambda: pltpu.make_async_copy(b, dst.at[rows], lsem.at[j]).start())
                pl.when(jnp.logical_not(local))(
                    lambda: pltpu.make_async_copy(g.at[j], dst.at[rows], lsem.at[j]).start()
                )
        for j in range(4):
            pltpu.make_async_copy(g.at[j], dst.at[pl.ds(j * width, width)], lsem.at[j]).wait()

    tx = remote(tok.at[1 - x], tbuf.at[2 + k], ssem.at[0], rsem.at[0], at(1 - x, k, y))
    cx = remote(cot.at[1 - x], cbuf.at[2 + k], ssem.at[1], rsem.at[1], at(1 - x, k, y))
    t1 = remote(tok.at[x], tbuf.at[k], ssem.at[2], rsem.at[2], at(x, 1 - k, y))
    c1 = remote(cot.at[x], cbuf.at[k], ssem.at[3], rsem.at[3], at(x, 1 - k, y))
    t2 = remote(tbuf.at[2 + k], tbuf.at[2 + k], ssem.at[4], rsem.at[4], at(x, 1 - k, y))
    c2 = remote(cbuf.at[2 + k], cbuf.at[2 + k], ssem.at[5], rsem.at[5], at(x, 1 - k, y))
    bs = remote(bias, bv, ssem.at[6], rsem.at[6], at(x, k, 1 - y))
    pe = remote(psend, precv, ssem.at[7], rsem.at[7], at(x, 1 - k, y))
    tl = pltpu.make_async_copy(tok.at[x], tbuf.at[k], csem.at[0])
    cl = pltpu.make_async_copy(cot.at[x], cbuf.at[k], csem.at[1])
    bl = pltpu.make_async_copy(bias, bv, csem.at[2])

    tx.start()
    t1.start()
    tl.start()
    start_own(0)
    both(lambda: (bl.start(), bs.start()) and None, lambda: None)
    cl.start()
    c1.start()

    tx.wait_recv()
    t2.start()
    tl.wait()
    t1.wait_recv()
    t2.wait_recv()
    for j in range(4):
        xb[:, j * width : (j + 1) * width] = tbuf[j]
    vecs = xb[SEQ - 1 : PADS, :].astype(F32)
    g1, g2, s1, s2, bo = (vecs[j : j + 1] for j in range(1, 6))

    def stats(v):
        mean = jnp.mean(v, axis=1, keepdims=True)
        c = v - mean
        return c * lax.rsqrt(jnp.mean(c * c, axis=1, keepdims=True) + EPS)

    def norm1(r, n):
        f1[pl.ds(r, n), :] = (stats(xb[pl.ds(r, n), :].astype(F32)) * g1 + s1).astype(BF)

    chunks(PADS, 32, norm1)
    start_relay(0)
    start_own(1)
    both(bl.wait, bs.wait_recv)
    wait_rest(0)
    load(0, gqv)

    def project(c, n):
        cols = pl.ds(c, n)
        qkv[:, cols] = (nn(f1[...], gqv[:, cols]) + bv[0:1, cols].astype(F32)).astype(BF)

    chunks(3 * hw, 256, project)
    start_relay(1)
    start_own(2)
    qh[...] = jnp.zeros_like(qh)
    for p in range(3):
        for h in range(heads):
            lo = p * hw + h * HD
            qh[p * heads + h, :, 0:HD] = qkv[:, lo : lo + HD]
    keymask = jnp.where(lax.broadcasted_iota(jnp.int32, (PADS, 1), 0) < SEQ, 0.0, -1e30)

    def attend(h, carry):
        st = nt(qh[heads + h], qh[h]) + keymask
        top = jnp.max(st, axis=0, keepdims=True)
        e = jnp.exp((st - top) * HD ** (-0.5))
        tot = jnp.sum(e, axis=0, keepdims=True)
        lse[pl.ds(h, 1), :] = top * HD ** (-0.5) + jnp.log(tot)
        out = tn(qh[2 * heads + h], e.astype(BF)) / tot
        qh[h] = out.T.astype(BF)
        return carry

    lax.fori_loop(0, heads, attend, 0)
    for h in range(heads):
        hflat[:, h * HD : (h + 1) * HD] = qh[h, :, 0:HD]
    wait_rest(1)
    load(1, gov)

    def out_project(c, n):
        cols = pl.ds(c, n)
        part = nt(hflat[...], gov[cols, :])
        psend[:, cols] = part.astype(BF)
        residual[:, cols] = part

    chunks(4 * width, 384, out_project)
    pe.start()
    pe.wait_recv()

    def norm2(r, n):
        rows = pl.ds(r, n)
        v = xb[rows, :].astype(F32) + bo + residual[rows, :] + precv[rows, :].astype(F32)
        residual[rows, :] = v
        f2[rows, :] = (stats(v) * g2 + s2).astype(BF)

    chunks(PADS, 32, norm2)
    start_relay(2)
    start_own(3)
    cx.start()
    wait_rest(2)
    load(2, guv)

    def expand(c, n):
        cols = pl.ds(c, n)
        u = nn(f2[...], guv[:, cols]) + bv[1:2, cols].astype(F32)
        value, grad = gelu_parts(u)
        hidden[:, cols] = value.astype(BF)
        slope[:, cols] = grad.astype(BF)

    chunks(hidden.shape[1], 256, expand)
    start_relay(3)
    cx.wait_recv()
    c2.start()
    cl.wait()
    c1.wait_recv()
    c2.wait_recv()
    for j in range(4):
        dyb[:, j * width : (j + 1) * width] = cbuf[j]
    wait_rest(3)
    for c in (tx, cx, t1, c1, t2, c2, pe):
        c.wait_send()
    both(bs.wait_send, lambda: None)
    for w in range(4):
        finish_sends(w)


def forward(tok, cot, bias, wq, wo, wu, wd):
    width, hw, ff = tok.shape[2], wo.shape[1], wu.shape[1]
    full = 4 * width
    heads = hw // HD
    anyspec = pl.BlockSpec(memory_space=pl.ANY)
    vspec = pl.BlockSpec(memory_space=pltpu.VMEM)
    shape = jax.ShapeDtypeStruct
    outs = [
        shape((4,) + wq.shape, BF), shape((4,) + wo.shape, BF), shape((4,) + wu.shape, BF), shape((4,) + wd.shape, BF),
        shape((PADS, full), BF), shape((PADS, full), BF), shape(bias.shape, BF), shape((PADS, full), BF),
        shape((PADS, 3 * hw), BF), shape((PADS, hw), BF), shape((heads, PADS), F32), shape((PADS, full), F32),
        shape((PADS, full), BF), shape((PADS, ff), BF), shape((PADS, ff), BF),
    ]
    dma = pltpu.SemaphoreType.DMA
    return pl.pallas_call(
        forward_kernel,
        out_shape=outs,
        in_specs=[anyspec] * 7,
        out_specs=[anyspec] * 4 + [vspec] * 11,
        scratch_shapes=[
            pltpu.VMEM((4, PADS, width), BF), pltpu.VMEM((4, PADS, width), BF),
            pltpu.VMEM((full, 3 * hw), BF), pltpu.VMEM((full, hw), BF), pltpu.VMEM((full, ff), BF),
            pltpu.VMEM((3 * heads, PADS, 128), BF), pltpu.VMEM((PADS, full), BF), pltpu.VMEM((PADS, full), BF),
            dma((8,)), dma((8,)), dma((3,)), dma((4,)), dma((4, 4)), dma((4, 4)),
        ],
        compiler_params=pltpu.CompilerParams(collective_id=0, has_side_effects=True, vmem_limit_bytes=VMEM_CAP),
        name="forward",
    )(tok, cot, bias, wq, wo, wu, wd)


def shards(tokens, ln_gain, ln_bias, w_qkv, b_qv, w_out, b_out, w_up, b_up, w_down, b_down, cotangent):
    row, y = lax.axis_index("row"), lax.axis_index("col")
    x, k = row // 2, row % 2
    is_a = k == y
    width = tokens.shape[1]
    hw = b_qv.shape[1]
    heads = hw // HD

    extra = jnp.concatenate(
        [ln_gain, ln_bias, b_out[None], b_down[None], jnp.zeros((1, width), BF)], axis=0
    )
    images = tokens.shape[0] // SEQ
    tok2 = jnp.concatenate([tokens.reshape(images, SEQ, width), jnp.stack([extra] * images)], axis=1)
    cot2 = jnp.pad(cotangent.reshape(images, SEQ, width), ((0, 0), (0, PADS - SEQ), (0, 0)))
    ff = b_up.shape[0]
    bias = jnp.zeros((16, ff), BF)
    bias = bias.at[0, :hw].set(b_qv[0]).at[0, 2 * hw : 3 * hw].set(b_qv[1]).at[1].set(b_up)
    gq, go, gu, gd, xb, dy, bv, f1, qkv, hflat, lse, residual, f2, hidden, slope = forward(
        tok2, cot2, bias, w_qkv.reshape(width, 3 * hw), w_out.T, w_up, w_down.T
    )

    def whole(g, own):
        j = lax.broadcasted_iota(jnp.int32, (4, 1, 1), 0)
        return jnp.where(is_a & (j == k), own[None], g).reshape(4 * width, own.shape[1])

    gq = whole(gq, w_qkv.reshape(width, 3 * hw))
    go, gu, gd = whole(go, w_out.T), whole(gu, w_up), whole(gd, w_down.T)
    vec = xb[SEQ:].astype(F32)
    g1, g2, s1, s2, bo, bd = (vec[j] for j in range(6))
    xb, dy, f1, qkv, hflat, lse, residual, f2, hidden, slope = (
        xb[:SEQ], dy[:SEQ], f1[:SEQ], qkv[:SEQ], hflat[:SEQ], lse[:, :SEQ], residual[:SEQ], f2[:SEQ], hidden[:SEQ], slope[:SEQ])
    n1, sc1, _ = norm_forward(xb.astype(F32), g1, s1)
    n2, sc2, _ = norm_forward(residual, g2, s2)
    q, kk, v = (qkv[:, j * hw : (j + 1) * hw].reshape(SEQ, heads, HD).transpose(1, 0, 2) for j in range(3))
    scores = jnp.einsum("hqd,hkd->hqk", q, kk, preferred_element_type=F32) * HD ** (-0.5)
    lse = lse[:, :, None]
    gdown = reduce_grad(tn(dy, hidden), is_a, k)
    output = home(nt(hidden, gd), residual + bd, x, k)

    dyf = dy.astype(F32)
    dup = (nn(dy, gd) * slope).astype(BF)
    gup = reduce_grad(tn(f2, dup), is_a, k)
    dpart = nt(dup, gu)
    dsec = dpart + send(dpart.astype(BF), TO_CORE).astype(F32)
    back2, dg2, ds2 = norm_backward(dsec, n2, sc2, g2)
    dres = dyf + back2
    dbr = dres.astype(BF)
    gout = reduce_grad(tn(dbr, hflat), is_a, k)
    dh = nn(dbr, go).astype(BF).reshape(SEQ, heads, HD).transpose(1, 0, 2)
    p = jnp.exp(scores - lse)
    dv = jnp.einsum("hqk,hqd->hkd", p.astype(BF), dh, preferred_element_type=F32)
    dp = jnp.einsum("hqd,hkd->hqk", dh, v, preferred_element_type=F32)
    dsc = (p * (dp - jnp.sum(p * dp, axis=-1, keepdims=True))).astype(BF)
    dq = jnp.einsum("hqk,hkd->hqd", dsc, kk, preferred_element_type=F32) * HD ** (-0.5)
    dk = jnp.einsum("hqk,hqd->hkd", dsc, q, preferred_element_type=F32) * HD ** (-0.5)
    dqkv = jnp.concatenate([a.astype(BF).transpose(1, 0, 2).reshape(SEQ, hw) for a in (dq, dk, dv)], axis=1)
    gqkv = reduce_grad(tn(f1, dqkv), is_a, k)
    fpart = nt(dqkv, gq)
    dfirst = fpart + send(fpart.astype(BF), TO_CORE).astype(F32)
    back1, dg1, ds1 = norm_backward(dfirst, n1, sc1, g1)
    gin = (dres + back1).astype(BF)
    w = width
    low = k == 0

    def pick(a, j):
        return jnp.where(low, a[:, j * w : (j + 1) * w], a[:, (j + 1) * w : (j + 2) * w])

    gmine, gtheirs = pick(gin, 0), pick(gin, 2)
    ggot = send(gtheirs, TO_X)
    input_grad = jnp.concatenate([jnp.where(x == 0, gmine, ggot), jnp.where(x == 0, ggot, gmine)], axis=0)

    dbo = jnp.sum(dbr.astype(F32), axis=0)
    dbd = jnp.sum(dyf, axis=0)
    rowvec = jnp.stack([dg1, dg2, ds1, ds2, dbo, dbd])
    rowvec = jnp.where(x == 0, rowvec, jnp.roll(rowvec, 2 * w, axis=1)) * jnp.where(k == 0, 1.0, 0.0)
    colvec = jnp.concatenate(
        [jnp.sum(dqkv[:, :hw].astype(F32), axis=0), jnp.sum(dqkv[:, 2 * hw :].astype(F32), axis=0),
         jnp.sum(dup.astype(F32), axis=0)]
    )
    colvec = jnp.concatenate([jnp.where(low, colvec, 0.0), jnp.where(low, 0.0, colvec)])
    total = lax.psum(jnp.concatenate([rowvec.reshape(-1), colvec]), ("dp", "row", "col"))
    rv = lax.dynamic_slice_in_dim(total[: 24 * w].reshape(6, 4 * w), row * w, w, 1)
    cv = lax.dynamic_slice_in_dim(total[24 * w :], y * colvec.shape[0] // 2, colvec.shape[0] // 2, 0)

    def over_dp(a, dim):
        return lax.psum_scatter(a, "dp", scatter_dimension=dim, tiled=True).astype(F32)

    t_qkv = over_dp(gqkv, 0)
    return (
        output,
        input_grad,
        rv[0:2],
        rv[2:4],
        t_qkv.reshape(-1, 3, hw),
        cv[: 2 * hw].reshape(2, hw),
        over_dp(gout, 1).T,
        rv[4],
        over_dp(gup, 0),
        cv[2 * hw :],
        over_dp(gdown, 0).T,
        rv[5],
    )


def solution(mesh):
    placed = (
        P(("dp", "col"), "row"),
        P(None, "row"),
        P(None, "row"),
        P("row", None, "col"),
        P(None, "col"),
        P("col", "row"),
        P("row"),
        P("row", "col"),
        P("col"),
        P("col", "row"),
        P("row"),
        P(("dp", "col"), "row"),
    )
    return jax.shard_map(
        shards,
        mesh=mesh,
        in_specs=placed,
        out_specs=(
            P(("dp", "col"), "row"),
            P(("dp", "col"), "row"),
            P(None, "row"),
            P(None, "row"),
            P(("row", "dp"), None, "col"),
            P(None, "col"),
            P(("col", "dp"), "row"),
            P("row"),
            P(("row", "dp"), "col"),
            P("col"),
            P("col", ("row", "dp")),
            P("row"),
        ),
        check_vma=False,
    )
```

```python
import jax
import jax.numpy as jnp
from jax import lax
from jax.experimental import pallas as pl
from jax.experimental.pallas import tpu as pltpu
from jax.sharding import PartitionSpec as P

HD = 72
SEQ = 729
EPS = 1e-06
BF = jnp.bfloat16
F32 = jnp.float32


def nn(a, b):
    return jnp.dot(a, b, preferred_element_type=F32)


def nt(a, b):
    return lax.dot_general(a, b, (((1,), (1,)), ((), ())), preferred_element_type=F32)


def tn(a, b):
    return lax.dot_general(a, b, (((0,), (0,)), ((), ())), preferred_element_type=F32)


def gelu_parts(u):
    t = jnp.tanh(0.7978845608028654 * (u + 0.044715 * u * u * u))
    value = 0.5 * u * (1.0 + t)
    slope = 0.5 * (1.0 + t) + 0.5 * u * (1.0 - t * t) * 0.7978845608028654 * (1.0 + 3 * 0.044715 * u * u)
    return value, slope


MESH = pl.DeviceIdType.MESH
PADS = 736
VMEM_CAP = 66_000_000


def place():
    row, col = lax.axis_index("row"), lax.axis_index("col")
    return row // 2, lax.rem(row, 2), col


def at(x, k, y):
    return {"row": 2 * x + k, "col": y}


def greet(peers):
    barrier = pltpu.get_barrier_semaphore()
    for peer in peers:
        pl.semaphore_signal(barrier, inc=1, device_id=peer, device_id_type=MESH)
    pl.semaphore_wait(barrier, len(peers))


def chunks(total, step, body):
    whole = total // step
    if whole > 0:
        lax.fori_loop(0, whole, lambda i, c: (body(pl.multiple_of(i * step, step), step), c)[1], 0)
    if total % step:
        body(whole * step, total % step)


def forward_kernel(
    tok, cot, bias, wq, wo, wu, wd,
    gq, go, gu, gd, xb, dyb, bv, f1b, qh, oh, hflat, lse, residual, f2b, hidden, slope, dd,
    tbuf, cbuf, gqv, gov, guv, f1, psend, precv,
    ssem, rsem, csem, lsem, wsend, wrecv,
):
    x, k, y = place()
    is_a, is_b = k == y, k != y
    hw = hflat.shape[1]
    heads = hw // HD
    width = tok.shape[2]
    greet([at(x, 1 - k, y), at(1 - x, k, y), at(1 - x, 1 - k, y), at(x, k, 1 - y), at(x, 1 - k, 1 - y)])

    def remote(src, dst, s, r, dest):
        return pltpu.make_async_remote_copy(
            src_ref=src, dst_ref=dst, send_sem=s, recv_sem=r, device_id=dest, device_id_type=MESH
        )

    blocks, wholes = (wq, wo, wu, wd), (gq, go, gu, gd)

    def own_sends(w):
        b, g = blocks[w], wholes[w]
        a = [
            remote(b, g.at[2 + k], wsend.at[w, 0], wrecv.at[w, 2 + k], at(1 - x, k, y)),
            remote(b, g.at[k], wsend.at[w, 1], wrecv.at[w, k], at(x, k, 1 - y)),
        ]
        bb = [
            remote(b, g.at[2 + k], wsend.at[w, 0], wrecv.at[w, 2 + k], at(1 - x, 1 - k, y)),
            remote(b, g.at[k], wsend.at[w, 1], wrecv.at[w, k], at(x, 1 - k, 1 - y)),
            remote(b, g.at[k], wsend.at[w, 2], wrecv.at[w, k], at(x, 1 - k, y)),
        ]
        return a, bb

    def relays(w):
        g = wholes[w]
        return (
            remote(g.at[2], g.at[2], wsend.at[w, 3], wrecv.at[w, 2], at(x, k, 1 - y)),
            remote(g.at[1], g.at[3], wsend.at[w, 3], wrecv.at[w, 3], at(1 - x, k, y)),
        )

    def both(fa, fb):
        pl.when(is_a)(fa)
        pl.when(is_b)(fb)

    def start_own(w):
        a, b = own_sends(w)
        both(lambda: [c.start() for c in a] and None, lambda: [c.start() for c in b] and None)

    def arrived(w, j):
        remote(blocks[w], wholes[w].at[j], wsend.at[w, 0], wrecv.at[w, j], at(x, 1 - k, y)).wait_recv()

    def start_relay(w):
        ra, rb = relays(w)

        def fa():
            arrived(w, 2)
            ra.start()

        def fb():
            arrived(w, 1)
            rb.start()

        both(fa, fb)

    def wait_rest(w):
        pl.when(is_b | (k == 1))(lambda: arrived(w, 0))
        pl.when(is_a & (k == 0))(lambda: arrived(w, 1))
        pl.when(is_b)(lambda: arrived(w, 2))
        arrived(w, 3)

    def finish_sends(w):
        a, b = own_sends(w)
        ra, rb = relays(w)
        both(
            lambda: [c.wait_send() for c in a + [ra]] and None,
            lambda: [c.wait_send() for c in b + [rb]] and None,
        )

    def load(w, dst):
        b, g = blocks[w], wholes[w]
        for j in range(4):
            rows = pl.ds(j * width, width)
            local = is_a & (k == j) if j < 2 else None
            if local is None:
                pltpu.make_async_copy(g.at[j], dst.at[rows], lsem.at[j]).start()
            else:
                pl.when(local)(lambda: pltpu.make_async_copy(b, dst.at[rows], lsem.at[j]).start())
                pl.when(jnp.logical_not(local))(
                    lambda: pltpu.make_async_copy(g.at[j], dst.at[rows], lsem.at[j]).start()
                )
        for j in range(4):
            pltpu.make_async_copy(g.at[j], dst.at[pl.ds(j * width, width)], lsem.at[j]).wait()

    tx = remote(tok.at[1 - x], tbuf.at[2 + k], ssem.at[0], rsem.at[0], at(1 - x, k, y))
    cx = remote(cot.at[1 - x], cbuf.at[2 + k], ssem.at[1], rsem.at[1], at(1 - x, k, y))
    t1 = remote(tok.at[x], tbuf.at[k], ssem.at[2], rsem.at[2], at(x, 1 - k, y))
    c1 = remote(cot.at[x], cbuf.at[k], ssem.at[3], rsem.at[3], at(x, 1 - k, y))
    t2 = remote(tbuf.at[2 + k], tbuf.at[2 + k], ssem.at[4], rsem.at[4], at(x, 1 - k, y))
    c2 = remote(cbuf.at[2 + k], cbuf.at[2 + k], ssem.at[5], rsem.at[5], at(x, 1 - k, y))
    bs = remote(bias, bv, ssem.at[6], rsem.at[6], at(x, k, 1 - y))
    pe = remote(psend, precv, ssem.at[7], rsem.at[7], at(x, 1 - k, y))
    tl = pltpu.make_async_copy(tok.at[x], tbuf.at[k], csem.at[0])
    cl = pltpu.make_async_copy(cot.at[x], cbuf.at[k], csem.at[1])
    bl = pltpu.make_async_copy(bias, bv, csem.at[2])

    tx.start()
    t1.start()
    tl.start()
    start_own(0)
    both(lambda: (bl.start(), bs.start()) and None, lambda: None)
    cl.start()
    c1.start()

    tx.wait_recv()
    t2.start()
    tl.wait()
    t1.wait_recv()
    t2.wait_recv()
    for j in range(4):
        xb[:, j * width : (j + 1) * width] = tbuf[j]
    vecs = xb[SEQ - 1 : PADS, :].astype(F32)
    g1, g2, s1, s2, bo = (vecs[j : j + 1] for j in range(1, 6))

    def stats(v):
        mean = jnp.mean(v, axis=1, keepdims=True)
        c = v - mean
        return c * lax.rsqrt(jnp.mean(c * c, axis=1, keepdims=True) + EPS)

    def norm1(r, n):
        f1[pl.ds(r, n), :] = (stats(xb[pl.ds(r, n), :].astype(F32)) * g1 + s1).astype(BF)

    chunks(PADS, 32, norm1)
    f2 = f1
    start_relay(0)
    start_own(1)
    both(bl.wait, bs.wait_recv)
    wait_rest(0)
    load(0, gqv)

    def project(c, n):
        cols = pl.ds(c, n)
        hidden[:, cols] = (nn(f1[...], gqv[:, cols]) + bv[0:1, cols].astype(F32)).astype(BF)

    chunks(gqv.shape[1], 256, project)
    start_relay(1)
    start_own(2)
    for j in range(4):
        f1b[j] = f1[:, j * width : (j + 1) * width]
    qh[...] = jnp.zeros_like(qh)
    for p in range(3):
        for h in range(heads):
            lo = p * hw + h * HD
            qh[p * heads + h, :, 0:HD] = hidden[:, lo : lo + HD]
    keymask = jnp.where(lax.broadcasted_iota(jnp.int32, (PADS, 1), 0) < SEQ, 0.0, -1e30)

    def attend(h, carry):
        st = nt(qh[heads + h], qh[h]) + keymask
        top = jnp.max(st, axis=0, keepdims=True)
        e = jnp.exp((st - top) * HD ** (-0.5))
        tot = jnp.sum(e, axis=0, keepdims=True)
        lse[pl.ds(h, 1), :] = top * HD ** (-0.5) + jnp.log(tot)
        out = tn(qh[2 * heads + h], e.astype(BF)) / tot
        oh[h] = out.T.astype(BF)
        return carry

    lax.fori_loop(0, heads, attend, 0)
    for h in range(heads):
        hflat[:, h * HD : (h + 1) * HD] = oh[h, :, 0:HD]
    wait_rest(1)
    load(1, gov)

    def out_project(c, n):
        cols = pl.ds(c, n)
        part = nt(hflat[...], gov[cols, :])
        psend[:, cols] = part.astype(BF)
        residual[:, cols] = part

    chunks(4 * width, 384, out_project)
    pe.start()
    pe.wait_recv()

    def norm2(r, n):
        rows = pl.ds(r, n)
        v = xb[rows, :].astype(F32) + bo + residual[rows, :] + precv[rows, :].astype(F32)
        residual[rows, :] = v
        f2[rows, :] = (stats(v) * g2 + s2).astype(BF)

    chunks(PADS, 32, norm2)
    start_relay(2)
    cx.start()
    start_own(3)
    wait_rest(2)
    load(2, guv)
    for j in range(4):
        f2b[j] = f2[:, j * width : (j + 1) * width]

    def expand(c, n):
        cols = pl.ds(c, n)
        u = nn(f2[...], guv[:, cols]) + bv[1:2, cols].astype(F32)
        value, grad = gelu_parts(u)
        hidden[:, cols] = value.astype(BF)
        slope[:, cols] = grad.astype(BF)

    chunks(hidden.shape[1], 256, expand)
    cx.wait_recv()
    c2.start()
    cl.wait()
    c1.wait_recv()
    c2.wait_recv()
    for j in range(4):
        dyb[:, j * width : (j + 1) * width] = cbuf[j]

    def down_grad(j, carry):
        dd[j] = tn(cbuf[j], hidden[...]).astype(BF)
        return carry

    lax.fori_loop(0, 4, down_grad, 0)
    start_relay(3)
    wait_rest(3)
    for c in (tx, cx, t1, c1, t2, c2, pe):
        c.wait_send()
    both(bs.wait_send, lambda: None)
    for w in range(4):
        finish_sends(w)


def forward(tok, cot, bias, wq, wo, wu, wd):
    width, hw, ff = tok.shape[2], wo.shape[1], wu.shape[1]
    full = 4 * width
    heads = hw // HD
    anyspec = pl.BlockSpec(memory_space=pl.ANY)
    vspec = pl.BlockSpec(memory_space=pltpu.VMEM)
    shape = jax.ShapeDtypeStruct
    outs = [
        shape((4,) + wq.shape, BF), shape((4,) + wo.shape, BF), shape((4,) + wu.shape, BF), shape((4,) + wd.shape, BF),
        shape((PADS, full), BF), shape((PADS, full), BF), shape(bias.shape, BF), shape((4, PADS, width), BF),
        shape((3 * heads, PADS, 128), BF), shape((heads, PADS, 128), BF), shape((PADS, hw), BF), shape((heads, PADS), F32),
        shape((PADS, full), F32), shape((4, PADS, width), BF), shape((PADS, ff), BF), shape((PADS, ff), BF),
        shape((4, width, ff), BF),
    ]
    dma = pltpu.SemaphoreType.DMA
    return pl.pallas_call(
        forward_kernel,
        out_shape=outs,
        in_specs=[anyspec] * 7,
        out_specs=[anyspec] * 4 + [vspec] * 13,
        scratch_shapes=[
            pltpu.VMEM((4, PADS, width), BF), pltpu.VMEM((4, PADS, width), BF),
            pltpu.VMEM((full, wq.shape[1]), BF), pltpu.VMEM((full, hw), BF), pltpu.VMEM((full, ff), BF),
            pltpu.VMEM((PADS, full), BF), pltpu.VMEM((PADS, full), BF), pltpu.VMEM((PADS, full), BF),
            dma((8,)), dma((8,)), dma((3,)), dma((4,)), dma((4, 4)), dma((4, 4)),
        ],
        compiler_params=pltpu.CompilerParams(collective_id=0, has_side_effects=True, vmem_limit_bytes=VMEM_CAP),
        name="forward",
    )(tok, cot, bias, wq, wo, wu, wd)


def load_weight(b, g, dst, sem, k, is_a):
    width = b.shape[0]
    for j in range(4):
        rows = pl.ds(j * width, width)
        if j < 2:
            local = is_a & (k == j)
            pl.when(local)(lambda: pltpu.make_async_copy(b, dst.at[rows], sem.at[j]).start())
            pl.when(jnp.logical_not(local))(lambda: pltpu.make_async_copy(g.at[j], dst.at[rows], sem.at[j]).start())
        else:
            pltpu.make_async_copy(g.at[j], dst.at[rows], sem.at[j]).start()

    def wait():
        for j in range(4):
            pltpu.make_async_copy(g.at[j], dst.at[pl.ds(j * width, width)], sem.at[j]).wait()

    return wait


def remote(src, dst, s, r, dest):
    return pltpu.make_async_remote_copy(
        src_ref=src, dst_ref=dst, send_sem=s, recv_sem=r, device_id=dest, device_id_type=MESH
    )


class Scatter:
    def __init__(self, d, r, zs, st, sb, cv, ss, rs, ls, spot):
        self.d, self.r, self.zs, self.st, self.sb, self.cv, self.ls, self.spot = d, r, zs, st, sb, cv, ls, spot
        x, k, y = spot
        self.is_a, self.is_b, self.k = k == y, k != y, k
        across, over, mate = at(1 - x, k, y), at(x, k, 1 - y), at(x, 1 - k, y)
        self.x1 = remote(d.at[2], r.at[0], ss.at[0], rs.at[0], across)
        self.y1 = remote(d.at[3], r.at[1], ss.at[1], rs.at[1], over)
        self.y1b = remote(d.at[1], r.at[2], ss.at[2], rs.at[2], over)
        self.x2 = remote(sb, r.at[3], ss.at[1], rs.at[3], across)
        self.y2 = remote(sb, r.at[4], ss.at[3], rs.at[4], over)
        self.home = remote(cv.at[1], zs, ss.at[2], rs.at[5], mate)

    def first(self):
        self.x1.start()

        def b():
            self.y1.start()
            self.y1b.start()

        pl.when(self.is_b)(b)

    def copy_in(self, pairs):
        for i, src in pairs:
            pltpu.make_async_copy(src, self.st.at[i], self.ls.at[i]).start()
        for i, src in pairs:
            pltpu.make_async_copy(src, self.st.at[i], self.ls.at[i]).wait()

    def second(self):
        st, sb = self.st, self.sb

        def fetch_a():
            self.y1.wait_recv()
            self.copy_in([(0, self.d.at[3]), (1, self.r.at[1])])

        def fetch_b():
            self.x1.wait_recv()
            self.copy_in([(0, self.d.at[0]), (1, self.r.at[0])])

        pl.when(self.is_a)(fetch_a)
        pl.when(self.is_b)(fetch_b)

        def add(c, n):
            cols = pl.ds(c, n)
            sb[:, cols] = (st[0, :, cols].astype(F32) + st[1, :, cols].astype(F32)).astype(BF)

        chunks(sb.shape[1], 256, add)
        pl.when(self.is_a)(self.x2.start)
        pl.when(self.is_b)(self.y2.start)

    def third(self):
        st, cv = self.st, self.cv
        parts, piece = cv.shape[1], cv.shape[2]

        def a():
            self.x1.wait_recv()
            self.y1b.wait_recv()
            self.x2.wait_recv()
            self.y2.wait_recv()
            d, r = self.d, self.r
            for which, trio in ((self.k, (d.at[0], r.at[0], r.at[4])), (1 - self.k, (d.at[1], r.at[2], r.at[3]))):
                self.copy_in(list(enumerate(trio)))

                def add(c, n):
                    cols = pl.ds(c, n)
                    total = sum(st[i, :, cols].astype(F32) for i in range(3))
                    for q in range(parts):
                        cv[which, q, :, cols] = total[q * piece : (q + 1) * piece].astype(BF)

                chunks(cv.shape[3], 256, add)
            self.home.start()
            keep = pltpu.make_async_copy(cv.at[0], self.zs, self.ls.at[0])
            keep.start()
            keep.wait()

        pl.when(self.is_a)(a)

    def fourth(self):
        pl.when(self.is_b)(self.home.wait_recv)

    def close(self):
        self.x1.wait_send()

        def a():
            self.x2.wait_send()
            self.home.wait_send()

        def b():
            self.y1.wait_send()
            self.y1b.wait_send()
            self.y2.wait_send()

        pl.when(self.is_a)(a)
        pl.when(self.is_b)(b)

    @staticmethod
    def peers(spot):
        x, k, y = spot
        return [at(1 - x, k, y), at(x, k, 1 - y), at(x, 1 - k, y)]


def scatter_scratch(rows, cols, parts):
    return [
        pltpu.VMEM((3, rows, cols), BF), pltpu.VMEM((rows, cols), BF), pltpu.VMEM((2, parts, rows // parts, cols), BF),
        pltpu.SemaphoreType.DMA((4,)), pltpu.SemaphoreType.DMA((6,)), pltpu.SemaphoreType.DMA((6,)),
    ]


def norm_back_rows(values, mine, theirs, gain):
    mean = jnp.mean(values, axis=1, keepdims=True)
    center = values - mean
    scale = lax.rsqrt(jnp.mean(center * center, axis=1, keepdims=True) + EPS)
    normed = center * scale
    incoming = mine.astype(F32) + theirs.astype(F32)
    e = incoming * gain
    back = scale * (e - jnp.mean(e, axis=1, keepdims=True) - normed * jnp.mean(e * normed, axis=1, keepdims=True))
    return back, normed, incoming


def fold(acc, i, rows):
    acc[i] += sum(rows[8 * j : 8 * j + 8] for j in range(rows.shape[0] // 8))


def middle_kernel(
    dd, gd, wd, gu, wu, xb, dyb, residual, f2b, hidden, slope,
    rd, zs, outb, du, dbr, dbrb, rowv, dbu,
    acc, psend, precv, gdv, guv, dup, osend, orecv, keep, theirs,
    st, sb, cv, ss, rs, ls, lsem, ps, pr, cs,
):
    spot = place()
    x, k, y = spot
    is_a = k == y
    width = wd.shape[0]
    greet(Scatter.peers(spot))
    ring = Scatter(dd, rd, zs, st, sb, cv, ss, rs, ls, spot)
    ring.first()
    got_d = load_weight(wd, gd, gdv, lsem.at[0], k, is_a)
    got_u = load_weight(wu, gu, guv, lsem.at[1], k, is_a)
    got_d()

    def contract(c, n):
        cols = pl.ds(c, n)
        grad = (nn(dyb[...], gdv[:, cols]) * slope[:, cols].astype(F32)).astype(BF)
        dup[:, cols] = grad
        dbu[:, cols] = jnp.sum(grad.astype(F32), axis=0, keepdims=True)

    chunks(slope.shape[1], 256, contract)
    got_u()

    def second_grad(c, n):
        rows = pl.ds(c, n)
        psend[:, rows] = nt(dup[...], guv[rows, :]).astype(BF)

    chunks(psend.shape[1], 384, second_grad)
    exchange = remote(psend, precv, ps.at[0], pr.at[0], at(x, 1 - k, y))
    exchange.start()
    low = k == 0
    bd = xb[SEQ - 1 : PADS, :].astype(F32)[6:7]

    def side(a, i):
        lo = 2 * i * width
        return jnp.where(low, a[:, lo : lo + width], a[:, lo + width : lo + 2 * width])

    for i in range(2):
        rows = pl.ds(pl.multiple_of((2 * i + 1 - k) * width, 32), width)
        osend[i] = nt(hidden[...], gdv[rows, :]).astype(BF)
    outs = remote(osend, orecv, ps.at[1], pr.at[1], at(x, 1 - k, y))
    outs.start()
    ring.second()
    for i in range(2):
        rows = pl.ds(pl.multiple_of((2 * i + k) * width, 32), width)
        keep[i] = nt(hidden[...], gdv[rows, :]) + side(residual[...], i) + side(bd, i)
    outs.wait_recv()
    theirs[0] = (keep[0] + orecv[0].astype(F32)).astype(BF)
    theirs[1] = (keep[1] + orecv[1].astype(F32)).astype(BF)
    mine = pltpu.make_async_copy(theirs.at[0], outb.at[x], cs)
    mine.start()
    away = remote(theirs.at[1], outb.at[x], ps.at[2], pr.at[2], at(1 - x, k, y))
    away.start()

    def up_grad(j, carry):
        du[j] = tn(f2b[j], dup[...]).astype(BF)
        return carry

    lax.fori_loop(0, 4, up_grad, 0)
    exchange.wait_recv()
    g2 = xb[SEQ - 1 : PADS, :].astype(F32)[2:3]
    acc[...] = jnp.zeros_like(acc)

    def norm2(r, n):
        rows = pl.ds(r, n)
        back, normed, incoming = norm_back_rows(residual[rows, :], psend[rows, :], precv[rows, :], g2)
        dyr = dyb[rows, :].astype(F32)
        low = (dyr + back).astype(BF)
        dbr[rows, :] = low
        fold(acc, 0, incoming * normed)
        fold(acc, 1, incoming)
        fold(acc, 2, low.astype(F32))
        fold(acc, 3, dyr)

    chunks(PADS, 32, norm2)
    rowv[...] = jnp.concatenate(
        [jnp.sum(acc[i], axis=0, keepdims=True) for i in range(4)] + [jnp.zeros((4, 4 * width), F32)], axis=0
    )
    for j in range(4):
        dbrb[j] = dbr[:, j * width : (j + 1) * width]
    ring.third()
    ring.fourth()
    mine.wait()
    remote(theirs.at[1], outb.at[1 - x], ps.at[2], pr.at[2], at(1 - x, k, y)).wait_recv()
    exchange.wait_send()
    outs.wait_send()
    away.wait_send()
    ring.close()


def middle(parts, dd, gd, wd, gu, wu, xb, dyb, residual, f2b, hidden, slope):
    width, ff = wd.shape
    anyspec = pl.BlockSpec(memory_space=pl.ANY)
    vspec = pl.BlockSpec(memory_space=pltpu.VMEM)
    shape = jax.ShapeDtypeStruct
    dma = pltpu.SemaphoreType.DMA
    outs = [
        shape((5, width, ff), BF), shape((parts, width // parts, ff), BF), shape((2, PADS, width), BF),
        shape((4, width, ff), BF), shape((PADS, 4 * width), BF), shape((4, PADS, width), BF),
        shape((8, 4 * width), F32), shape((1, ff), F32),
    ]
    return pl.pallas_call(
        middle_kernel,
        out_shape=outs,
        in_specs=[anyspec] * 5 + [vspec] * 6,
        out_specs=[anyspec] * 3 + [vspec] * 5,
        scratch_shapes=[
            pltpu.VMEM((4, 8, 4 * width), F32), pltpu.VMEM((PADS, 4 * width), BF), pltpu.VMEM((PADS, 4 * width), BF),
            pltpu.VMEM((4 * width, ff), BF), pltpu.VMEM((4 * width, ff), BF), pltpu.VMEM((PADS, ff), BF),
            pltpu.VMEM((2, PADS, width), BF), pltpu.VMEM((2, PADS, width), BF),
            pltpu.VMEM((2, PADS, width), F32), pltpu.VMEM((2, PADS, width), BF),
        ] + scatter_scratch(width, ff, parts) + [dma((2, 4)), dma((3,)), dma((3,)), dma(())],
        compiler_params=pltpu.CompilerParams(collective_id=1, has_side_effects=True, vmem_limit_bytes=VMEM_CAP),
        name="middle",
    )(dd, gd, wd, gu, wu, xb, dyb, residual, f2b, hidden, slope)


class DpSum:
    def __init__(self, zs, zr, buf, out, ss, rs, ls):
        self.zs, self.zr, self.buf, self.out, self.ls = zs, zr, buf, out, ls
        size = lax.axis_size("dp")
        self.me = lax.axis_index("dp")
        self.copies = []
        for o in range(1, size):
            dest = lax.rem(self.me + o, size)
            self.copies.append(remote(zs.at[dest], zr.at[o - 1], ss.at[o - 1], rs.at[o - 1], {"dp": dest}))

    def start(self):
        for c in self.copies:
            c.start()

    def finish(self):
        for c in self.copies:
            c.wait_recv()
        sources = [self.zs.at[self.me]] + [self.zr.at[i] for i in range(len(self.copies))]
        for i, src in enumerate(sources):
            pltpu.make_async_copy(src, self.buf.at[i], self.ls.at[i]).start()
        for i, src in enumerate(sources):
            pltpu.make_async_copy(src, self.buf.at[i], self.ls.at[i]).wait()
        buf, out = self.buf, self.out

        def add(c, n):
            cols = pl.ds(c, n)
            out[:, cols] = sum(buf[i, :, cols].astype(F32) for i in range(len(sources)))

        chunks(out.shape[1], 256, add)

    def close(self):
        for c in self.copies:
            c.wait_send()


def backward_kernel(
    du, zsd, go, wo, gq, wq, xb, f1b, hflat, qh, oh, lse, dbr, dbrb,
    ru, zsu, ro, zso, rq, zsq, zrd, zru, zro, zrq, gin, td, tu, to, tq, rowv, colv,
    acc, gov, gqv, dh, dqh, dqkv, ps, pr, do, dq, home,
    stu, sbu, cvu, ssu, rsu, lsu, sto, sbo, cvo, sso, rso, lso, stq, sbq, cvq, ssq, rsq, lsq,
    lsem, zss, zrs, zls, es, er, hs, hr, cs,
):
    spot = place()
    x, k, y = spot
    is_a = k == y
    width, hw = xb.shape[1] // 4, hflat.shape[1]
    heads = hw // HD
    size, me = lax.axis_size("dp"), lax.axis_index("dp")
    summed = cvu.shape[1] > 1
    greet(Scatter.peers(spot) + [{"dp": lax.rem(me + o, size)} for o in range(1, size) if summed])
    ring_u = Scatter(du, ru, zsu, stu, sbu, cvu, ssu, rsu, lsu, spot)
    ring_o = Scatter(do, ro, zso, sto, sbo, cvo, sso, rso, lso, spot)
    ring_q = Scatter(dq, rq, zsq, stq, sbq, cvq, ssq, rsq, lsq, spot)
    if summed:
        sums = [
            DpSum(zs, zr, cv.at[0], t, zss.at[i], zrs.at[i], zls.at[i])
            for i, (zs, zr, cv, t) in enumerate(
                ((zsd, zrd, cvu, td), (zsu, zru, cvu, tu), (zso, zro, cvo, to), (zsq, zrq, cvq, tq))
            )
        ]
    ring_u.first()
    if summed:
        sums[0].start()
    got_o = load_weight(wo, go, gov, lsem.at[0], k, is_a)
    got_q = load_weight(wq, gq, gqv, lsem.at[1], k, is_a)
    dh[...] = jnp.zeros_like(dh)
    got_o()
    dqkv[:, 0:hw] = nn(dbr[...], gov[...]).astype(BF)
    for h in range(heads):
        dh[h, :, 0:HD] = dqkv[:, h * HD : (h + 1) * HD]

    def out_grad(j, carry):
        do[j] = tn(hflat[...], dbrb[j]).astype(BF)
        return carry

    lax.fori_loop(0, 4, out_grad, 0)
    ring_o.first()
    keymask = jnp.where(lax.broadcasted_iota(jnp.int32, (PADS, 1), 0) < SEQ, 0.0, -1e30)
    ones = jnp.ones((8, 128), F32)

    def attend(h, carry):
        q, kk, v, g = qh[h], qh[heads + h], qh[2 * heads + h], dh[h]
        p = jnp.exp(nt(kk, q) * HD ** (-0.5) + keymask - lse[pl.ds(h, 1), :])
        delta = lax.dot_general(
            ones, g.astype(F32) * oh[h].astype(F32), (((1,), (1,)), ((), ())),
            precision=lax.Precision.HIGHEST, preferred_element_type=F32,
        )[0:1]
        ds = (p * (nt(v, g) - delta)).astype(BF)
        dqh[2 * heads + h] = nn(p.astype(BF), g).astype(BF)
        dqh[heads + h] = (nn(ds, q) * HD ** (-0.5)).astype(BF)
        dqh[h] = (tn(kk, ds) * HD ** (-0.5)).T.astype(BF)
        return carry

    lax.fori_loop(0, heads // 2, attend, 0)
    ring_u.second()
    lax.fori_loop(heads // 2, heads, attend, 0)
    ring_o.second()
    dqkv[:, 3 * hw :] = jnp.zeros((PADS, dqkv.shape[1] - 3 * hw), BF)
    for i in range(3 * heads):
        dqkv[:, i * HD : (i + 1) * HD] = dqh[i, :, 0:HD]
    ring_u.third()
    got_q()

    def qkv_grad(j, carry):
        dq[j] = tn(f1b[j], dqkv[...]).astype(BF)
        return carry

    lax.fori_loop(0, 4, qkv_grad, 0)
    ring_q.first()

    def first_grad(c, n):
        rows = pl.ds(c, n)
        ps[:, rows] = nt(dqkv[...], gqv[rows, :]).astype(BF)

    chunks(ps.shape[1], 384, first_grad)
    exchange = remote(ps, pr, es, er, at(x, 1 - k, y))
    exchange.start()
    ring_u.fourth()
    if summed:
        sums[0].finish()
        sums[1].start()
    ring_o.third()
    ring_o.fourth()
    if summed:
        sums[2].start()

    def bias_grad(c, n):
        cols = pl.ds(c, n)
        colv[:, cols] = jnp.sum(dqkv[:, cols].astype(F32), axis=0, keepdims=True)

    chunks(colv.shape[1], 256, bias_grad)
    exchange.wait_recv()
    exchange.wait_send()
    g1 = xb[SEQ - 1 : PADS, :].astype(F32)[1:2]
    acc[...] = jnp.zeros_like(acc)

    def norm1(r, n):
        rows = pl.ds(r, n)
        back, normed, incoming = norm_back_rows(xb[rows, :].astype(F32), ps[rows, :], pr[rows, :], g1)
        ps[rows, :] = (dbr[rows, :].astype(F32) + back).astype(BF)
        fold(acc, 0, incoming * normed)
        fold(acc, 1, incoming)

    chunks(PADS, 32, norm1)
    rowv[...] = jnp.concatenate(
        [jnp.sum(acc[i], axis=0, keepdims=True) for i in range(2)] + [jnp.zeros((6, 4 * width), F32)], axis=0
    )
    low = k == 0
    for i in range(2):
        lo = 2 * i * width
        home[i] = jnp.where(low, ps[:, lo : lo + width], ps[:, lo + width : lo + 2 * width])
    mine = pltpu.make_async_copy(home.at[0], gin.at[x], cs)
    mine.start()
    away = remote(home.at[1], gin.at[x], hs, hr, at(1 - x, k, y))
    away.start()
    ring_q.second()
    if summed:
        sums[1].finish()
        sums[2].finish()
    ring_q.third()
    ring_q.fourth()
    if summed:
        sums[3].start()
    mine.wait()
    remote(home.at[1], gin.at[1 - x], hs, hr, at(1 - x, k, y)).wait_recv()
    away.wait_send()
    for ring in (ring_u, ring_o, ring_q):
        ring.close()
    if summed:
        sums[3].finish()
        for total in sums:
            total.close()


def backward(parts, du, zsd, go, wo, gq, wq, xb, f1b, hflat, qh, oh, lse, dbr, dbrb):
    width, ff = du.shape[1:]
    hw, nq = wo.shape[1], wq.shape[1]
    full, heads = 4 * width, hw // HD
    anyspec = pl.BlockSpec(memory_space=pl.ANY)
    vspec = pl.BlockSpec(memory_space=pltpu.VMEM)
    shape = jax.ShapeDtypeStruct
    dma = pltpu.SemaphoreType.DMA
    others = max(parts - 1, 1)
    piece, slab = width // parts, hw // parts
    outs = [
        shape((5, width, ff), BF), shape((parts, piece, ff), BF), shape((5, hw, width), BF), shape((parts, slab, width), BF),
        shape((5, width, nq), BF), shape((parts, piece, nq), BF),
        shape((others, piece, ff), BF), shape((others, piece, ff), BF), shape((others, slab, width), BF),
        shape((others, piece, nq), BF), shape((2, PADS, width), BF),
        *(shape(d if parts > 1 else (8, 128), F32) for d in ((piece, ff), (piece, ff), (slab, width), (piece, nq))),
        shape((8, full), F32), shape((1, nq), F32),
    ]
    return pl.pallas_call(
        backward_kernel,
        out_shape=outs,
        in_specs=[anyspec] * 6 + [vspec] * 8,
        out_specs=[anyspec] * 11 + [vspec] * 6,
        scratch_shapes=[
            pltpu.VMEM((2, 8, full), F32), pltpu.VMEM((full, hw), BF), pltpu.VMEM((full, nq), BF),
            pltpu.VMEM((heads, PADS, 128), BF), pltpu.VMEM((3 * heads, PADS, 128), BF), pltpu.VMEM((PADS, nq), BF),
            pltpu.VMEM((PADS, full), BF), pltpu.VMEM((PADS, full), BF),
            pltpu.VMEM((4, hw, width), BF), pltpu.VMEM((4, width, nq), BF), pltpu.VMEM((2, PADS, width), BF),
        ]
        + scatter_scratch(width, ff, parts) + scatter_scratch(hw, width, parts) + scatter_scratch(width, nq, parts)
        + [dma((2, 4)), dma((4, others)), dma((4, others)), dma((4, others + 1)), dma(()), dma(()), dma(()), dma(()), dma(())],
        compiler_params=pltpu.CompilerParams(collective_id=2, has_side_effects=True, vmem_limit_bytes=VMEM_CAP),
        name="backward",
    )(du, zsd, go, wo, gq, wq, xb, f1b, hflat, qh, oh, lse, dbr, dbrb)


def shards(tokens, ln_gain, ln_bias, w_qkv, b_qv, w_out, b_out, w_up, b_up, w_down, b_down, cotangent):
    row, y = lax.axis_index("row"), lax.axis_index("col")
    x, k = row // 2, row % 2
    is_a = k == y
    width = tokens.shape[1]
    hw = b_qv.shape[1]
    heads = hw // HD

    extra = jnp.concatenate(
        [ln_gain, ln_bias, b_out[None], b_down[None], jnp.zeros((1, width), BF)], axis=0
    )
    images = tokens.shape[0] // SEQ
    tok2 = jnp.concatenate([tokens.reshape(images, SEQ, width), jnp.stack([extra] * images)], axis=1)
    cot2 = jnp.pad(cotangent.reshape(images, SEQ, width), ((0, 0), (0, PADS - SEQ), (0, 0)))
    ff = b_up.shape[0]
    bias = jnp.zeros((16, ff), BF)
    bias = bias.at[0, :hw].set(b_qv[0]).at[0, 2 * hw : 3 * hw].set(b_qv[1]).at[1].set(b_up)
    qblock = jnp.pad(w_qkv.reshape(width, 3 * hw), ((0, 0), (0, 64)))
    wot, wdt = w_out.T, w_down.T
    gq, go, gu, gd, xb, dy, bv, f1b, qh, oh, hflat, lse, residual, f2b, hidden, slope, dd = forward(
        tok2, cot2, bias, qblock, wot, w_up, wdt
    )
    dp_size = lax.axis_size("dp")
    parts = dp_size if width % dp_size == 0 and (width // dp_size) % 8 == 0 else 1
    _, zsd, outb, du, dbr, dbrb, vec2, dbu = middle(parts, dd, gd, wdt, gu, w_up, xb, dy, residual, f2b, hidden, slope)
    output = outb[:, :SEQ].reshape(-1, width)
    (_, zsu, _, zso, _, zsq, _, _, _, _, gin, td, tu, to, tq, vec1, dbqkv) = backward(
        parts, du, zsd, go, wot, gq, qblock, xb, f1b, hflat, qh, oh, lse, dbr, dbrb
    )
    input_grad = gin[:, :SEQ].reshape(-1, width)
    if parts == 1:

        def over_dp(a):
            return lax.psum_scatter(a[0], "dp", scatter_dimension=0, tiled=True).astype(F32)

        td, tu, to, tq = over_dp(zsd), over_dp(zsu), over_dp(zso), over_dp(zsq)

    w = width
    low = k == 0
    rowvec = jnp.stack([vec1[0], vec2[0], vec1[1], vec2[1], vec2[2], vec2[3]])
    rowvec = jnp.where(x == 0, rowvec, jnp.roll(rowvec, 2 * w, axis=1)) * jnp.where(low, 1.0, 0.0)
    colvec = jnp.concatenate([dbqkv[0, :hw], dbqkv[0, 2 * hw : 3 * hw], dbu[0]])
    colvec = jnp.concatenate([jnp.where(low, colvec, 0.0), jnp.where(low, 0.0, colvec)])
    total = lax.psum(jnp.concatenate([rowvec.reshape(-1), colvec]), ("dp", "row", "col"))
    rv = lax.dynamic_slice_in_dim(total[: 24 * w].reshape(6, 4 * w), row * w, w, 1)
    cv = lax.dynamic_slice_in_dim(total[24 * w :], y * (colvec.shape[0] // 2), colvec.shape[0] // 2, 0)
    return (
        output,
        input_grad,
        rv[0:2],
        rv[2:4],
        tq[:, : 3 * hw].reshape(-1, 3, hw),
        cv[: 2 * hw].reshape(2, hw),
        to,
        rv[4],
        tu,
        cv[2 * hw :],
        td.T,
        rv[5],
    )


def solution(mesh):
    placed = (
        P(("dp", "col"), "row"),
        P(None, "row"),
        P(None, "row"),
        P("row", None, "col"),
        P(None, "col"),
        P("col", "row"),
        P("row"),
        P("row", "col"),
        P("col"),
        P("col", "row"),
        P("row"),
        P(("dp", "col"), "row"),
    )
    return jax.shard_map(
        shards,
        mesh=mesh,
        in_specs=placed,
        out_specs=(
            P(("dp", "col"), "row"),
            P(("dp", "col"), "row"),
            P(None, "row"),
            P(None, "row"),
            P(("row", "dp"), None, "col"),
            P(None, "col"),
            P(("col", "dp"), "row"),
            P("row"),
            P(("row", "dp"), "col"),
            P("col"),
            P("col", ("row", "dp")),
            P("row"),
        ),
        check_vma=False,
    )
```

```python
import jax
import jax.numpy as jnp
from jax import lax
from jax.experimental import pallas as pl
from jax.experimental.pallas import tpu as pltpu
from jax.sharding import PartitionSpec as P

HD = 72
SEQ = 729
EPS = 1e-06
BF = jnp.bfloat16
F32 = jnp.float32


def nn(a, b):
    return jnp.dot(a, b, preferred_element_type=F32)


def nt(a, b):
    return lax.dot_general(a, b, (((1,), (1,)), ((), ())), preferred_element_type=F32)


def tn(a, b):
    return lax.dot_general(a, b, (((0,), (0,)), ((), ())), preferred_element_type=F32)


def gelu_parts(u):
    t = jnp.tanh(0.7978845608028654 * (u + 0.044715 * u * u * u))
    value = 0.5 * u * (1.0 + t)
    slope = 0.5 * (1.0 + t) + 0.5 * u * (1.0 - t * t) * 0.7978845608028654 * (1.0 + 3 * 0.044715 * u * u)
    return value, slope


MESH = pl.DeviceIdType.MESH
PADS = 736
VMEM_CAP = 66_000_000


def place():
    row, col = lax.axis_index("row"), lax.axis_index("col")
    return row // 2, lax.rem(row, 2), col


def at(x, k, y):
    return {"row": 2 * x + k, "col": y}


def greet(peers):
    barrier = pltpu.get_barrier_semaphore()
    for peer in peers:
        pl.semaphore_signal(barrier, inc=1, device_id=peer, device_id_type=MESH)
    pl.semaphore_wait(barrier, len(peers))


def chunks(total, step, body):
    whole = total // step
    if whole > 0:
        lax.fori_loop(0, whole, lambda i, c: (body(pl.multiple_of(i * step, step), step), c)[1], 0)
    if total % step:
        body(whole * step, total % step)


def forward_kernel(
    tok, cot, bias, wq, wo, wu, wd,
    gq, go, gu, gd, xb, dyb, bv, f1b, qh, oh, hflat, lse, residual, f2b, hidden, slope, dd,
    tbuf, cbuf, gqv, gov, guv, f1, psend, precv,
    ssem, rsem, csem, lsem, wsend, wrecv,
):
    x, k, y = place()
    is_a, is_b = k == y, k != y
    hw = hflat.shape[1]
    heads = hw // HD
    width = tok.shape[2]
    greet([at(x, 1 - k, y), at(1 - x, k, y), at(1 - x, 1 - k, y), at(x, k, 1 - y), at(x, 1 - k, 1 - y)])

    def remote(src, dst, s, r, dest):
        return pltpu.make_async_remote_copy(
            src_ref=src, dst_ref=dst, send_sem=s, recv_sem=r, device_id=dest, device_id_type=MESH
        )

    blocks, wholes = (wq, wo, wu, wd), (gq, go, gu, gd)

    def own_sends(w):
        b, g = blocks[w], wholes[w]
        a = [
            remote(b, g.at[2 + k], wsend.at[w, 0], wrecv.at[w, 2 + k], at(1 - x, k, y)),
            remote(b, g.at[k], wsend.at[w, 1], wrecv.at[w, k], at(x, k, 1 - y)),
        ]
        bb = [
            remote(b, g.at[2 + k], wsend.at[w, 0], wrecv.at[w, 2 + k], at(1 - x, 1 - k, y)),
            remote(b, g.at[k], wsend.at[w, 1], wrecv.at[w, k], at(x, 1 - k, 1 - y)),
            remote(b, g.at[k], wsend.at[w, 2], wrecv.at[w, k], at(x, 1 - k, y)),
        ]
        return a, bb

    def relays(w):
        g = wholes[w]
        return (
            remote(g.at[2], g.at[2], wsend.at[w, 3], wrecv.at[w, 2], at(x, k, 1 - y)),
            remote(g.at[1], g.at[3], wsend.at[w, 3], wrecv.at[w, 3], at(1 - x, k, y)),
        )

    def both(fa, fb):
        pl.when(is_a)(fa)
        pl.when(is_b)(fb)

    def start_own(w):
        a, b = own_sends(w)
        both(lambda: [c.start() for c in a] and None, lambda: [c.start() for c in b] and None)

    def arrived(w, j):
        remote(blocks[w], wholes[w].at[j], wsend.at[w, 0], wrecv.at[w, j], at(x, 1 - k, y)).wait_recv()

    def start_relay(w):
        ra, rb = relays(w)

        def fa():
            arrived(w, 2)
            ra.start()

        def fb():
            arrived(w, 1)
            rb.start()

        both(fa, fb)

    def wait_rest(w):
        pl.when(is_b | (k == 1))(lambda: arrived(w, 0))
        pl.when(is_a & (k == 0))(lambda: arrived(w, 1))
        pl.when(is_b)(lambda: arrived(w, 2))
        arrived(w, 3)

    def finish_sends(w):
        a, b = own_sends(w)
        ra, rb = relays(w)
        both(
            lambda: [c.wait_send() for c in a + [ra]] and None,
            lambda: [c.wait_send() for c in b + [rb]] and None,
        )

    def load(w, dst):
        b, g = blocks[w], wholes[w]
        for j in range(4):
            rows = pl.ds(j * width, width)
            local = is_a & (k == j) if j < 2 else None
            if local is None:
                pltpu.make_async_copy(g.at[j], dst.at[rows], lsem.at[j]).start()
            else:
                pl.when(local)(lambda: pltpu.make_async_copy(b, dst.at[rows], lsem.at[j]).start())
                pl.when(jnp.logical_not(local))(
                    lambda: pltpu.make_async_copy(g.at[j], dst.at[rows], lsem.at[j]).start()
                )
        for j in range(4):
            pltpu.make_async_copy(g.at[j], dst.at[pl.ds(j * width, width)], lsem.at[j]).wait()

    tx = remote(tok.at[1 - x], tbuf.at[2 + k], ssem.at[0], rsem.at[0], at(1 - x, k, y))
    cx = remote(cot.at[1 - x], cbuf.at[2 + k], ssem.at[1], rsem.at[1], at(1 - x, k, y))
    t1 = remote(tok.at[x], tbuf.at[k], ssem.at[2], rsem.at[2], at(x, 1 - k, y))
    c1 = remote(cot.at[x], cbuf.at[k], ssem.at[3], rsem.at[3], at(x, 1 - k, y))
    t2 = remote(tbuf.at[2 + k], tbuf.at[2 + k], ssem.at[4], rsem.at[4], at(x, 1 - k, y))
    c2 = remote(cbuf.at[2 + k], cbuf.at[2 + k], ssem.at[5], rsem.at[5], at(x, 1 - k, y))
    bs = remote(bias, bv, ssem.at[6], rsem.at[6], at(x, k, 1 - y))
    pe = remote(psend, precv, ssem.at[7], rsem.at[7], at(x, 1 - k, y))
    tl = pltpu.make_async_copy(tok.at[x], tbuf.at[k], csem.at[0])
    cl = pltpu.make_async_copy(cot.at[x], cbuf.at[k], csem.at[1])
    bl = pltpu.make_async_copy(bias, bv, csem.at[2])

    tx.start()
    t1.start()
    tl.start()
    start_own(0)
    both(lambda: (bl.start(), bs.start()) and None, lambda: None)
    cl.start()
    c1.start()

    tx.wait_recv()
    t2.start()
    tl.wait()
    t1.wait_recv()
    t2.wait_recv()
    for j in range(4):
        xb[:, j * width : (j + 1) * width] = tbuf[j]
    vecs = xb[SEQ - 1 : PADS, :].astype(F32)
    g1, g2, s1, s2, bo = (vecs[j : j + 1] for j in range(1, 6))

    def stats(v):
        mean = jnp.mean(v, axis=1, keepdims=True)
        c = v - mean
        return c * lax.rsqrt(jnp.mean(c * c, axis=1, keepdims=True) + EPS)

    def norm1(r, n):
        f1[pl.ds(r, n), :] = (stats(xb[pl.ds(r, n), :].astype(F32)) * g1 + s1).astype(BF)

    chunks(PADS, 128, norm1)
    f2 = f1
    start_relay(0)
    start_own(1)
    both(bl.wait, bs.wait_recv)
    wait_rest(0)
    load(0, gqv)

    def project(c, n):
        cols = pl.ds(c, n)
        hidden[:, cols] = (nn(f1[...], gqv[:, cols]) + bv[0:1, cols].astype(F32)).astype(BF)

    chunks(gqv.shape[1], 256, project)
    start_relay(1)
    start_own(2)
    for j in range(4):
        f1b[j] = f1[:, j * width : (j + 1) * width]
    qh[...] = jnp.zeros_like(qh)
    for p in range(3):
        for h in range(heads):
            lo = p * hw + h * HD
            qh[p * heads + h, :, 0:HD] = hidden[:, lo : lo + HD]
    keymask = jnp.where(lax.broadcasted_iota(jnp.int32, (PADS, 1), 0) < SEQ, 0.0, -1e30)

    def attend(h, carry):
        st = nt(qh[heads + h], qh[h]) + keymask
        top = jnp.max(st, axis=0, keepdims=True)
        e = jnp.exp((st - top) * HD ** (-0.5))
        tot = jnp.sum(e, axis=0, keepdims=True)
        lse[pl.ds(h, 1), :] = top * HD ** (-0.5) + jnp.log(tot)
        out = tn(qh[2 * heads + h], e.astype(BF)) / tot
        oh[h] = out.T.astype(BF)
        return carry

    lax.fori_loop(0, heads, attend, 0)
    for h in range(heads):
        hflat[:, h * HD : (h + 1) * HD] = oh[h, :, 0:HD]
    wait_rest(1)
    load(1, gov)

    def out_project(c, n):
        cols = pl.ds(c, n)
        part = nt(hflat[...], gov[cols, :])
        psend[:, cols] = part.astype(BF)
        residual[:, cols] = part

    chunks(4 * width, 512, out_project)
    pe.start()
    pe.wait_recv()

    def norm2(r, n):
        rows = pl.ds(r, n)
        v = xb[rows, :].astype(F32) + bo + residual[rows, :] + precv[rows, :].astype(F32)
        residual[rows, :] = v
        f2[rows, :] = (stats(v) * g2 + s2).astype(BF)

    chunks(PADS, 128, norm2)
    start_relay(2)
    cx.start()
    start_own(3)
    wait_rest(2)
    load(2, guv)
    for j in range(4):
        f2b[j] = f2[:, j * width : (j + 1) * width]

    def expand(c, n):
        cols = pl.ds(c, n)
        u = nn(f2[...], guv[:, cols]) + bv[1:2, cols].astype(F32)
        value, grad = gelu_parts(u)
        hidden[:, cols] = value.astype(BF)
        slope[:, cols] = grad.astype(BF)

    chunks(hidden.shape[1], 256, expand)
    cx.wait_recv()
    c2.start()
    cl.wait()
    c1.wait_recv()
    c2.wait_recv()
    for j in range(4):
        dyb[:, j * width : (j + 1) * width] = cbuf[j]

    def down_grad(j, carry):
        dd[j] = tn(cbuf[j], hidden[...]).astype(BF)
        return carry

    lax.fori_loop(0, 4, down_grad, 0)
    start_relay(3)
    wait_rest(3)
    for c in (tx, cx, t1, c1, t2, c2, pe):
        c.wait_send()
    both(bs.wait_send, lambda: None)
    for w in range(4):
        finish_sends(w)


def forward(tok, cot, bias, wq, wo, wu, wd):
    width, hw, ff = tok.shape[2], wo.shape[1], wu.shape[1]
    full = 4 * width
    heads = hw // HD
    anyspec = pl.BlockSpec(memory_space=pl.ANY)
    vspec = pl.BlockSpec(memory_space=pltpu.VMEM)
    shape = jax.ShapeDtypeStruct
    outs = [
        shape((4,) + wq.shape, BF), shape((4,) + wo.shape, BF), shape((4,) + wu.shape, BF), shape((4,) + wd.shape, BF),
        shape((PADS, full), BF), shape((PADS, full), BF), shape(bias.shape, BF), shape((4, PADS, width), BF),
        shape((3 * heads, PADS, 128), BF), shape((heads, PADS, 128), BF), shape((PADS, hw), BF), shape((heads, PADS), F32),
        shape((PADS, full), F32), shape((4, PADS, width), BF), shape((PADS, ff), BF), shape((PADS, ff), BF),
        shape((4, width, ff), BF),
    ]
    dma = pltpu.SemaphoreType.DMA
    return pl.pallas_call(
        forward_kernel,
        out_shape=outs,
        in_specs=[anyspec] * 7,
        out_specs=[anyspec] * 4 + [vspec] * 13,
        scratch_shapes=[
            pltpu.VMEM((4, PADS, width), BF), pltpu.VMEM((4, PADS, width), BF),
            pltpu.VMEM((full, wq.shape[1]), BF), pltpu.VMEM((full, hw), BF), pltpu.VMEM((full, ff), BF),
            pltpu.VMEM((PADS, full), BF), pltpu.VMEM((PADS, full), BF), pltpu.VMEM((PADS, full), BF),
            dma((8,)), dma((8,)), dma((3,)), dma((4,)), dma((4, 4)), dma((4, 4)),
        ],
        compiler_params=pltpu.CompilerParams(collective_id=0, has_side_effects=True, vmem_limit_bytes=VMEM_CAP),
        name="forward",
    )(tok, cot, bias, wq, wo, wu, wd)


def load_weight(b, g, dst, sem, k, is_a):
    width = b.shape[0]
    for j in range(4):
        rows = pl.ds(j * width, width)
        if j < 2:
            local = is_a & (k == j)
            pl.when(local)(lambda: pltpu.make_async_copy(b, dst.at[rows], sem.at[j]).start())
            pl.when(jnp.logical_not(local))(lambda: pltpu.make_async_copy(g.at[j], dst.at[rows], sem.at[j]).start())
        else:
            pltpu.make_async_copy(g.at[j], dst.at[rows], sem.at[j]).start()

    def wait():
        for j in range(4):
            pltpu.make_async_copy(g.at[j], dst.at[pl.ds(j * width, width)], sem.at[j]).wait()

    return wait


def remote(src, dst, s, r, dest):
    return pltpu.make_async_remote_copy(
        src_ref=src, dst_ref=dst, send_sem=s, recv_sem=r, device_id=dest, device_id_type=MESH
    )


class Scatter:
    def __init__(self, d, r, zs, st, sb, cv, ss, rs, ls, spot):
        self.d, self.r, self.zs, self.st, self.sb, self.cv, self.ls, self.spot = d, r, zs, st, sb, cv, ls, spot
        x, k, y = spot
        self.is_a, self.is_b, self.k = k == y, k != y, k
        across, over, mate = at(1 - x, k, y), at(x, k, 1 - y), at(x, 1 - k, y)
        self.x1 = remote(d.at[2], r.at[0], ss.at[0], rs.at[0], across)
        self.y1 = remote(d.at[3], r.at[1], ss.at[1], rs.at[1], over)
        self.y1b = remote(d.at[1], r.at[2], ss.at[2], rs.at[2], over)
        self.x2 = remote(sb, r.at[3], ss.at[1], rs.at[3], across)
        self.y2 = remote(sb, r.at[4], ss.at[3], rs.at[4], over)
        self.home = remote(cv.at[1], zs, ss.at[2], rs.at[5], mate)

    def first(self):
        self.x1.start()

        def b():
            self.y1.start()
            self.y1b.start()

        pl.when(self.is_b)(b)

    def copy_in(self, pairs):
        for i, src in pairs:
            pltpu.make_async_copy(src, self.st.at[i], self.ls.at[i]).start()
        for i, src in pairs:
            pltpu.make_async_copy(src, self.st.at[i], self.ls.at[i]).wait()

    def second(self):
        st, sb = self.st, self.sb

        def fetch_a():
            self.y1.wait_recv()
            self.copy_in([(0, self.d.at[3]), (1, self.r.at[1])])

        def fetch_b():
            self.x1.wait_recv()
            self.copy_in([(0, self.d.at[0]), (1, self.r.at[0])])

        pl.when(self.is_a)(fetch_a)
        pl.when(self.is_b)(fetch_b)

        def add(c, n):
            cols = pl.ds(c, n)
            sb[:, cols] = (st[0, :, cols].astype(F32) + st[1, :, cols].astype(F32)).astype(BF)

        chunks(sb.shape[1], 256, add)
        pl.when(self.is_a)(self.x2.start)
        pl.when(self.is_b)(self.y2.start)

    def third(self):
        st, cv = self.st, self.cv
        parts, piece = cv.shape[1], cv.shape[2]

        def a():
            self.x1.wait_recv()
            self.y1b.wait_recv()
            self.x2.wait_recv()
            self.y2.wait_recv()
            d, r = self.d, self.r
            for which, trio in ((self.k, (d.at[0], r.at[0], r.at[4])), (1 - self.k, (d.at[1], r.at[2], r.at[3]))):
                self.copy_in(list(enumerate(trio)))

                def add(c, n):
                    cols = pl.ds(c, n)
                    total = sum(st[i, :, cols].astype(F32) for i in range(3))
                    for q in range(parts):
                        cv[which, q, :, cols] = total[q * piece : (q + 1) * piece].astype(BF)

                chunks(cv.shape[3], 256, add)
            self.home.start()
            keep = pltpu.make_async_copy(cv.at[0], self.zs, self.ls.at[0])
            keep.start()
            keep.wait()

        pl.when(self.is_a)(a)

    def fourth(self):
        pl.when(self.is_b)(self.home.wait_recv)

    def close(self):
        self.x1.wait_send()

        def a():
            self.x2.wait_send()
            self.home.wait_send()

        def b():
            self.y1.wait_send()
            self.y1b.wait_send()
            self.y2.wait_send()

        pl.when(self.is_a)(a)
        pl.when(self.is_b)(b)

    @staticmethod
    def peers(spot):
        x, k, y = spot
        return [at(1 - x, k, y), at(x, k, 1 - y), at(x, 1 - k, y)]


def scatter_scratch(rows, cols, parts):
    return [
        pltpu.VMEM((3, rows, cols), BF), pltpu.VMEM((rows, cols), BF), pltpu.VMEM((2, parts, rows // parts, cols), BF),
        pltpu.SemaphoreType.DMA((4,)), pltpu.SemaphoreType.DMA((6,)), pltpu.SemaphoreType.DMA((6,)),
    ]


def norm_back_rows(values, mine, theirs, gain):
    mean = jnp.mean(values, axis=1, keepdims=True)
    center = values - mean
    scale = lax.rsqrt(jnp.mean(center * center, axis=1, keepdims=True) + EPS)
    normed = center * scale
    incoming = mine.astype(F32) + theirs.astype(F32)
    e = incoming * gain
    back = scale * (e - jnp.mean(e, axis=1, keepdims=True) - normed * jnp.mean(e * normed, axis=1, keepdims=True))
    return back, normed, incoming


def fold(acc, i, rows):
    acc[i] += sum(rows[8 * j : 8 * j + 8] for j in range(rows.shape[0] // 8))


def middle_kernel(
    dd, gd, wd, gu, wu, xb, dyb, residual, f2b, hidden, slope,
    rd, zs, outb, du, dbr, dbrb, rowv, dbu,
    acc, psend, precv, gdv, guv, dup, osend, orecv, full, theirs,
    st, sb, cv, ss, rs, ls, lsem, ps, pr, cs,
):
    spot = place()
    x, k, y = spot
    is_a = k == y
    width = wd.shape[0]
    greet(Scatter.peers(spot))
    ring = Scatter(dd, rd, zs, st, sb, cv, ss, rs, ls, spot)
    ring.first()
    got_d = load_weight(wd, gd, gdv, lsem.at[0], k, is_a)
    got_u = load_weight(wu, gu, guv, lsem.at[1], k, is_a)
    got_d()

    def contract(c, n):
        cols = pl.ds(c, n)
        grad = (nn(dyb[...], gdv[:, cols]) * slope[:, cols].astype(F32)).astype(BF)
        dup[:, cols] = grad
        dbu[:, cols] = jnp.sum(grad.astype(F32), axis=0, keepdims=True)

    chunks(slope.shape[1], 256, contract)
    got_u()

    def second_grad(c, n):
        rows = pl.ds(c, n)
        psend[:, rows] = nt(dup[...], guv[rows, :]).astype(BF)

    chunks(psend.shape[1], 512, second_grad)
    exchange = remote(psend, precv, ps.at[0], pr.at[0], at(x, 1 - k, y))
    exchange.start()
    low = k == 0
    bd = xb[SEQ - 1 : PADS, :].astype(F32)[6:7]

    def side(a, i):
        lo = 2 * i * width
        return jnp.where(low, a[:, lo : lo + width], a[:, lo + width : lo + 2 * width])

    def down(c, n):
        rows = pl.ds(c, n)
        full[:, rows] = nt(hidden[...], gdv[rows, :])

    chunks(4 * width, 512, down)

    def far(a, i):
        lo = 2 * i * width
        return jnp.where(low, a[:, lo + width : lo + 2 * width], a[:, lo : lo + width])

    for i in range(2):
        osend[i] = far(full, i).astype(BF)
    outs = remote(osend, orecv, ps.at[1], pr.at[1], at(x, 1 - k, y))
    outs.start()
    ring.second()
    outs.wait_recv()
    for i in range(2):
        theirs[i] = (side(full, i) + side(residual, i) + side(bd, i) + orecv[i].astype(F32)).astype(BF)
    mine = pltpu.make_async_copy(theirs.at[0], outb.at[x], cs)
    mine.start()
    away = remote(theirs.at[1], outb.at[x], ps.at[2], pr.at[2], at(1 - x, k, y))
    away.start()

    def up_grad(j, carry):
        du[j] = tn(f2b[j], dup[...]).astype(BF)
        return carry

    lax.fori_loop(0, 4, up_grad, 0)
    exchange.wait_recv()
    g2 = xb[SEQ - 1 : PADS, :].astype(F32)[2:3]
    acc[...] = jnp.zeros_like(acc)

    def norm2(r, n):
        rows = pl.ds(r, n)
        back, normed, incoming = norm_back_rows(residual[rows, :], psend[rows, :], precv[rows, :], g2)
        dyr = dyb[rows, :].astype(F32)
        low = (dyr + back).astype(BF)
        dbr[rows, :] = low
        fold(acc, 0, incoming * normed)
        fold(acc, 1, incoming)
        fold(acc, 2, low.astype(F32))
        fold(acc, 3, dyr)

    chunks(PADS, 128, norm2)
    rowv[...] = jnp.concatenate(
        [jnp.sum(acc[i], axis=0, keepdims=True) for i in range(4)] + [jnp.zeros((4, 4 * width), F32)], axis=0
    )
    for j in range(4):
        dbrb[j] = dbr[:, j * width : (j + 1) * width]
    ring.third()
    ring.fourth()
    mine.wait()
    remote(theirs.at[1], outb.at[1 - x], ps.at[2], pr.at[2], at(1 - x, k, y)).wait_recv()
    exchange.wait_send()
    outs.wait_send()
    away.wait_send()
    ring.close()


def middle(parts, dd, gd, wd, gu, wu, xb, dyb, residual, f2b, hidden, slope):
    width, ff = wd.shape
    anyspec = pl.BlockSpec(memory_space=pl.ANY)
    vspec = pl.BlockSpec(memory_space=pltpu.VMEM)
    shape = jax.ShapeDtypeStruct
    dma = pltpu.SemaphoreType.DMA
    outs = [
        shape((5, width, ff), BF), shape((parts, width // parts, ff), BF), shape((2, PADS, width), BF),
        shape((4, width, ff), BF), shape((PADS, 4 * width), BF), shape((4, PADS, width), BF),
        shape((8, 4 * width), F32), shape((1, ff), F32),
    ]
    return pl.pallas_call(
        middle_kernel,
        out_shape=outs,
        in_specs=[anyspec] * 5 + [vspec] * 6,
        out_specs=[anyspec] * 3 + [vspec] * 5,
        scratch_shapes=[
            pltpu.VMEM((4, 8, 4 * width), F32), pltpu.VMEM((PADS, 4 * width), BF), pltpu.VMEM((PADS, 4 * width), BF),
            pltpu.VMEM((4 * width, ff), BF), pltpu.VMEM((4 * width, ff), BF), pltpu.VMEM((PADS, ff), BF),
            pltpu.VMEM((2, PADS, width), BF), pltpu.VMEM((2, PADS, width), BF),
            pltpu.VMEM((PADS, 4 * width), F32), pltpu.VMEM((2, PADS, width), BF),
        ] + scatter_scratch(width, ff, parts) + [dma((2, 4)), dma((3,)), dma((3,)), dma(())],
        compiler_params=pltpu.CompilerParams(collective_id=1, has_side_effects=True, vmem_limit_bytes=VMEM_CAP),
        name="middle",
    )(dd, gd, wd, gu, wu, xb, dyb, residual, f2b, hidden, slope)


class DpSum:
    def __init__(self, zs, zr, buf, out, ss, rs, ls):
        self.zs, self.zr, self.buf, self.out, self.ls = zs, zr, buf, out, ls
        size = lax.axis_size("dp")
        self.me = lax.axis_index("dp")
        self.copies = []
        for o in range(1, size):
            dest = lax.rem(self.me + o, size)
            self.copies.append(remote(zs.at[dest], zr.at[o - 1], ss.at[o - 1], rs.at[o - 1], {"dp": dest}))

    def start(self):
        for c in self.copies:
            c.start()

    def finish(self):
        for c in self.copies:
            c.wait_recv()
        sources = [self.zs.at[self.me]] + [self.zr.at[i] for i in range(len(self.copies))]
        for i, src in enumerate(sources):
            pltpu.make_async_copy(src, self.buf.at[i], self.ls.at[i]).start()
        for i, src in enumerate(sources):
            pltpu.make_async_copy(src, self.buf.at[i], self.ls.at[i]).wait()
        buf, out = self.buf, self.out

        def add(c, n):
            cols = pl.ds(c, n)
            out[:, cols] = sum(buf[i, :, cols].astype(F32) for i in range(len(sources)))

        chunks(out.shape[1], 256, add)

    def close(self):
        for c in self.copies:
            c.wait_send()


def backward_kernel(
    du, zsd, go, wo, gq, wq, xb, f1b, hflat, qh, oh, lse, dbr, dbrb, vec2, dbu,
    ru, zsu, ro, zso, rq, zsq, zrd, zru, zro, zrq, gin, td, tu, to, tq, rowt, colt,
    acc, gov, gqv, dh, dqh, dqkv, ps, pr, do, dq, home,
    stu, sbu, cvu, ssu, rsu, lsu, sto, sbo, cvo, sso, rso, lso, stq, sbq, cvq, ssq, rsq, lsq,
    rowb, colv, rr, cr, rsum, csum, rz, cz, lsem, zss, zrs, zls, es, er, hs, hr, cs, vs, vr, ws, wr,
):
    spot = place()
    x, k, y = spot
    is_a, is_b = k == y, k != y
    width, hw = xb.shape[1] // 4, hflat.shape[1]
    heads = hw // HD
    size, me = lax.axis_size("dp"), lax.axis_index("dp")
    summed = cvu.shape[1] > 1
    plane = [at(1 - x, k, y), at(x, k, 1 - y), at(1 - x, k, 1 - y)]
    plane += [at(x, 1 - k, y), at(1 - x, 1 - k, y), at(x, 1 - k, 1 - y), at(1 - x, 1 - k, 1 - y)]
    greet(plane + [{"dp": lax.rem(me + o, size)} for o in range(1, size)])
    side = jnp.where(is_a, 0, 1)
    row_sends = [
        remote(rowb.at[k if i == 1 else 2 + k], rr.at[i], vs.at[i], vr.at[i], plane[i]) for i in range(3)
    ]
    col_sends = [
        remote(colv, cr.at[side], vs.at[3], vr.at[3 + side], at(x, 1 - k, k)),
        remote(colv, cr.at[2 + side], vs.at[4], vr.at[5 + side], at(1 - x, k, k)),
        remote(colv, cr.at[2 + side], vs.at[5], vr.at[5 + side], at(1 - x, 1 - k, k)),
    ]
    col_extra = remote(colv, cr.at[1], vs.at[6], vr.at[4], at(x, k, k))
    dp_sends = []
    for o in range(1, size):
        dest = {"dp": lax.rem(me + o, size)}
        dp_sends.append(remote(rsum, rz.at[o - 1], ws.at[0, o - 1], wr.at[0, o - 1], dest))
        dp_sends.append(remote(csum, cz.at[o - 1], ws.at[1, o - 1], wr.at[1, o - 1], dest))
    ring_u = Scatter(du, ru, zsu, stu, sbu, cvu, ssu, rsu, lsu, spot)
    ring_o = Scatter(do, ro, zso, sto, sbo, cvo, sso, rso, lso, spot)
    ring_q = Scatter(dq, rq, zsq, stq, sbq, cvq, ssq, rsq, lsq, spot)
    if summed:
        sums = [
            DpSum(zs, zr, cv.at[0], t, zss.at[i], zrs.at[i], zls.at[i])
            for i, (zs, zr, cv, t) in enumerate(
                ((zsd, zrd, cvu, td), (zsu, zru, cvu, tu), (zso, zro, cvo, to), (zsq, zrq, cvq, tq))
            )
        ]
    ring_u.first()
    if summed:
        sums[0].start()
    got_o = load_weight(wo, go, gov, lsem.at[0], k, is_a)
    got_q = load_weight(wq, gq, gqv, lsem.at[1], k, is_a)
    dh[...] = jnp.zeros_like(dh)
    got_o()
    dqkv[:, 0:hw] = nn(dbr[...], gov[...]).astype(BF)
    for h in range(heads):
        dh[h, :, 0:HD] = dqkv[:, h * HD : (h + 1) * HD]

    def out_grad(j, carry):
        do[j] = tn(hflat[...], dbrb[j]).astype(BF)
        return carry

    lax.fori_loop(0, 4, out_grad, 0)
    ring_o.first()
    keymask = jnp.where(lax.broadcasted_iota(jnp.int32, (PADS, 1), 0) < SEQ, 0.0, -1e30)
    ones = jnp.ones((8, 128), F32)

    def attend(h, carry):
        q, kk, v, g = qh[h], qh[heads + h], qh[2 * heads + h], dh[h]
        p = jnp.exp(nt(kk, q) * HD ** (-0.5) + keymask - lse[pl.ds(h, 1), :])
        delta = lax.dot_general(
            ones, g.astype(F32) * oh[h].astype(F32), (((1,), (1,)), ((), ())),
            precision=lax.Precision.HIGHEST, preferred_element_type=F32,
        )[0:1]
        ds = (p * (nt(v, g) - delta)).astype(BF)
        dqh[2 * heads + h] = nn(p.astype(BF), g).astype(BF)
        dqh[heads + h] = (nn(ds, q) * HD ** (-0.5)).astype(BF)
        dqh[h] = (tn(kk, ds) * HD ** (-0.5)).T.astype(BF)
        return carry

    lax.fori_loop(0, heads // 2, attend, 0)
    ring_u.second()
    lax.fori_loop(heads // 2, heads, attend, 0)
    ring_o.second()
    dqkv[:, 3 * hw :] = jnp.zeros((PADS, dqkv.shape[1] - 3 * hw), BF)
    for i in range(3 * heads):
        dqkv[:, i * HD : (i + 1) * HD] = dqh[i, :, 0:HD]
    got_q()

    def qkv_grad(j, carry):
        dq[j] = tn(f1b[j], dqkv[...]).astype(BF)
        return carry

    lax.fori_loop(0, 4, qkv_grad, 0)
    ring_q.first()

    def first_grad(c, n):
        rows = pl.ds(c, n)
        ps[:, rows] = nt(dqkv[...], gqv[rows, :]).astype(BF)

    chunks(ps.shape[1], 512, first_grad)
    exchange = remote(ps, pr, es, er, at(x, 1 - k, y))
    exchange.start()
    ring_u.third()
    ring_u.fourth()
    if summed:
        sums[0].finish()
        sums[1].start()
    ring_o.third()
    ring_o.fourth()
    if summed:
        sums[2].start()

    def bias_grad(c, n):
        cols = pl.ds(c, n)
        colv[0:1, cols] = jnp.sum(dqkv[:, cols].astype(F32), axis=0, keepdims=True)

    chunks(dqkv.shape[1], 256, bias_grad)
    colv[1:2, :] = dbu[...]
    exchange.wait_recv()
    exchange.wait_send()
    g1 = xb[SEQ - 1 : PADS, :].astype(F32)[1:2]
    acc[...] = jnp.zeros_like(acc)

    def norm1(r, n):
        rows = pl.ds(r, n)
        back, normed, incoming = norm_back_rows(xb[rows, :].astype(F32), ps[rows, :], pr[rows, :], g1)
        ps[rows, :] = (dbr[rows, :].astype(F32) + back).astype(BF)
        fold(acc, 0, incoming * normed)
        fold(acc, 1, incoming)

    chunks(PADS, 128, norm1)
    gain, shift = (jnp.sum(acc[i], axis=0, keepdims=True) for i in range(2))
    rows6 = jnp.concatenate(
        [gain, vec2[0:1], shift, vec2[1:2], vec2[2:3], vec2[3:4], jnp.zeros((2, 4 * width), F32)], axis=0
    )
    for j in range(4):
        rowb[j] = rows6[:, j * width : (j + 1) * width]
    for c in row_sends + col_sends:
        c.start()
    pl.when(is_b)(col_extra.start)
    low = k == 0
    for i in range(2):
        lo = 2 * i * width
        home[i] = jnp.where(low, ps[:, lo : lo + width], ps[:, lo + width : lo + 2 * width])
    mine = pltpu.make_async_copy(home.at[0], gin.at[x], cs)
    mine.start()
    away = remote(home.at[1], gin.at[x], hs, hr, at(1 - x, k, y))
    away.start()
    ring_q.second()
    for c in row_sends:
        c.wait_recv()
    for i in range(1, 4):
        remote(colv, cr.at[i], vs.at[3], vr.at[3 + i], at(x, 1 - k, k)).wait_recv()
    pl.when(is_b)(lambda: remote(colv, cr.at[0], vs.at[3], vr.at[3], at(x, 1 - k, k)).wait_recv())
    rsum[...] = rowb[k] + rr[0] + rr[1] + rr[2]

    @pl.when(is_a)
    def _():
        csum[...] = colv[...] + cr[1] + cr[2] + cr[3]

    @pl.when(is_b)
    def _():
        csum[...] = cr[0] + cr[1] + cr[2] + cr[3]

    for c in dp_sends:
        c.start()
    if summed:
        sums[1].finish()
        sums[2].finish()
    ring_q.third()
    ring_q.fourth()
    if summed:
        sums[3].start()
    mine.wait()
    remote(home.at[1], gin.at[1 - x], hs, hr, at(1 - x, k, y)).wait_recv()
    away.wait_send()
    for ring in (ring_u, ring_o, ring_q):
        ring.close()
    for c in row_sends + col_sends:
        c.wait_send()
    pl.when(is_b)(col_extra.wait_send)
    for c in dp_sends:
        c.wait_recv()
        c.wait_send()
    rowt[...] = rsum[...] + sum(rz[o] for o in range(size - 1))
    colt[...] = csum[...] + sum(cz[o] for o in range(size - 1))
    if summed:
        sums[3].finish()
        for total in sums:
            total.close()


def backward(parts, du, zsd, go, wo, gq, wq, xb, f1b, hflat, qh, oh, lse, dbr, dbrb, vec2, dbu):
    width, ff = du.shape[1:]
    hw, nq = wo.shape[1], wq.shape[1]
    full, heads = 4 * width, hw // HD
    anyspec = pl.BlockSpec(memory_space=pl.ANY)
    vspec = pl.BlockSpec(memory_space=pltpu.VMEM)
    shape = jax.ShapeDtypeStruct
    dma = pltpu.SemaphoreType.DMA
    others = max(parts - 1, 1)
    peers = lax.axis_size("dp") - 1
    piece, slab = width // parts, hw // parts
    outs = [
        shape((5, width, ff), BF), shape((parts, piece, ff), BF), shape((5, hw, width), BF), shape((parts, slab, width), BF),
        shape((5, width, nq), BF), shape((parts, piece, nq), BF),
        shape((others, piece, ff), BF), shape((others, piece, ff), BF), shape((others, slab, width), BF),
        shape((others, piece, nq), BF), shape((2, PADS, width), BF),
        *(shape(d if parts > 1 else (8, 128), F32) for d in ((piece, ff), (piece, ff), (slab, width), (piece, nq))),
        shape((8, width), F32), shape((2, ff), F32),
    ]
    return pl.pallas_call(
        backward_kernel,
        out_shape=outs,
        in_specs=[anyspec] * 6 + [vspec] * 10,
        out_specs=[anyspec] * 11 + [vspec] * 6,
        scratch_shapes=[
            pltpu.VMEM((2, 8, full), F32), pltpu.VMEM((full, hw), BF), pltpu.VMEM((full, nq), BF),
            pltpu.VMEM((heads, PADS, 128), BF), pltpu.VMEM((3 * heads, PADS, 128), BF), pltpu.VMEM((PADS, nq), BF),
            pltpu.VMEM((PADS, full), BF), pltpu.VMEM((PADS, full), BF),
            pltpu.VMEM((4, hw, width), BF), pltpu.VMEM((4, width, nq), BF), pltpu.VMEM((2, PADS, width), BF),
        ]
        + scatter_scratch(width, ff, parts) + scatter_scratch(hw, width, parts) + scatter_scratch(width, nq, parts)
        + [
            pltpu.VMEM((4, 8, width), F32), pltpu.VMEM((2, ff), F32), pltpu.VMEM((3, 8, width), F32), pltpu.VMEM((4, 2, ff), F32),
            pltpu.VMEM((8, width), F32), pltpu.VMEM((2, ff), F32), pltpu.VMEM((peers, 8, width), F32), pltpu.VMEM((peers, 2, ff), F32),
        ]
        + [dma((2, 4)), dma((4, others)), dma((4, others)), dma((4, others + 1)), dma(()), dma(()), dma(()), dma(()), dma(()),
           dma((7,)), dma((7,)), dma((2, peers)), dma((2, peers))],
        compiler_params=pltpu.CompilerParams(collective_id=2, has_side_effects=True, vmem_limit_bytes=VMEM_CAP),
        name="backward",
    )(du, zsd, go, wo, gq, wq, xb, f1b, hflat, qh, oh, lse, dbr, dbrb, vec2, dbu)


def shards(tokens, ln_gain, ln_bias, w_qkv, b_qv, w_out, b_out, w_up, b_up, w_down, b_down, cotangent):
    width = tokens.shape[1]
    hw = b_qv.shape[1]

    extra = jnp.concatenate(
        [ln_gain, ln_bias, b_out[None], b_down[None], jnp.zeros((1, width), BF)], axis=0
    )
    images = tokens.shape[0] // SEQ
    blank = jnp.zeros((PADS - SEQ, width), BF)

    def with_rows(a, tail):
        return jnp.stack([jnp.concatenate([a[i * SEQ : (i + 1) * SEQ], tail]) for i in range(images)])

    tok2, cot2 = with_rows(tokens, extra), with_rows(cotangent, blank)
    ff = b_up.shape[0]
    bqkv = jnp.concatenate([b_qv[0], jnp.zeros_like(b_qv[0]), b_qv[1], jnp.zeros((ff - 3 * hw,), BF)])
    bias = jnp.concatenate([bqkv[None], b_up[None], jnp.zeros((14, ff), BF)])
    qblock = jnp.pad(w_qkv.reshape(width, 3 * hw), ((0, 0), (0, 64)))
    wot, wdt = w_out.T, w_down.T
    gq, go, gu, gd, xb, dy, bv, f1b, qh, oh, hflat, lse, residual, f2b, hidden, slope, dd = forward(
        tok2, cot2, bias, qblock, wot, w_up, wdt
    )
    dp_size = lax.axis_size("dp")
    parts = dp_size if width % dp_size == 0 and (width // dp_size) % 8 == 0 else 1
    _, zsd, outb, du, dbr, dbrb, vec2, dbu = middle(parts, dd, gd, wdt, gu, w_up, xb, dy, residual, f2b, hidden, slope)
    output = jnp.concatenate([outb[i, :SEQ] for i in range(images)])
    (_, zsu, _, zso, _, zsq, _, _, _, _, gin, td, tu, to, tq, rowt, colt) = backward(
        parts, du, zsd, go, wot, gq, qblock, xb, f1b, hflat, qh, oh, lse, dbr, dbrb, vec2, dbu
    )
    input_grad = jnp.concatenate([gin[i, :SEQ] for i in range(images)])
    if parts == 1:

        def over_dp(a):
            return lax.psum_scatter(a[0], "dp", scatter_dimension=0, tiled=True).astype(F32)

        td, tu, to, tq = over_dp(zsd), over_dp(zsu), over_dp(zso), over_dp(zsq)

    return (
        output,
        input_grad,
        rowt[0:2],
        rowt[2:4],
        tq[:, : 3 * hw].reshape(-1, 3, hw),
        jnp.stack([colt[0, :hw], colt[0, 2 * hw : 3 * hw]]),
        to,
        rowt[4],
        tu,
        colt[1],
        td.T,
        rowt[5],
    )


def solution(mesh):
    placed = (
        P(("dp", "col"), "row"),
        P(None, "row"),
        P(None, "row"),
        P("row", None, "col"),
        P(None, "col"),
        P("col", "row"),
        P("row"),
        P("row", "col"),
        P("col"),
        P("col", "row"),
        P("row"),
        P(("dp", "col"), "row"),
    )
    return jax.shard_map(
        shards,
        mesh=mesh,
        in_specs=placed,
        out_specs=(
            P(("dp", "col"), "row"),
            P(("dp", "col"), "row"),
            P(None, "row"),
            P(None, "row"),
            P(("row", "dp"), None, "col"),
            P(None, "col"),
            P(("col", "dp"), "row"),
            P("row"),
            P(("row", "dp"), "col"),
            P("col"),
            P("col", ("row", "dp")),
            P("row"),
        ),
        check_vma=False,
    )
```

```python
import jax
import jax.numpy as jnp
from jax import lax
from jax.experimental import pallas as pl
from jax.experimental.pallas import tpu as pltpu
from jax.sharding import PartitionSpec as P

HD = 72
SEQ = 729
EPS = 1e-06
BF = jnp.bfloat16
F32 = jnp.float32


def nn(a, b):
    return jnp.dot(a, b, preferred_element_type=F32)


def nt(a, b):
    return lax.dot_general(a, b, (((1,), (1,)), ((), ())), preferred_element_type=F32)


def tn(a, b):
    return lax.dot_general(a, b, (((0,), (0,)), ((), ())), preferred_element_type=F32)


def gelu_parts(u):
    t = jnp.tanh(0.7978845608028654 * (u + 0.044715 * u * u * u))
    value = 0.5 * u * (1.0 + t)
    slope = 0.5 * (1.0 + t) + 0.5 * u * (1.0 - t * t) * 0.7978845608028654 * (1.0 + 3 * 0.044715 * u * u)
    return value, slope


MESH = pl.DeviceIdType.MESH
PADS = 736
VMEM_CAP = 66_000_000


def place():
    row, col = lax.axis_index("row"), lax.axis_index("col")
    return row // 2, lax.rem(row, 2), col


def at(x, k, y):
    return {"row": 2 * x + k, "col": y}


def greet(peers):
    barrier = pltpu.get_barrier_semaphore()
    for peer in peers:
        pl.semaphore_signal(barrier, inc=1, device_id=peer, device_id_type=MESH)
    pl.semaphore_wait(barrier, len(peers))


def chunks(total, step, body):
    whole = total // step
    if whole > 0:
        lax.fori_loop(0, whole, lambda i, c: (body(pl.multiple_of(i * step, step), step), c)[1], 0)
    if total % step:
        body(whole * step, total % step)


def column(part, head, hw):
    half, left = divmod(head, hw // HD // 2)
    return half * (padded(hw) // 2) + part * (hw // 2) + left * HD


def padded(hw):
    return 2 * (-(-3 * hw // 2 // 128) * 128)


class Moves:
    def __init__(self, sems):
        self.sems, self.open = sems, {}

    def start(self, src, dst):
        c = pltpu.make_async_copy(src, dst, self.sems.at[len(self.open)])
        c.start()
        self.open[len(self.open)] = c
        return c

    def finish(self):
        for c in self.open.values():
            c.wait()


def forward_kernel(
    tok, cot, bias, wq, wo, wu, wd,
    gq, go, gu, gd, xb_h, dyb_h, f1b_h, qh_h, oh_h, hflat_h, lse_h, residual_h, f2b_h, hidden_h, slope_h, dd_h,
    xb, dyb, bv, f1b, qh, oh, hflat, lse, residual, f2b, hidden, slope, dd,
    tbuf, cbuf, gqv, gov, guv, f1, psend, precv,
    ssem, rsem, csem, lsem, wsend, wrecv, msem,
):
    x, k, y = place()
    is_a, is_b = k == y, k != y
    hw = hflat.shape[1]
    heads = hw // HD
    width = tok.shape[2]
    greet([at(x, 1 - k, y), at(1 - x, k, y), at(1 - x, 1 - k, y), at(x, k, 1 - y), at(x, 1 - k, 1 - y)])

    def remote(src, dst, s, r, dest):
        return pltpu.make_async_remote_copy(
            src_ref=src, dst_ref=dst, send_sem=s, recv_sem=r, device_id=dest, device_id_type=MESH
        )

    blocks, wholes = (wq, wo, wu, wd), (gq, go, gu, gd)
    out = Moves(msem)

    def own_sends(w):
        b, g = blocks[w], wholes[w]
        a = [
            remote(b, g.at[2 + k], wsend.at[w, 0], wrecv.at[w, 2 + k], at(1 - x, k, y)),
            remote(b, g.at[k], wsend.at[w, 1], wrecv.at[w, k], at(x, k, 1 - y)),
        ]
        bb = [
            remote(b, g.at[2 + k], wsend.at[w, 0], wrecv.at[w, 2 + k], at(1 - x, 1 - k, y)),
            remote(b, g.at[k], wsend.at[w, 1], wrecv.at[w, k], at(x, 1 - k, 1 - y)),
            remote(b, g.at[k], wsend.at[w, 2], wrecv.at[w, k], at(x, 1 - k, y)),
        ]
        return a, bb

    def relays(w):
        g = wholes[w]
        return (
            remote(g.at[2], g.at[2], wsend.at[w, 3], wrecv.at[w, 2], at(x, k, 1 - y)),
            remote(g.at[1], g.at[3], wsend.at[w, 3], wrecv.at[w, 3], at(1 - x, k, y)),
        )

    def both(fa, fb):
        pl.when(is_a)(fa)
        pl.when(is_b)(fb)

    def start_own(w):
        a, b = own_sends(w)
        both(lambda: [c.start() for c in a] and None, lambda: [c.start() for c in b] and None)

    def arrived(w, j):
        remote(blocks[w], wholes[w].at[j], wsend.at[w, 0], wrecv.at[w, j], at(x, 1 - k, y)).wait_recv()

    def start_relay(w):
        ra, rb = relays(w)

        def fa():
            arrived(w, 2)
            ra.start()

        def fb():
            arrived(w, 1)
            rb.start()

        both(fa, fb)

    def wait_rest(w):
        pl.when(is_b | (k == 1))(lambda: arrived(w, 0))
        pl.when(is_a & (k == 0))(lambda: arrived(w, 1))
        pl.when(is_b)(lambda: arrived(w, 2))
        arrived(w, 3)

    def finish_sends(w):
        a, b = own_sends(w)
        ra, rb = relays(w)
        both(
            lambda: [c.wait_send() for c in a + [ra]] and None,
            lambda: [c.wait_send() for c in b + [rb]] and None,
        )

    def load(w, dst):
        b, g = blocks[w], wholes[w]
        for j in range(4):
            rows = pl.ds(j * width, width)
            local = is_a & (k == j) if j < 2 else None
            if local is None:
                pltpu.make_async_copy(g.at[j], dst.at[rows], lsem.at[j]).start()
            else:
                pl.when(local)(lambda: pltpu.make_async_copy(b, dst.at[rows], lsem.at[j]).start())
                pl.when(jnp.logical_not(local))(
                    lambda: pltpu.make_async_copy(g.at[j], dst.at[rows], lsem.at[j]).start()
                )
        for j in range(4):
            pltpu.make_async_copy(g.at[j], dst.at[pl.ds(j * width, width)], lsem.at[j]).wait()

    tx = remote(tok.at[1 - x], tbuf.at[2 + k], ssem.at[0], rsem.at[0], at(1 - x, k, y))
    cx = remote(cot.at[1 - x], cbuf.at[2 + k], ssem.at[1], rsem.at[1], at(1 - x, k, y))
    t1 = remote(tok.at[x], tbuf.at[k], ssem.at[2], rsem.at[2], at(x, 1 - k, y))
    c1 = remote(cot.at[x], cbuf.at[k], ssem.at[3], rsem.at[3], at(x, 1 - k, y))
    t2 = remote(tbuf.at[2 + k], tbuf.at[2 + k], ssem.at[4], rsem.at[4], at(x, 1 - k, y))
    c2 = remote(cbuf.at[2 + k], cbuf.at[2 + k], ssem.at[5], rsem.at[5], at(x, 1 - k, y))
    bs = remote(bias, bv, ssem.at[6], rsem.at[6], at(x, k, 1 - y))
    pe = remote(psend, precv, ssem.at[7], rsem.at[7], at(x, 1 - k, y))
    tl = pltpu.make_async_copy(tok.at[x], tbuf.at[k], csem.at[0])
    cl = pltpu.make_async_copy(cot.at[x], cbuf.at[k], csem.at[1])
    bl = pltpu.make_async_copy(bias, bv, csem.at[2])

    tx.start()
    t1.start()
    tl.start()
    start_own(0)
    both(lambda: (bl.start(), bs.start()) and None, lambda: None)
    cl.start()
    c1.start()

    tx.wait_recv()
    t2.start()
    tl.wait()
    t1.wait_recv()
    t2.wait_recv()
    for j in range(4):
        xb[:, j * width : (j + 1) * width] = tbuf[j]
    vecs = xb[SEQ - 1 : PADS, :].astype(F32)
    g1, g2, s1, s2, bo = (vecs[j : j + 1] for j in range(1, 6))

    def stats(v):
        mean = jnp.mean(v, axis=1, keepdims=True)
        c = v - mean
        return c * lax.rsqrt(jnp.mean(c * c, axis=1, keepdims=True) + EPS)

    def norm1(r, n):
        f1[pl.ds(r, n), :] = (stats(xb[pl.ds(r, n), :].astype(F32)) * g1 + s1).astype(BF)

    chunks(PADS, 128, norm1)
    f2 = f1
    start_relay(0)
    start_own(1)
    both(bl.wait, bs.wait_recv)
    wait_rest(0)
    load(0, gqv)

    def project(c, n):
        cols = pl.ds(c, n)
        hidden[:, cols] = (nn(f1[...], gqv[:, cols]) + bv[0:1, cols].astype(F32)).astype(BF)

    chunks(gqv.shape[1], 256, project)
    start_relay(1)
    start_own(2)
    for j in range(4):
        f1b[j] = f1[:, j * width : (j + 1) * width]
    qh[...] = jnp.zeros_like(qh)
    for p in range(3):
        for h in range(heads):
            lo = column(p, h, hw)
            qh[p * heads + h, :, 0:HD] = hidden[:, lo : lo + HD]
    out.start(xb, xb_h)
    out.start(f1b, f1b_h)
    out.start(qh, qh_h)
    keymask = jnp.where(lax.broadcasted_iota(jnp.int32, (PADS, 1), 0) < SEQ, 0.0, -1e30)

    def attend(h, carry):
        st = nt(qh[heads + h], qh[h]) + keymask
        top = jnp.max(st, axis=0, keepdims=True)
        e = jnp.exp((st - top) * HD ** (-0.5))
        tot = jnp.sum(e, axis=0, keepdims=True)
        lse[pl.ds(h, 1), :] = top * HD ** (-0.5) + jnp.log(tot)
        out = tn(qh[2 * heads + h], e.astype(BF)) / tot
        oh[h] = out.T.astype(BF)
        return carry

    lax.fori_loop(0, heads, attend, 0)
    for h in range(heads):
        hflat[:, h * HD : (h + 1) * HD] = oh[h, :, 0:HD]
    out.start(oh, oh_h)
    out.start(hflat, hflat_h)
    out.start(lse, lse_h)
    wait_rest(1)
    load(1, gov)

    def out_project(c, n):
        cols = pl.ds(c, n)
        part = nt(hflat[...], gov[cols, :])
        psend[:, cols] = part.astype(BF)
        residual[:, cols] = part

    chunks(4 * width, 384, out_project)
    pe.start()
    pe.wait_recv()

    def norm2(r, n):
        rows = pl.ds(r, n)
        v = xb[rows, :].astype(F32) + bo + residual[rows, :] + precv[rows, :].astype(F32)
        residual[rows, :] = v
        f2[rows, :] = (stats(v) * g2 + s2).astype(BF)

    chunks(PADS, 128, norm2)
    start_relay(2)
    cx.start()
    start_own(3)
    wait_rest(2)
    load(2, guv)
    for j in range(4):
        f2b[j] = f2[:, j * width : (j + 1) * width]
    out.start(residual, residual_h)
    out.start(f2b, f2b_h)

    def expand(c, n):
        cols = pl.ds(c, n)
        u = nn(f2[...], guv[:, cols]) + bv[1:2, cols].astype(F32)
        value, grad = gelu_parts(u)
        hidden[:, cols] = value.astype(BF)
        slope[:, cols] = grad.astype(BF)

    chunks(hidden.shape[1], 256, expand)
    out.start(hidden, hidden_h)
    out.start(slope, slope_h)
    cx.wait_recv()
    c2.start()
    cl.wait()
    c1.wait_recv()
    c2.wait_recv()
    for j in range(4):
        dyb[:, j * width : (j + 1) * width] = cbuf[j]

    def down_grad(j, carry):
        dd[j] = tn(cbuf[j], hidden[...]).astype(BF)
        return carry

    out.start(dyb, dyb_h)
    lax.fori_loop(0, 4, down_grad, 0)
    out.start(dd, dd_h)
    start_relay(3)
    wait_rest(3)
    for c in (tx, cx, t1, c1, t2, c2, pe):
        c.wait_send()
    both(bs.wait_send, lambda: None)
    for w in range(4):
        finish_sends(w)
    out.finish()


def forward(tok, cot, bias, wq, wo, wu, wd):
    width, hw, ff = tok.shape[2], wo.shape[1], wu.shape[1]
    full = 4 * width
    heads = hw // HD
    anyspec = pl.BlockSpec(memory_space=pl.ANY)
    shape = jax.ShapeDtypeStruct
    outs = [
        shape((4,) + wq.shape, BF), shape((4,) + wo.shape, BF), shape((4,) + wu.shape, BF), shape((4,) + wd.shape, BF),
        shape((PADS, full), BF), shape((PADS, full), BF), shape((4, PADS, width), BF),
        shape((3 * heads, PADS, 128), BF), shape((heads, PADS, 128), BF), shape((PADS, hw), BF), shape((heads, PADS), F32),
        shape((PADS, full), F32), shape((4, PADS, width), BF), shape((PADS, ff), BF), shape((PADS, ff), BF),
        shape((4, width, ff), BF),
    ]
    dma = pltpu.SemaphoreType.DMA
    return pl.pallas_call(
        forward_kernel,
        out_shape=outs,
        in_specs=[anyspec] * 7,
        out_specs=[anyspec] * len(outs),
        scratch_shapes=[pltpu.VMEM(o.shape, o.dtype) for o in outs[4:6]] + [pltpu.VMEM(bias.shape, BF)]
        + [pltpu.VMEM(o.shape, o.dtype) for o in outs[6:]]
        + [
            pltpu.VMEM((4, PADS, width), BF), pltpu.VMEM((4, PADS, width), BF),
            pltpu.VMEM((full, wq.shape[1]), BF), pltpu.VMEM((full, hw), BF), pltpu.VMEM((full, ff), BF),
            pltpu.VMEM((PADS, full), BF), pltpu.VMEM((PADS, full), BF), pltpu.VMEM((PADS, full), BF),
            dma((8,)), dma((8,)), dma((3,)), dma((4,)), dma((4, 4)), dma((4, 4)), dma((12,)),
        ],
        compiler_params=pltpu.CompilerParams(collective_id=0, has_side_effects=True, vmem_limit_bytes=VMEM_CAP),
        name="forward",
    )(tok, cot, bias, wq, wo, wu, wd)


def load_weight(b, g, dst, sem, k, is_a):
    width = b.shape[0]
    for j in range(4):
        rows = pl.ds(j * width, width)
        if j < 2:
            local = is_a & (k == j)
            pl.when(local)(lambda: pltpu.make_async_copy(b, dst.at[rows], sem.at[j]).start())
            pl.when(jnp.logical_not(local))(lambda: pltpu.make_async_copy(g.at[j], dst.at[rows], sem.at[j]).start())
        else:
            pltpu.make_async_copy(g.at[j], dst.at[rows], sem.at[j]).start()

    def wait():
        for j in range(4):
            pltpu.make_async_copy(g.at[j], dst.at[pl.ds(j * width, width)], sem.at[j]).wait()

    return wait


def remote(src, dst, s, r, dest):
    return pltpu.make_async_remote_copy(
        src_ref=src, dst_ref=dst, send_sem=s, recv_sem=r, device_id=dest, device_id_type=MESH
    )


class Scatter:
    def __init__(self, d, r, zs, st, sb, cv, ss, rs, ls, spot):
        self.d, self.r, self.zs, self.st, self.sb, self.cv, self.ls, self.spot = d, r, zs, st, sb, cv, ls, spot
        x, k, y = spot
        self.is_a, self.is_b, self.k = k == y, k != y, k
        across, over, mate = at(1 - x, k, y), at(x, k, 1 - y), at(x, 1 - k, y)
        self.x1 = remote(d.at[2], r.at[0], ss.at[0], rs.at[0], across)
        self.y1 = remote(d.at[3], r.at[1], ss.at[1], rs.at[1], over)
        self.y1b = remote(d.at[1], r.at[2], ss.at[2], rs.at[2], over)
        self.x2 = remote(sb, r.at[3], ss.at[1], rs.at[3], across)
        self.y2 = remote(sb, r.at[4], ss.at[3], rs.at[4], over)
        if zs is not None:
            self.home = remote(cv.at[1], zs, ss.at[2], rs.at[5], mate)

    def first(self):
        self.x1.start()

        def b():
            self.y1.start()
            self.y1b.start()

        pl.when(self.is_b)(b)

    def copy_in(self, pairs):
        for i, src in pairs:
            pltpu.make_async_copy(src, self.st.at[i], self.ls.at[i]).start()
        for i, src in pairs:
            pltpu.make_async_copy(src, self.st.at[i], self.ls.at[i]).wait()

    def second(self):
        st, sb = self.st, self.sb

        def fetch_a():
            self.y1.wait_recv()
            self.copy_in([(0, self.d.at[3]), (1, self.r.at[1])])

        def fetch_b():
            self.x1.wait_recv()
            self.copy_in([(0, self.d.at[0]), (1, self.r.at[0])])

        pl.when(self.is_a)(fetch_a)
        pl.when(self.is_b)(fetch_b)

        def add(c, n):
            cols = pl.ds(c, n)
            sb[:, cols] = (st[0, :, cols].astype(F32) + st[1, :, cols].astype(F32)).astype(BF)

        chunks(sb.shape[1], 128, add)
        pl.when(self.is_a)(self.x2.start)
        pl.when(self.is_b)(self.y2.start)

    def settle(self):
        def a():
            self.x1.wait_recv()
            self.y1b.wait_recv()
            self.x2.wait_recv()
            self.y2.wait_recv()

        pl.when(self.is_a)(a)

    def third(self, settled=False):
        if not settled:
            self.settle()
        st, cv = self.st, self.cv
        parts, piece = cv.shape[1], cv.shape[2]

        def a():
            d, r = self.d, self.r
            for which, trio in ((self.k, (d.at[0], r.at[0], r.at[4])), (1 - self.k, (d.at[1], r.at[2], r.at[3]))):
                self.copy_in(list(enumerate(trio)))

                def add(c, n):
                    cols = pl.ds(c, n)
                    total = sum(st[i, :, cols].astype(F32) for i in range(3))
                    for q in range(parts):
                        cv[which, q, :, cols] = total[q * piece : (q + 1) * piece].astype(BF)

                chunks(cv.shape[3], 128, add)
            self.home.start()
            keep = pltpu.make_async_copy(cv.at[0], self.zs, self.ls.at[0])
            keep.start()
            keep.wait()

        pl.when(self.is_a)(a)

    def fourth(self):
        pl.when(self.is_b)(self.home.wait_recv)

    def home_sent(self):
        pl.when(self.is_a)(self.home.wait_send)

    def close(self, home=True):
        self.x1.wait_send()
        pl.when(self.is_a)(self.x2.wait_send)
        if home:
            self.home_sent()

        def b():
            self.y1.wait_send()
            self.y1b.wait_send()
            self.y2.wait_send()

        pl.when(self.is_b)(b)

    @staticmethod
    def peers(spot):
        x, k, y = spot
        return [at(1 - x, k, y), at(x, k, 1 - y), at(x, 1 - k, y)]


def scatter_scratch(rows, cols, parts):
    return [
        pltpu.VMEM((3, rows, cols), BF), pltpu.VMEM((rows, cols), BF), pltpu.VMEM((2, parts, rows // parts, cols), BF),
        pltpu.SemaphoreType.DMA((4,)), pltpu.SemaphoreType.DMA((6,)), pltpu.SemaphoreType.DMA((6,)),
    ]


def norm_back_rows(values, mine, theirs, gain):
    mean = jnp.mean(values, axis=1, keepdims=True)
    center = values - mean
    scale = lax.rsqrt(jnp.mean(center * center, axis=1, keepdims=True) + EPS)
    normed = center * scale
    incoming = mine.astype(F32) + theirs.astype(F32)
    e = incoming * gain
    back = scale * (e - jnp.mean(e, axis=1, keepdims=True) - normed * jnp.mean(e * normed, axis=1, keepdims=True))
    return back, normed, incoming


def fold(acc, i, rows):
    acc[i] += sum(rows[8 * j : 8 * j + 8] for j in range(rows.shape[0] // 8))


def middle_kernel(
    dd, gd, wd, gu, wu, xb_h, dyb_h, residual_h, f2b_h, hidden_h, slope_h,
    rd, outb, du_h, dbr_h, dbrb_h, rowv_h, dbu_h,
    xb, dyb, residual, f2b, hidden, slope, du, dbr, dbrb, rowv, dbu,
    acc, psend, precv, gdv, guv, dup, osend, orecv, full, theirs,
    st, sb, ss, rs, ls, lsem, ps, pr, cs, msem,
):
    spot = place()
    x, k, y = spot
    is_a = k == y
    width = wd.shape[0]
    greet(Scatter.peers(spot))
    ring = Scatter(dd, rd, None, st, sb, None, ss, rs, ls, spot)
    ring.first()
    got_d = load_weight(wd, gd, gdv, lsem.at[0], k, is_a)
    moves = Moves(msem)
    got = [moves.start(a, b) for a, b in ((dyb_h, dyb), (slope_h, slope))]
    got_u = load_weight(wu, gu, guv, lsem.at[1], k, is_a)
    more = [
        moves.start(a, b) for a, b in ((hidden_h, hidden), (f2b_h, f2b), (residual_h, residual), (xb_h, xb))
    ]
    got_d()
    for c in got:
        c.wait()

    def contract(c, n):
        cols = pl.ds(c, n)
        grad = (nn(dyb[...], gdv[:, cols]) * slope[:, cols].astype(F32)).astype(BF)
        dup[:, cols] = grad
        dbu[:, cols] = jnp.sum(grad.astype(F32), axis=0, keepdims=True)

    chunks(slope.shape[1], 256, contract)
    got_u()
    for c in more:
        c.wait()
    tail = [pltpu.make_async_copy(a, b, msem.at[6 + i]) for i, (a, b) in enumerate(
        ((du, du_h), (dbr, dbr_h), (dbrb, dbrb_h), (rowv, rowv_h), (dbu, dbu_h)))]

    def second_grad(c, n):
        rows = pl.ds(c, n)
        psend[:, rows] = nt(dup[...], guv[rows, :]).astype(BF)

    chunks(psend.shape[1], 384, second_grad)
    exchange = remote(psend, precv, ps.at[0], pr.at[0], at(x, 1 - k, y))
    exchange.start()
    low = k == 0
    bd = xb[SEQ - 1 : PADS, :].astype(F32)[6:7]

    def side(a, i):
        lo = 2 * i * width
        return jnp.where(low, a[:, lo : lo + width], a[:, lo + width : lo + 2 * width])

    def down(c, n):
        rows = pl.ds(c, n)
        full[:, rows] = nt(hidden[...], gdv[rows, :])

    chunks(4 * width, 384, down)

    def far(a, i):
        lo = 2 * i * width
        return jnp.where(low, a[:, lo + width : lo + 2 * width], a[:, lo : lo + width])

    for i in range(2):
        osend[i] = far(full, i).astype(BF)
    outs = remote(osend, orecv, ps.at[1], pr.at[1], at(x, 1 - k, y))
    outs.start()
    ring.second()
    outs.wait_recv()
    for i in range(2):
        theirs[i] = (side(full, i) + side(residual, i) + side(bd, i) + orecv[i].astype(F32)).astype(BF)
    mine = pltpu.make_async_copy(theirs.at[0], outb.at[x], cs)
    mine.start()
    away = remote(theirs.at[1], outb.at[x], ps.at[2], pr.at[2], at(1 - x, k, y))
    away.start()

    def up_grad(j, carry):
        du[j] = tn(f2b[j], dup[...]).astype(BF)
        return carry

    lax.fori_loop(0, 4, up_grad, 0)
    tail[0].start()
    exchange.wait_recv()
    g2 = xb[SEQ - 1 : PADS, :].astype(F32)[2:3]
    acc[...] = jnp.zeros_like(acc)

    def norm2(r, n):
        rows = pl.ds(r, n)
        back, normed, incoming = norm_back_rows(residual[rows, :], psend[rows, :], precv[rows, :], g2)
        dyr = dyb[rows, :].astype(F32)
        low = (dyr + back).astype(BF)
        dbr[rows, :] = low
        fold(acc, 0, incoming * normed)
        fold(acc, 1, incoming)
        fold(acc, 2, low.astype(F32))
        fold(acc, 3, dyr)

    chunks(PADS, 128, norm2)
    rowv[...] = jnp.concatenate(
        [jnp.sum(acc[i], axis=0, keepdims=True) for i in range(4)] + [jnp.zeros((4, 4 * width), F32)], axis=0
    )
    for j in range(4):
        dbrb[j] = dbr[:, j * width : (j + 1) * width]
    for c in tail[1:]:
        c.start()
    ring.settle()
    mine.wait()
    remote(theirs.at[1], outb.at[1 - x], ps.at[2], pr.at[2], at(1 - x, k, y)).wait_recv()
    exchange.wait_send()
    outs.wait_send()
    away.wait_send()
    ring.close(home=False)
    for c in tail:
        c.wait()


def middle(dd, gd, wd, gu, wu, xb, dyb, residual, f2b, hidden, slope):
    width, ff = wd.shape
    anyspec = pl.BlockSpec(memory_space=pl.ANY)
    shape = jax.ShapeDtypeStruct
    dma = pltpu.SemaphoreType.DMA
    outs = [
        shape((5, width, ff), BF), shape((2, PADS, width), BF),
        shape((4, width, ff), BF), shape((PADS, 4 * width), BF), shape((4, PADS, width), BF),
        shape((8, 4 * width), F32), shape((1, ff), F32),
    ]
    return pl.pallas_call(
        middle_kernel,
        out_shape=outs,
        in_specs=[anyspec] * 11,
        out_specs=[anyspec] * len(outs),
        scratch_shapes=[
            *(pltpu.VMEM(a.shape, a.dtype) for a in (xb, dyb, residual, f2b, hidden, slope)),
            *(pltpu.VMEM(o.shape, o.dtype) for o in outs[2:]),
            pltpu.VMEM((4, 8, 4 * width), F32), pltpu.VMEM((PADS, 4 * width), BF), pltpu.VMEM((PADS, 4 * width), BF),
            pltpu.VMEM((4 * width, ff), BF), pltpu.VMEM((4 * width, ff), BF), pltpu.VMEM((PADS, ff), BF),
            pltpu.VMEM((2, PADS, width), BF), pltpu.VMEM((2, PADS, width), BF),
            pltpu.VMEM((PADS, 4 * width), F32), pltpu.VMEM((2, PADS, width), BF),
            pltpu.VMEM((3, width, ff), BF), pltpu.VMEM((width, ff), BF), dma((4,)), dma((6,)), dma((6,)),
            dma((2, 4)), dma((3,)), dma((3,)), dma(()), dma((11,)),
        ],
        compiler_params=pltpu.CompilerParams(collective_id=1, has_side_effects=True, vmem_limit_bytes=VMEM_CAP),
        name="middle",
    )(dd, gd, wd, gu, wu, xb, dyb, residual, f2b, hidden, slope)


class DpSum:
    def __init__(self, zs, zr, buf, out, ss, rs, ls):
        self.zs, self.zr, self.buf, self.out, self.ls = zs, zr, buf, out, ls
        size = lax.axis_size("dp")
        self.me = lax.axis_index("dp")
        self.copies = []
        for o in range(1, size):
            dest = lax.rem(self.me + o, size)
            self.copies.append(remote(zs.at[dest], zr.at[o - 1], ss.at[o - 1], rs.at[o - 1], {"dp": dest}))

    def start(self):
        for c in self.copies:
            c.start()

    def finish(self):
        for c in self.copies:
            c.wait_recv()
        sources = [self.zs.at[self.me]] + [self.zr.at[i] for i in range(len(self.copies))]
        for i, src in enumerate(sources):
            pltpu.make_async_copy(src, self.buf.at[i], self.ls.at[i]).start()
        for i, src in enumerate(sources):
            pltpu.make_async_copy(src, self.buf.at[i], self.ls.at[i]).wait()
        buf, out = self.buf, self.out

        def add(c, n):
            cols = pl.ds(c, n)
            out[:, cols] = sum(buf[i, :, cols].astype(F32) for i in range(len(sources)))

        chunks(out.shape[1], 128, add)

    def close(self):
        for c in self.copies:
            c.wait_send()


def backward_kernel(
    du, dd, rd, go, wo, gq, wq, xb_h, f1b_h, hflat_h, qh_h, oh_h, lse_h, dbr_h, dbrb_h, vec2_h, dbu_h,
    zsd, ru, zsu, ro, zso, ra, zsa, rb, zsb, zrd, zru, zro, zra, zrb, gin,
    td, tu, to, ta, tb, rowt, colt,
    xb, f1b, hflat, qh, oh, lse, dbr, dbrb, vec2, dbu,
    acc, gov, gqv, dh, dqh, dqkv, ps, pr, do, dq, home,
    stu, sbu, cvu, ssu, rsu, lsu, sto, sbo, cvo, sso, rso, lso,
    sta, sba, cva, ssa, rsa, lsa, stb, sbb, cvb, ssb, rsb, lsb, ssd, rsd,
    rowb, colv, rr, cr, rsum, csum, rz, cz, lsem, zss, zrs, zls, es, er, hs, hr, cs, vs, vr, ws, wr, msem,
):
    spot = place()
    x, k, y = spot
    is_a, is_b = k == y, k != y
    width, hw = xb.shape[1] // 4, hflat.shape[1]
    heads = hw // HD
    size, me = lax.axis_size("dp"), lax.axis_index("dp")
    summed = cvu.shape[1] > 1
    plane = [at(1 - x, k, y), at(x, k, 1 - y), at(1 - x, k, 1 - y)]
    plane += [at(x, 1 - k, y), at(1 - x, 1 - k, y), at(x, 1 - k, 1 - y), at(1 - x, 1 - k, 1 - y)]
    greet(plane + [{"dp": lax.rem(me + o, size)} for o in range(1, size)])
    side = jnp.where(is_a, 0, 1)
    row_sends = [
        remote(rowb.at[k if i == 1 else 2 + k], rr.at[i], vs.at[i], vr.at[i], plane[i]) for i in range(3)
    ]
    col_sends = [
        remote(colv, cr.at[side], vs.at[3], vr.at[3 + side], at(x, 1 - k, k)),
        remote(colv, cr.at[2 + side], vs.at[4], vr.at[5 + side], at(1 - x, k, k)),
        remote(colv, cr.at[2 + side], vs.at[5], vr.at[5 + side], at(1 - x, 1 - k, k)),
    ]
    col_extra = remote(colv, cr.at[1], vs.at[6], vr.at[4], at(x, k, k))
    dp_sends = []
    for o in range(1, size):
        dest = {"dp": lax.rem(me + o, size)}
        dp_sends.append(remote(rsum, rz.at[o - 1], ws.at[0, o - 1], wr.at[0, o - 1], dest))
        dp_sends.append(remote(csum, cz.at[o - 1], ws.at[1, o - 1], wr.at[1, o - 1], dest))
    ring_u = Scatter(du, ru, zsu, stu, sbu, cvu, ssu, rsu, lsu, spot)
    ring_u.first()
    moves = Moves(msem)
    got = [moves.start(a, b) for a, b in ((dbr_h, dbr), (hflat_h, hflat), (dbrb_h, dbrb))]
    got_o = load_weight(wo, go, gov, lsem.at[0], k, is_a)
    more = [
        moves.start(a, b)
        for a, b in ((qh_h, qh), (oh_h, oh), (lse_h, lse), (f1b_h, f1b), (xb_h, xb), (vec2_h, vec2), (dbu_h, dbu))
    ]
    got_q = load_weight(wq, gq, gqv, lsem.at[1], k, is_a)
    ring_d = Scatter(dd, rd, zsd, stu, sbu, cvu, ssd, rsd, lsu, spot)
    ring_o = Scatter(do, ro, zso, sto, sbo, cvo, sso, rso, lso, spot)
    ring_a = Scatter(dq.at[0], ra, zsa, sta, sba, cva, ssa, rsa, lsa, spot)
    ring_b = Scatter(dq.at[1], rb, zsb, stb, sbb, cvb, ssb, rsb, lsb, spot)
    if summed:
        sums = [
            DpSum(zs, zr, cv.at[0], t, zss.at[i], zrs.at[i], zls.at[i])
            for i, (zs, zr, cv, t) in enumerate(
                ((zsd, zrd, cvu, td), (zsu, zru, cvu, tu), (zso, zro, cvo, to), (zsa, zra, cva, ta), (zsb, zrb, cvb, tb))
            )
        ]
    dh[...] = jnp.zeros_like(dh)
    for c in got:
        c.wait()
    got_o()
    dqkv[:, 0:hw] = nn(dbr[...], gov[...]).astype(BF)
    for h in range(heads):
        dh[h, :, 0:HD] = dqkv[:, h * HD : (h + 1) * HD]

    def out_grad(j, carry):
        do[j] = tn(hflat[...], dbrb[j]).astype(BF)
        return carry

    lax.fori_loop(0, 4, out_grad, 0)
    ring_o.first()
    for c in more:
        c.wait()
    keymask = jnp.where(lax.broadcasted_iota(jnp.int32, (PADS, 1), 0) < SEQ, 0.0, -1e30)
    ones = jnp.ones((8, 128), F32)

    def attend(h, carry):
        q, kk, v, g = qh[h], qh[heads + h], qh[2 * heads + h], dh[h]
        p = jnp.exp(nt(kk, q) * HD ** (-0.5) + keymask - lse[pl.ds(h, 1), :])
        delta = lax.dot_general(
            ones, g.astype(F32) * oh[h].astype(F32), (((1,), (1,)), ((), ())),
            precision=lax.Precision.HIGHEST, preferred_element_type=F32,
        )[0:1]
        ds = (p * (nt(v, g) - delta)).astype(BF)
        dqh[2 * heads + h] = nn(p.astype(BF), g).astype(BF)
        dqh[heads + h] = (nn(ds, q) * HD ** (-0.5)).astype(BF)
        dqh[h] = (tn(kk, ds) * HD ** (-0.5)).T.astype(BF)
        return carry

    half_cols, group = dq.shape[3], heads // 2

    def one_half(half, carry):
        lax.fori_loop(half * group, (half + 1) * group, attend, 0)
        cols = pl.ds(pl.multiple_of(half * half_cols, 128), half_cols)
        block = dqkv.at[:, cols]
        for p in range(3):
            for i in range(group):
                lo = (p * group + i) * HD
                block[:, lo : lo + HD] = dqh[p * heads + half * group + i, :, 0:HD]
        block[:, 3 * group * HD :] = jnp.zeros((PADS, half_cols - 3 * group * HD), BF)

        def qkv_grad(j, c):
            dq[half, j] = tn(f1b[j], block[...]).astype(BF)
            return c

        lax.fori_loop(0, 4, qkv_grad, 0)

        @pl.when(half == 0)
        def _():
            ring_u.second()
            ring_a.first()
            ring_d.third(settled=True)
            ring_d.fourth()
            if summed:
                sums[0].start()

        return carry

    lax.fori_loop(0, 2, one_half, 0)
    ring_b.first()
    ring_o.second()
    got_q()

    def first_grad(c, n):
        rows = pl.ds(c, n)
        ps[:, rows] = nt(dqkv[...], gqv[rows, :]).astype(BF)

    chunks(ps.shape[1], 384, first_grad)
    exchange = remote(ps, pr, es, er, at(x, 1 - k, y))
    exchange.start()
    ring_d.home_sent()
    ring_u.third()
    ring_u.fourth()
    ring_a.second()
    if summed:
        sums[1].start()

    def bias_grad(c, n):
        cols = pl.ds(c, n)
        colv[0:1, cols] = jnp.sum(dqkv[:, cols].astype(F32), axis=0, keepdims=True)

    chunks(dqkv.shape[1], 128, bias_grad)
    colv[1:2, :] = dbu[...]
    exchange.wait_recv()
    exchange.wait_send()
    g1 = xb[SEQ - 1 : PADS, :].astype(F32)[1:2]
    acc[...] = jnp.zeros_like(acc)

    def norm1(r, n):
        rows = pl.ds(r, n)
        back, normed, incoming = norm_back_rows(xb[rows, :].astype(F32), ps[rows, :], pr[rows, :], g1)
        ps[rows, :] = (dbr[rows, :].astype(F32) + back).astype(BF)
        fold(acc, 0, incoming * normed)
        fold(acc, 1, incoming)

    chunks(PADS, 128, norm1)
    gain, shift = (jnp.sum(acc[i], axis=0, keepdims=True) for i in range(2))
    rows6 = jnp.concatenate(
        [gain, vec2[0:1], shift, vec2[1:2], vec2[2:3], vec2[3:4], jnp.zeros((2, 4 * width), F32)], axis=0
    )
    for j in range(4):
        rowb[j] = rows6[:, j * width : (j + 1) * width]
    for c in row_sends + col_sends:
        c.start()
    pl.when(is_b)(col_extra.start)
    low = k == 0
    for i in range(2):
        lo = 2 * i * width
        home[i] = jnp.where(low, ps[:, lo : lo + width], ps[:, lo + width : lo + 2 * width])
    mine = pltpu.make_async_copy(home.at[0], gin.at[x], cs)
    mine.start()
    away = remote(home.at[1], gin.at[x], hs, hr, at(1 - x, k, y))
    away.start()
    ring_b.second()
    ring_o.third()
    ring_o.fourth()
    if summed:
        sums[0].finish()
        sums[2].start()
    ring_a.third()
    ring_a.fourth()
    if summed:
        sums[3].start()
    for c in row_sends:
        c.wait_recv()
    for i in range(1, 4):
        remote(colv, cr.at[i], vs.at[3], vr.at[3 + i], at(x, 1 - k, k)).wait_recv()
    pl.when(is_b)(lambda: remote(colv, cr.at[0], vs.at[3], vr.at[3], at(x, 1 - k, k)).wait_recv())
    rsum[...] = rowb[k] + rr[0] + rr[1] + rr[2]

    @pl.when(is_a)
    def _():
        csum[...] = colv[...] + cr[1] + cr[2] + cr[3]

    @pl.when(is_b)
    def _():
        csum[...] = cr[0] + cr[1] + cr[2] + cr[3]

    for c in dp_sends:
        c.start()
    ring_b.third()
    ring_b.fourth()
    if summed:
        sums[4].start()
        sums[1].finish()
    mine.wait()
    remote(home.at[1], gin.at[1 - x], hs, hr, at(1 - x, k, y)).wait_recv()
    away.wait_send()
    for ring in (ring_u, ring_o, ring_a, ring_b):
        ring.close()
    for c in row_sends + col_sends:
        c.wait_send()
    pl.when(is_b)(col_extra.wait_send)
    for c in dp_sends:
        c.wait_recv()
        c.wait_send()
    rowt[...] = rsum[...] + sum(rz[o] for o in range(size - 1))
    colt[...] = csum[...] + sum(cz[o] for o in range(size - 1))
    if summed:
        for total in sums[2:]:
            total.finish()
        for total in sums:
            total.close()


def backward(parts, du, dd, rd, go, wo, gq, wq, xb, f1b, hflat, qh, oh, lse, dbr, dbrb, vec2, dbu):
    width, ff = du.shape[1:]
    hw, nq = wo.shape[1], wq.shape[1]
    full, heads = 4 * width, hw // HD
    anyspec = pl.BlockSpec(memory_space=pl.ANY)
    vspec = pl.BlockSpec(memory_space=pltpu.VMEM)
    shape = jax.ShapeDtypeStruct
    dma = pltpu.SemaphoreType.DMA
    others = max(parts - 1, 1)
    peers = lax.axis_size("dp") - 1
    piece, slab = width // parts, hw // parts
    nh = nq // 2
    outs = [
        shape((parts, piece, ff), BF), shape((5, width, ff), BF), shape((parts, piece, ff), BF),
        shape((5, hw, width), BF), shape((parts, slab, width), BF),
        shape((5, width, nh), BF), shape((parts, piece, nh), BF), shape((5, width, nh), BF), shape((parts, piece, nh), BF),
        shape((others, piece, ff), BF), shape((others, piece, ff), BF), shape((others, slab, width), BF),
        shape((others, piece, nh), BF), shape((others, piece, nh), BF), shape((2, PADS, width), BF),
        *(
            shape(d if parts > 1 else (8, 128), F32)
            for d in ((piece, ff), (piece, ff), (slab, width), (piece, nh), (piece, nh))
        ),
        shape((8, width), F32), shape((2, ff), F32),
    ]
    return pl.pallas_call(
        backward_kernel,
        out_shape=outs,
        in_specs=[anyspec] * 17,
        out_specs=[anyspec] * 15 + [vspec] * 7,
        scratch_shapes=[pltpu.VMEM(a.shape, a.dtype) for a in (xb, f1b, hflat, qh, oh, lse, dbr, dbrb, vec2, dbu)]
        + [
            pltpu.VMEM((2, 8, full), F32), pltpu.VMEM((full, hw), BF), pltpu.VMEM((full, nq), BF),
            pltpu.VMEM((heads, PADS, 128), BF), pltpu.VMEM((3 * heads, PADS, 128), BF), pltpu.VMEM((PADS, nq), BF),
            pltpu.VMEM((PADS, full), BF), pltpu.VMEM((PADS, full), BF),
            pltpu.VMEM((4, hw, width), BF), pltpu.VMEM((2, 4, width, nh), BF), pltpu.VMEM((2, PADS, width), BF),
        ]
        + scatter_scratch(width, ff, parts) + scatter_scratch(hw, width, parts)
        + scatter_scratch(width, nh, parts) + scatter_scratch(width, nh, parts) + [dma((4,)), dma((6,))]
        + [
            pltpu.VMEM((4, 8, width), F32), pltpu.VMEM((2, ff), F32), pltpu.VMEM((3, 8, width), F32), pltpu.VMEM((4, 2, ff), F32),
            pltpu.VMEM((8, width), F32), pltpu.VMEM((2, ff), F32), pltpu.VMEM((peers, 8, width), F32), pltpu.VMEM((peers, 2, ff), F32),
        ]
        + [dma((2, 4)), dma((5, others)), dma((5, others)), dma((5, others + 1)), dma(()), dma(()), dma(()), dma(()), dma(()),
           dma((7,)), dma((7,)), dma((2, peers)), dma((2, peers)), dma((10,))],
        compiler_params=pltpu.CompilerParams(collective_id=2, has_side_effects=True, vmem_limit_bytes=VMEM_CAP),
        name="backward",
    )(du, dd, rd, go, wo, gq, wq, xb, f1b, hflat, qh, oh, lse, dbr, dbrb, vec2, dbu)


def shards(tokens, ln_gain, ln_bias, w_qkv, b_qv, w_out, b_out, w_up, b_up, w_down, b_down, cotangent):
    width = tokens.shape[1]
    hw = b_qv.shape[1]

    extra = jnp.concatenate(
        [ln_gain, ln_bias, b_out[None], b_down[None], jnp.zeros((1, width), BF)], axis=0
    )
    images = tokens.shape[0] // SEQ
    blank = jnp.zeros((PADS - SEQ, width), BF)

    def with_rows(a, tail):
        return jnp.stack([jnp.concatenate([a[i * SEQ : (i + 1) * SEQ], tail]) for i in range(images)])

    tok2, cot2 = with_rows(tokens, extra), with_rows(cotangent, blank)
    ff = b_up.shape[0]
    nq, hh = padded(hw), hw // 2
    gap = jnp.zeros((nq // 2 - 3 * hh,), BF)
    nil = jnp.zeros((hh,), BF)
    bqkv = jnp.concatenate(
        [b_qv[0, :hh], nil, b_qv[1, :hh], gap, b_qv[0, hh:], nil, b_qv[1, hh:], gap, jnp.zeros((ff - nq,), BF)]
    )
    bias = jnp.concatenate([bqkv[None], b_up[None], jnp.zeros((14, ff), BF)])
    side = jnp.zeros((width, gap.shape[0]), BF)
    qblock = jnp.concatenate(
        [w_qkv[:, p, i * hh : (i + 1) * hh] if p < 3 else side for i in range(2) for p in range(4)], axis=1
    )
    wot, wdt = w_out.T, w_down.T
    gq, go, gu, gd, xb, dy, f1b, qh, oh, hflat, lse, residual, f2b, hidden, slope, dd = forward(
        tok2, cot2, bias, qblock, wot, w_up, wdt
    )
    dp_size = lax.axis_size("dp")
    parts = dp_size if width % dp_size == 0 and (width // dp_size) % 8 == 0 else 1
    rd, outb, du, dbr, dbrb, vec2, dbu = middle(dd, gd, wdt, gu, w_up, xb, dy, residual, f2b, hidden, slope)
    output = jnp.concatenate([outb[i, :SEQ] for i in range(images)])
    back = backward(parts, du, dd, rd, go, wot, gq, qblock, xb, f1b, hflat, qh, oh, lse, dbr, dbrb, vec2, dbu)
    zsd, _, zsu, _, zso, _, zsa, _, zsb = back[:9]
    gin, td, tu, to, ta, tb, rowt, colt = back[14:]
    input_grad = jnp.concatenate([gin[i, :SEQ] for i in range(images)])
    if parts == 1:

        def over_dp(a):
            return lax.psum_scatter(a[0], "dp", scatter_dimension=0, tiled=True).astype(F32)

        td, tu, to, ta, tb = (over_dp(a) for a in (zsd, zsu, zso, zsa, zsb))

    return (
        output,
        input_grad,
        rowt[0:2],
        rowt[2:4],
        jnp.concatenate([a[:, : 3 * hh].reshape(-1, 3, hh) for a in (ta, tb)], axis=2),
        jnp.stack(
            [jnp.concatenate([colt[0, i * nq // 2 + p * hh :][:hh] for i in range(2)]) for p in (0, 2)]
        ),
        to,
        rowt[4],
        tu,
        colt[1],
        td.T,
        rowt[5],
    )


def solution(mesh):
    placed = (
        P(("dp", "col"), "row"),
        P(None, "row"),
        P(None, "row"),
        P("row", None, "col"),
        P(None, "col"),
        P("col", "row"),
        P("row"),
        P("row", "col"),
        P("col"),
        P("col", "row"),
        P("row"),
        P(("dp", "col"), "row"),
    )
    return jax.shard_map(
        shards,
        mesh=mesh,
        in_specs=placed,
        out_specs=(
            P(("dp", "col"), "row"),
            P(("dp", "col"), "row"),
            P(None, "row"),
            P(None, "row"),
            P(("row", "dp"), None, "col"),
            P(None, "col"),
            P(("col", "dp"), "row"),
            P("row"),
            P(("row", "dp"), "col"),
            P("col"),
            P("col", ("row", "dp")),
            P("row"),
        ),
        check_vma=False,
    )
```

```python
import types

import jax
import jax.numpy as jnp
from jax import lax
from jax.experimental import pallas as pl
from jax.experimental.pallas import tpu as pltpu
from jax.sharding import PartitionSpec as P

HD = 72
SEQ = 729
EPS = 1e-06
BF = jnp.bfloat16
F32 = jnp.float32


def nn(a, b):
    return jnp.dot(a, b, preferred_element_type=F32)


def nt(a, b):
    return lax.dot_general(a, b, (((1,), (1,)), ((), ())), preferred_element_type=F32)


def tn(a, b):
    return lax.dot_general(a, b, (((0,), (0,)), ((), ())), preferred_element_type=F32)


def gelu_parts(u):
    t = jnp.tanh(0.7978845608028654 * (u + 0.044715 * u * u * u))
    value = 0.5 * u * (1.0 + t)
    slope = 0.5 * (1.0 + t) + 0.5 * u * (1.0 - t * t) * 0.7978845608028654 * (1.0 + 3 * 0.044715 * u * u)
    return value, slope


MESH = pl.DeviceIdType.MESH
PADS = 736
VMEM_CAP = 66_000_000


def place():
    row, col = lax.axis_index("row"), lax.axis_index("col")
    return row // 2, lax.rem(row, 2), col


def at(x, k, y):
    return {"row": 2 * x + k, "col": y}


def greet(peers):
    barrier = pltpu.get_barrier_semaphore()
    for peer in peers:
        pl.semaphore_signal(barrier, inc=1, device_id=peer, device_id_type=MESH)
    pl.semaphore_wait(barrier, len(peers))


def chunks(total, step, body):
    whole = total // step
    if whole > 0:
        lax.fori_loop(0, whole, lambda i, c: (body(pl.multiple_of(i * step, step), step), c)[1], 0)
    if total % step:
        body(whole * step, total % step)


def column(part, head, hw):
    half, left = divmod(head, hw // HD // 2)
    return half * (padded(hw) // 2) + part * (hw // 2) + left * HD


def padded(hw):
    return 2 * (-(-3 * hw // 2 // 128) * 128)


class Moves:
    def __init__(self, sems):
        self.sems, self.open = sems, {}

    def start(self, src, dst):
        c = pltpu.make_async_copy(src, dst, self.sems.at[len(self.open)])
        c.start()
        self.open[len(self.open)] = c
        return c

    def finish(self):
        for c in self.open.values():
            c.wait()


def forward_phase(
    tok, cot, bias, wq, wo, wu, wd,
    gq, go, gu, gd, xb_h, dyb_h, f1b_h, qh_h, oh_h, hflat_h, lse_h, residual_h, f2b_h, hidden_h, slope_h, dd_h,
    tbuf, cbuf, bv, precv, ssem, rsem, csem, lsem, wsend, wrecv, msem, spot, after,
    xb, dyb, f1b, qh, oh, hflat, lse, residual, f2b, hidden, slope, dd, tb, gqv, gov, guv, f1, psend,
):
    x, k, y = spot
    is_a, is_b = k == y, k != y
    hw = hflat.shape[1]
    heads = hw // HD
    width = tok.shape[2]
    blocks, wholes = (wq, wo, wu, wd), (gq, go, gu, gd)
    out = Moves(msem)

    def own_sends(w):
        b, g = blocks[w], wholes[w]
        a = [
            remote(b, g.at[2 + k], wsend.at[w, 0], wrecv.at[w, 2 + k], at(1 - x, k, y)),
            remote(b, g.at[k], wsend.at[w, 1], wrecv.at[w, k], at(x, k, 1 - y)),
        ]
        bb = [
            remote(b, g.at[2 + k], wsend.at[w, 0], wrecv.at[w, 2 + k], at(1 - x, 1 - k, y)),
            remote(b, g.at[k], wsend.at[w, 1], wrecv.at[w, k], at(x, 1 - k, 1 - y)),
            remote(b, g.at[k], wsend.at[w, 2], wrecv.at[w, k], at(x, 1 - k, y)),
        ]
        return a, bb

    def relays(w):
        g = wholes[w]
        return (
            remote(g.at[2], g.at[2], wsend.at[w, 3], wrecv.at[w, 2], at(x, k, 1 - y)),
            remote(g.at[1], g.at[3], wsend.at[w, 3], wrecv.at[w, 3], at(1 - x, k, y)),
        )

    def both(fa, fb):
        pl.when(is_a)(fa)
        pl.when(is_b)(fb)

    def start_own(w):
        a, b = own_sends(w)
        both(lambda: [c.start() for c in a] and None, lambda: [c.start() for c in b] and None)

    def arrived(w, j):
        remote(blocks[w], wholes[w].at[j], wsend.at[w, 0], wrecv.at[w, j], at(x, 1 - k, y)).wait_recv()

    def start_relay(w):
        ra, rb = relays(w)

        def fa():
            arrived(w, 2)
            ra.start()

        def fb():
            arrived(w, 1)
            rb.start()

        both(fa, fb)

    def wait_rest(w):
        pl.when(is_b | (k == 1))(lambda: arrived(w, 0))
        pl.when(is_a & (k == 0))(lambda: arrived(w, 1))
        pl.when(is_b)(lambda: arrived(w, 2))
        arrived(w, 3)

    def finish_sends(w):
        a, b = own_sends(w)
        ra, rb = relays(w)
        both(
            lambda: [c.wait_send() for c in a + [ra]] and None,
            lambda: [c.wait_send() for c in b + [rb]] and None,
        )

    def load(w, dst):
        b, g = blocks[w], wholes[w]
        for j in range(4):
            rows = pl.ds(j * width, width)
            local = is_a & (k == j) if j < 2 else None
            if local is None:
                pltpu.make_async_copy(g.at[j], dst.at[rows], lsem.at[j]).start()
            else:
                pl.when(local)(lambda: pltpu.make_async_copy(b, dst.at[rows], lsem.at[j]).start())
                pl.when(jnp.logical_not(local))(
                    lambda: pltpu.make_async_copy(g.at[j], dst.at[rows], lsem.at[j]).start()
                )
        for j in range(4):
            pltpu.make_async_copy(g.at[j], dst.at[pl.ds(j * width, width)], lsem.at[j]).wait()

    tx = remote(tok.at[1 - x], tbuf.at[2 + k], ssem.at[0], rsem.at[0], at(1 - x, k, y))
    cx = remote(cot.at[1 - x], cbuf.at[2 + k], ssem.at[1], rsem.at[1], at(1 - x, k, y))
    t1 = remote(tok.at[x], tbuf.at[k], ssem.at[2], rsem.at[2], at(x, 1 - k, y))
    c1 = remote(cot.at[x], cbuf.at[k], ssem.at[3], rsem.at[3], at(x, 1 - k, y))
    t2 = remote(tbuf.at[2 + k], tbuf.at[2 + k], ssem.at[4], rsem.at[4], at(x, 1 - k, y))
    c2 = remote(cbuf.at[2 + k], cbuf.at[2 + k], ssem.at[5], rsem.at[5], at(x, 1 - k, y))
    bs = remote(bias, bv, ssem.at[6], rsem.at[6], at(x, k, 1 - y))
    pe = remote(psend, precv, ssem.at[7], rsem.at[7], at(x, 1 - k, y))

    def collect(src, buf, wide):
        parts = [(src.at[x], k), (buf.at[1 - k], 1 - k), (buf.at[2], 2), (buf.at[3], 3)]
        copies = [pltpu.make_async_copy(a, tb.at[j], lsem.at[i]) for i, (a, j) in enumerate(parts)]
        for c in copies:
            c.start()
        for c in copies:
            c.wait()
        for j in range(4):
            wide[:, j * width : (j + 1) * width] = tb[j]

    bl = pltpu.make_async_copy(bias, bv, csem.at[2])

    tx.start()
    t1.start()
    start_own(0)
    both(lambda: (bl.start(), bs.start()) and None, lambda: None)
    c1.start()

    tx.wait_recv()
    t2.start()
    t1.wait_recv()
    t2.wait_recv()
    collect(tok, tbuf, xb)
    vecs = xb[SEQ - 1 : PADS, :].astype(F32)
    g1, g2, s1, s2, bo = (vecs[j : j + 1] for j in range(1, 6))

    def stats(v):
        mean = jnp.mean(v, axis=1, keepdims=True)
        c = v - mean
        return c * lax.rsqrt(jnp.mean(c * c, axis=1, keepdims=True) + EPS)

    def norm1(r, n):
        f1[pl.ds(r, n), :] = (stats(xb[pl.ds(r, n), :].astype(F32)) * g1 + s1).astype(BF)

    chunks(PADS, 128, norm1)
    f2 = f1
    start_relay(0)
    start_own(1)
    both(bl.wait, bs.wait_recv)
    wait_rest(0)
    load(0, gqv)

    def project(c, n):
        cols = pl.ds(c, n)
        hidden[:, cols] = (nn(f1[...], gqv[:, cols]) + bv[0:1, cols].astype(F32)).astype(BF)

    chunks(gqv.shape[1], 256, project)
    start_relay(1)
    start_own(2)
    for j in range(4):
        f1b[j] = f1[:, j * width : (j + 1) * width]
    qh[...] = jnp.zeros_like(qh)
    for p in range(3):
        for h in range(heads):
            lo = column(p, h, hw)
            qh[p * heads + h, :, 0:HD] = hidden[:, lo : lo + HD]
    out.start(xb, xb_h)
    out.start(f1b, f1b_h)
    out.start(qh, qh_h)
    keymask = jnp.where(lax.broadcasted_iota(jnp.int32, (PADS, 1), 0) < SEQ, 0.0, -1e30)

    def attend(h, carry):
        st = nt(qh[heads + h], qh[h]) + keymask
        top = jnp.max(st, axis=0, keepdims=True)
        e = jnp.exp((st - top) * HD ** (-0.5))
        tot = jnp.sum(e, axis=0, keepdims=True)
        lse[pl.ds(h, 1), :] = top * HD ** (-0.5) + jnp.log(tot)
        out = tn(qh[2 * heads + h], e.astype(BF)) / tot
        oh[h] = out.T.astype(BF)
        return carry

    lax.fori_loop(0, heads, attend, 0)
    for h in range(heads):
        hflat[:, h * HD : (h + 1) * HD] = oh[h, :, 0:HD]
    out.start(oh, oh_h)
    out.start(hflat, hflat_h)
    out.start(lse, lse_h)
    wait_rest(1)
    load(1, gov)

    def out_project(c, n):
        cols = pl.ds(c, n)
        part = nt(hflat[...], gov[cols, :])
        psend[:, cols] = part.astype(BF)
        residual[:, cols] = part

    chunks(4 * width, 384, out_project)
    pe.start()
    pe.wait_recv()

    def norm2(r, n):
        rows = pl.ds(r, n)
        v = xb[rows, :].astype(F32) + bo + residual[rows, :] + precv[rows, :].astype(F32)
        residual[rows, :] = v
        f2[rows, :] = (stats(v) * g2 + s2).astype(BF)

    chunks(PADS, 128, norm2)
    start_relay(2)
    cx.start()
    start_own(3)
    wait_rest(2)
    load(2, guv)
    for j in range(4):
        f2b[j] = f2[:, j * width : (j + 1) * width]
    out.start(residual, residual_h)
    out.start(f2b, f2b_h)

    def expand(c, n):
        cols = pl.ds(c, n)
        u = nn(f2[...], guv[:, cols]) + bv[1:2, cols].astype(F32)
        value, grad = gelu_parts(u)
        hidden[:, cols] = value.astype(BF)
        slope[:, cols] = grad.astype(BF)

    chunks(hidden.shape[1], 256, expand)
    out.start(hidden, hidden_h)
    out.start(slope, slope_h)
    cx.wait_recv()
    c2.start()
    c1.wait_recv()
    c2.wait_recv()
    collect(cot, cbuf, dyb)

    def down_grad(j, carry):
        dd[j] = tn(tb[j], hidden[...]).astype(BF)
        return carry

    out.start(dyb, dyb_h)
    start_relay(3)
    lax.fori_loop(0, 4, down_grad, 0)
    out.start(dd, dd_h)
    out.finish()
    wait_rest(3)
    after()
    for c in (tx, cx, t1, c1, t2, c2, pe):
        c.wait_send()
    both(bs.wait_send, lambda: None)
    for w in range(4):
        finish_sends(w)


def load_weight(b, g, dst, sem, k, is_a):
    width = b.shape[0]
    for j in range(4):
        rows = pl.ds(j * width, width)
        if j < 2:
            local = is_a & (k == j)
            pl.when(local)(lambda: pltpu.make_async_copy(b, dst.at[rows], sem.at[j]).start())
            pl.when(jnp.logical_not(local))(lambda: pltpu.make_async_copy(g.at[j], dst.at[rows], sem.at[j]).start())
        else:
            pltpu.make_async_copy(g.at[j], dst.at[rows], sem.at[j]).start()

    def wait():
        for j in range(4):
            pltpu.make_async_copy(g.at[j], dst.at[pl.ds(j * width, width)], sem.at[j]).wait()

    return wait


def remote(src, dst, s, r, dest):
    return pltpu.make_async_remote_copy(
        src_ref=src, dst_ref=dst, send_sem=s, recv_sem=r, device_id=dest, device_id_type=MESH
    )


class Scatter:
    def __init__(self, d, r, zs, st, sb, cv, ss, rs, ls, spot):
        self.d, self.r, self.zs, self.st, self.sb, self.cv, self.ls, self.spot = d, r, zs, st, sb, cv, ls, spot
        x, k, y = spot
        self.is_a, self.is_b, self.k = k == y, k != y, k
        across, over, mate = at(1 - x, k, y), at(x, k, 1 - y), at(x, 1 - k, y)
        self.x1 = remote(d.at[2], r.at[0], ss.at[0], rs.at[0], across)
        self.y1 = remote(d.at[3], r.at[1], ss.at[1], rs.at[1], over)
        self.y1b = remote(d.at[1], r.at[2], ss.at[2], rs.at[2], over)
        if sb is not None:
            self.x2 = remote(sb, r.at[3], ss.at[1], rs.at[3], across)
            self.y2 = remote(sb, r.at[4], ss.at[3], rs.at[4], over)
        if zs is not None:
            self.home = remote(cv.at[1], zs, ss.at[2], rs.at[5], mate)

    def first(self):
        self.x1.start()

        def b():
            self.y1.start()
            self.y1b.start()

        pl.when(self.is_b)(b)

    def copy_in(self, pairs):
        for i, src in pairs:
            pltpu.make_async_copy(src, self.st.at[i], self.ls.at[i]).start()
        for i, src in pairs:
            pltpu.make_async_copy(src, self.st.at[i], self.ls.at[i]).wait()

    def second(self):
        st, sb = self.st, self.sb

        def fetch_a():
            self.y1.wait_recv()
            self.copy_in([(0, self.d.at[3]), (1, self.r.at[1])])

        def fetch_b():
            self.x1.wait_recv()
            self.copy_in([(0, self.d.at[0]), (1, self.r.at[0])])

        pl.when(self.is_a)(fetch_a)
        pl.when(self.is_b)(fetch_b)

        def add(c, n):
            cols = pl.ds(c, n)
            sb[:, cols] = (st[0, :, cols].astype(F32) + st[1, :, cols].astype(F32)).astype(BF)

        chunks(sb.shape[1], 128, add)
        pl.when(self.is_a)(self.x2.start)
        pl.when(self.is_b)(self.y2.start)

    def settle(self):
        def a():
            self.x1.wait_recv()
            self.y1b.wait_recv()
            self.x2.wait_recv()
            self.y2.wait_recv()

        pl.when(self.is_a)(a)

    def third(self):
        self.settle()
        st, cv = self.st, self.cv
        parts, piece = cv.shape[1], cv.shape[2]

        def a():
            d, r = self.d, self.r
            for which, trio in ((self.k, (d.at[0], r.at[0], r.at[4])), (1 - self.k, (d.at[1], r.at[2], r.at[3]))):
                self.copy_in(list(enumerate(trio)))

                def add(c, n):
                    cols = pl.ds(c, n)
                    total = sum(st[i, :, cols].astype(F32) for i in range(3))
                    for q in range(parts):
                        cv[which, q, :, cols] = total[q * piece : (q + 1) * piece].astype(BF)

                chunks(cv.shape[3], 128, add)
            self.home.start()
            keep = pltpu.make_async_copy(cv.at[0], self.zs, self.ls.at[0])
            keep.start()
            keep.wait()

        pl.when(self.is_a)(a)

    def fourth(self):
        pl.when(self.is_b)(self.home.wait_recv)

    def home_sent(self):
        pl.when(self.is_a)(self.home.wait_send)

    def close(self, home=True):
        self.x1.wait_send()
        pl.when(self.is_a)(self.x2.wait_send)
        if home:
            self.home_sent()

        def b():
            self.y1.wait_send()
            self.y1b.wait_send()
            self.y2.wait_send()

        pl.when(self.is_b)(b)

    @staticmethod
    def peers(spot):
        x, k, y = spot
        return [at(1 - x, k, y), at(x, k, 1 - y), at(x, 1 - k, y)]


def norm_back_rows(values, mine, theirs, gain):
    mean = jnp.mean(values, axis=1, keepdims=True)
    center = values - mean
    scale = lax.rsqrt(jnp.mean(center * center, axis=1, keepdims=True) + EPS)
    normed = center * scale
    incoming = mine.astype(F32) + theirs.astype(F32)
    e = incoming * gain
    back = scale * (e - jnp.mean(e, axis=1, keepdims=True) - normed * jnp.mean(e * normed, axis=1, keepdims=True))
    return back, normed, incoming


def fold(acc, i, rows):
    acc[i] += sum(rows[8 * j : 8 * j + 8] for j in range(rows.shape[0] // 8))


def middle_phase(
    dd, gd, wd, gu, wu, xb_h, dyb_h, residual_h, f2b_h, hidden_h, slope_h,
    rd, outb, du_h, dbr_h, dbrb_h, rowv_h, dbu_h,
    precv, orecv, theirs, sb, ss, rs, ls, lsem, ps, pr, cs, msem, spot, after,
    xb, dyb, residual, f2b, hidden, slope, du, dbr, dbrb, rowv, dbu,
    acc, psend, gdv, guv, dup, osend, full, st,
):
    x, k, y = spot
    is_a = k == y
    width = wd.shape[0]
    ring = Scatter(dd, rd, None, st, sb, None, ss, rs, ls, spot)
    got_d = load_weight(wd, gd, gdv, lsem.at[0], k, is_a)
    moves = Moves(msem)
    got = [moves.start(a, b) for a, b in ((dyb_h, dyb), (slope_h, slope))]
    got_u = load_weight(wu, gu, guv, lsem.at[1], k, is_a)
    more = [
        moves.start(a, b) for a, b in ((hidden_h, hidden), (f2b_h, f2b), (residual_h, residual), (xb_h, xb))
    ]
    got_d()
    for c in got:
        c.wait()

    def contract(c, n):
        cols = pl.ds(c, n)
        grad = (nn(dyb[...], gdv[:, cols]) * slope[:, cols].astype(F32)).astype(BF)
        dup[:, cols] = grad
        dbu[:, cols] = jnp.sum(grad.astype(F32), axis=0, keepdims=True)

    chunks(slope.shape[1], 256, contract)
    got_u()
    for c in more:
        c.wait()
    tail = [pltpu.make_async_copy(a, b, msem.at[6 + i]) for i, (a, b) in enumerate(
        ((du, du_h), (dbr, dbr_h), (dbrb, dbrb_h), (rowv, rowv_h), (dbu, dbu_h)))]

    def up_grad(j, carry):
        du[j] = tn(f2b[j], dup[...]).astype(BF)
        return carry

    lax.fori_loop(0, 4, up_grad, 0)
    tail[0].start()

    def second_grad(c, n):
        rows = pl.ds(c, n)
        psend[:, rows] = nt(dup[...], guv[rows, :]).astype(BF)

    chunks(psend.shape[1], 384, second_grad)
    exchange = remote(psend, precv, ps.at[0], pr.at[0], at(x, 1 - k, y))
    exchange.start()
    tail[0].wait()
    ring.second()
    after()
    low = k == 0
    bd = xb[SEQ - 1 : PADS, :].astype(F32)[6:7]

    def side(a, i):
        lo = 2 * i * width
        return jnp.where(low, a[:, lo : lo + width], a[:, lo + width : lo + 2 * width])

    def down(c, n):
        rows = pl.ds(c, n)
        full[:, rows] = nt(hidden[...], gdv[rows, :])

    chunks(4 * width, 384, down)

    def far(a, i):
        lo = 2 * i * width
        return jnp.where(low, a[:, lo + width : lo + 2 * width], a[:, lo : lo + width])

    for i in range(2):
        osend[i] = far(full, i).astype(BF)
    outs = remote(osend, orecv, ps.at[1], pr.at[1], at(x, 1 - k, y))
    outs.start()
    outs.wait_recv()
    for i in range(2):
        theirs[i] = (side(full, i) + side(residual, i) + side(bd, i) + orecv[i].astype(F32)).astype(BF)
    mine = pltpu.make_async_copy(theirs.at[0], outb.at[x], cs)
    mine.start()
    away = remote(theirs.at[1], outb.at[x], ps.at[2], pr.at[2], at(1 - x, k, y))
    away.start()

    exchange.wait_recv()
    g2 = xb[SEQ - 1 : PADS, :].astype(F32)[2:3]
    acc[...] = jnp.zeros_like(acc)

    def norm2(r, n):
        rows = pl.ds(r, n)
        back, normed, incoming = norm_back_rows(residual[rows, :], psend[rows, :], precv[rows, :], g2)
        dyr = dyb[rows, :].astype(F32)
        low = (dyr + back).astype(BF)
        dbr[rows, :] = low
        fold(acc, 0, incoming * normed)
        fold(acc, 1, incoming)
        fold(acc, 2, low.astype(F32))
        fold(acc, 3, dyr)

    chunks(PADS, 128, norm2)
    rowv[...] = jnp.concatenate(
        [jnp.sum(acc[i], axis=0, keepdims=True) for i in range(4)] + [jnp.zeros((4, 4 * width), F32)], axis=0
    )
    for j in range(4):
        dbrb[j] = dbr[:, j * width : (j + 1) * width]
    for c in tail[1:]:
        c.start()
    exchange.wait_send()
    outs.wait_send()
    for c in tail[1:]:
        c.wait()


class DpSum:
    def __init__(self, zs, zr, buf, out, ss, rs, ls):
        self.zs, self.zr, self.buf, self.out, self.ls = zs, zr, buf, out, ls
        size = lax.axis_size("dp")
        self.me = lax.axis_index("dp")
        self.copies = []
        for o in range(1, size):
            dest = lax.rem(self.me + o, size)
            self.copies.append(remote(zs.at[dest], zr.at[o - 1], ss.at[o - 1], rs.at[o - 1], {"dp": dest}))

    def start(self):
        for c in self.copies:
            c.start()

    def finish(self):
        for c in self.copies:
            c.wait_recv()
        sources = [self.zs.at[self.me]] + [self.zr.at[i] for i in range(len(self.copies))]
        for i, src in enumerate(sources):
            pltpu.make_async_copy(src, self.buf.at[i], self.ls.at[i]).start()
        for i, src in enumerate(sources):
            pltpu.make_async_copy(src, self.buf.at[i], self.ls.at[i]).wait()
        buf, out = self.buf, self.out

        def add(c, n):
            cols = pl.ds(c, n)
            out[:, cols] = sum(buf[i, :, cols].astype(F32) for i in range(len(sources)))

        chunks(out.shape[1], 128, add)

    def close(self):
        for c in self.copies:
            c.wait_send()


def backward_phase(
    du, dd, rd, go, wo, gq, wq, xb_h, f1b_h, hflat_h, qh_h, oh_h, lse_h, dbr_h, dbrb_h, vec2_h, dbu_h,
    zsd, ru, zsu, ro, zso, ra, zsa, rb, zsb, zrd, zru, zro, zra, zrb, gin,
    td, tu, to, ta, tb, rowt, colt,
    pr, sbd, rowb, colv, rr, cr, rsum, csum, rz, cz,
    ssu, rsu, lsu, sso, rso, lso, ssa, rsa, lsa, ssb, rsb, lsb, ssd, rsd,
    lsem, zss, zrs, zls, es, er, hs, hr, cs, vs, vr, ws, wr, msem, spot, later,
    xb, f1b, hflat, dbr, dbrb, vec2, dbu,
    acc, gov, dqkv, do, dq,
    stu, sbu, cvu, sto, sbo, cvo, sta, sba, cva, sbb, cvb,
):
    x, k, y = spot
    is_a, is_b = k == y, k != y
    width, hw = xb.shape[1] // 4, hflat.shape[1]
    heads = hw // HD
    size, me = lax.axis_size("dp"), lax.axis_index("dp")
    summed = cvu.shape[1] > 1
    plane = [at(1 - x, k, y), at(x, k, 1 - y), at(1 - x, k, 1 - y)]
    side = jnp.where(is_a, 0, 1)
    row_sends = [
        remote(rowb.at[k if i == 1 else 2 + k], rr.at[i], vs.at[i], vr.at[i], plane[i]) for i in range(3)
    ]
    col_sends = [
        remote(colv, cr.at[side], vs.at[3], vr.at[3 + side], at(x, 1 - k, k)),
        remote(colv, cr.at[2 + side], vs.at[4], vr.at[5 + side], at(1 - x, k, k)),
        remote(colv, cr.at[2 + side], vs.at[5], vr.at[5 + side], at(1 - x, 1 - k, k)),
    ]
    col_extra = remote(colv, cr.at[1], vs.at[6], vr.at[4], at(x, k, k))
    dp_sends = []
    for o in range(1, size):
        dest = {"dp": lax.rem(me + o, size)}
        dp_sends.append(remote(rsum, rz.at[o - 1], ws.at[0, o - 1], wr.at[0, o - 1], dest))
        dp_sends.append(remote(csum, cz.at[o - 1], ws.at[1, o - 1], wr.at[1, o - 1], dest))
    ring_u = Scatter(du, ru, zsu, stu, sbu, cvu, ssu, rsu, lsu, spot)
    moves = Moves(msem)
    got = [moves.start(a, b) for a, b in ((dbr_h, dbr), (hflat_h, hflat), (dbrb_h, dbrb))]
    got_o = load_weight(wo, go, gov, lsem.at[0], k, is_a)
    more = [moves.start(a, b) for a, b in ((f1b_h, f1b), (xb_h, xb), (vec2_h, vec2), (dbu_h, dbu))]
    ring_d = Scatter(dd, rd, zsd, stu, sbd, cvu, ssd, rsd, lsu, spot)
    ring_o = Scatter(do, ro, zso, sto, sbo, cvo, sso, rso, lso, spot)
    ring_a = Scatter(dq.at[0], ra, zsa, sta, sba, cva, ssa, rsa, lsa, spot)
    ring_b = Scatter(dq.at[1], rb, zsb, sta, sbb, cvb, ssb, rsb, lsb, spot)
    if summed:
        sums = [
            DpSum(zs, zr, cv.at[0], t, zss.at[i], zrs.at[i], zls.at[i])
            for i, (zs, zr, cv, t) in enumerate(
                ((zsd, zrd, cvu, td), (zsu, zru, cvu, tu), (zso, zro, cvo, to), (zsa, zra, cva, ta), (zsb, zrb, cvb, tb))
            )
        ]
    def attention(qh, oh, lse, dh, dqh):
        inner = [moves.start(a, b) for a, b in ((qh_h, qh), (oh_h, oh), (lse_h, lse))]
        ring_d.third()
        dh[...] = jnp.zeros_like(dh)
        for c in got:
            c.wait()
        got_o()
        dqkv[:, 0:hw] = nn(dbr[...], gov[...]).astype(BF)
        for h in range(heads):
            dh[h, :, 0:HD] = dqkv[:, h * HD : (h + 1) * HD]

        def out_grad(j, carry):
            do[j] = tn(hflat[...], dbrb[j]).astype(BF)
            return carry

        lax.fori_loop(0, 4, out_grad, 0)
        ring_d.fourth()
        if summed:
            sums[0].start()
        for c in more + inner:
            c.wait()
        keymask = jnp.where(lax.broadcasted_iota(jnp.int32, (PADS, 1), 0) < SEQ, 0.0, -1e30)
        ones = jnp.ones((8, 128), F32)

        def attend(h, carry):
            q, kk, v, g = qh[h], qh[heads + h], qh[2 * heads + h], dh[h]
            p = jnp.exp(nt(kk, q) * HD ** (-0.5) + keymask - lse[pl.ds(h, 1), :])
            delta = lax.dot_general(
                ones, g.astype(F32) * oh[h].astype(F32), (((1,), (1,)), ((), ())),
                precision=lax.Precision.HIGHEST, preferred_element_type=F32,
            )[0:1]
            ds = (p * (nt(v, g) - delta)).astype(BF)
            dqh[2 * heads + h] = nn(p.astype(BF), g).astype(BF)
            dqh[heads + h] = (nn(ds, q) * HD ** (-0.5)).astype(BF)
            dqh[h] = (tn(kk, ds) * HD ** (-0.5)).T.astype(BF)
            return carry

        half_cols, group = dq.shape[3], heads // 2

        def one_half(half, carry):
            lax.fori_loop(half * group, (half + 1) * group, attend, 0)
            cols = pl.ds(pl.multiple_of(half * half_cols, 128), half_cols)
            block = dqkv.at[:, cols]
            for p in range(3):
                for i in range(group):
                    lo = (p * group + i) * HD
                    block[:, lo : lo + HD] = dqh[p * heads + half * group + i, :, 0:HD]
            block[:, 3 * group * HD :] = jnp.zeros((PADS, half_cols - 3 * group * HD), BF)

            def qkv_grad(j, c):
                dq[half, j] = tn(f1b[j], block[...]).astype(BF)
                return c

            lax.fori_loop(0, 4, qkv_grad, 0)

            @pl.when(half == 0)
            def _():
                ring_u.second()
                ring_o.first()
                ring_a.first()

            return carry

        lax.fori_loop(0, 2, one_half, 0)

    pl.run_scoped(
        attention,
        pltpu.VMEM(qh_h.shape, BF), pltpu.VMEM(oh_h.shape, BF), pltpu.VMEM(lse_h.shape, F32),
        pltpu.VMEM((heads,) + qh_h.shape[1:], BF), pltpu.VMEM(qh_h.shape, BF),
    )
    ring_b.first()

    def ending(gqv, ps, home):
        got_q = load_weight(wq, gq, gqv, lsem.at[1], k, is_a)
        ring_d.home_sent()
        ring_u.third()
        ring_u.fourth()
        if summed:
            sums[1].start()
        ring_o.second()
        got_q()

        def first_grad(c, n):
            rows = pl.ds(c, n)
            ps[:, rows] = nt(dqkv[...], gqv[rows, :]).astype(BF)

        chunks(ps.shape[1], 384, first_grad)
        exchange = remote(ps, pr, es, er, at(x, 1 - k, y))
        exchange.start()
        ring_a.second()

        def bias_grad(c, n):
            cols = pl.ds(c, n)
            colv[0:1, cols] = jnp.sum(dqkv[:, cols].astype(F32), axis=0, keepdims=True)

        chunks(dqkv.shape[1], 128, bias_grad)
        colv[1:2, :] = dbu[...]
        exchange.wait_recv()
        exchange.wait_send()
        g1 = xb[SEQ - 1 : PADS, :].astype(F32)[1:2]
        acc[...] = jnp.zeros_like(acc)

        def norm1(r, n):
            rows = pl.ds(r, n)
            back, normed, incoming = norm_back_rows(xb[rows, :].astype(F32), ps[rows, :], pr[rows, :], g1)
            ps[rows, :] = (dbr[rows, :].astype(F32) + back).astype(BF)
            fold(acc, 0, incoming * normed)
            fold(acc, 1, incoming)

        chunks(PADS, 128, norm1)
        gain, shift = (jnp.sum(acc[i], axis=0, keepdims=True) for i in range(2))
        rows6 = jnp.concatenate(
            [gain, vec2[0:1], shift, vec2[1:2], vec2[2:3], vec2[3:4], jnp.zeros((2, 4 * width), F32)], axis=0
        )
        for j in range(4):
            rowb[j] = rows6[:, j * width : (j + 1) * width]
        for c in row_sends + col_sends:
            c.start()
        pl.when(is_b)(col_extra.start)
        low = k == 0
        for i in range(2):
            lo = 2 * i * width
            home[i] = jnp.where(low, ps[:, lo : lo + width], ps[:, lo + width : lo + 2 * width])
        mine = pltpu.make_async_copy(home.at[0], gin.at[x], cs)
        mine.start()
        away = remote(home.at[1], gin.at[x], hs, hr, at(1 - x, k, y))
        away.start()
        ring_b.second()
        ring_o.third()
        ring_o.fourth()
        if summed:
            sums[0].finish()
            sums[2].start()
        ring_a.third()
        ring_a.fourth()
        if summed:
            sums[3].start()
        for c in row_sends:
            c.wait_recv()
        for i in range(1, 4):
            remote(colv, cr.at[i], vs.at[3], vr.at[3 + i], at(x, 1 - k, k)).wait_recv()
        pl.when(is_b)(lambda: remote(colv, cr.at[0], vs.at[3], vr.at[3], at(x, 1 - k, k)).wait_recv())
        rsum[...] = rowb[k] + rr[0] + rr[1] + rr[2]

        @pl.when(is_a)
        def _():
            csum[...] = colv[...] + cr[1] + cr[2] + cr[3]

        @pl.when(is_b)
        def _():
            csum[...] = cr[0] + cr[1] + cr[2] + cr[3]

        for c in dp_sends:
            c.start()
        ring_b.third()
        ring_b.fourth()
        if summed:
            sums[4].start()
            sums[1].finish()
        mine.wait()
        remote(home.at[1], gin.at[1 - x], hs, hr, at(1 - x, k, y)).wait_recv()
        away.wait_send()
        for ring in (ring_u, ring_o, ring_a, ring_b):
            ring.close()
        for c in row_sends + col_sends:
            c.wait_send()
        pl.when(is_b)(col_extra.wait_send)
        for c in dp_sends:
            c.wait_recv()
            c.wait_send()
        rowt[...] = rsum[...] + sum(rz[o] for o in range(size - 1))
        colt[...] = csum[...] + sum(cz[o] for o in range(size - 1))
        if summed:
            for total in sums[2:]:
                total.finish()
            for total in sums:
                total.close()

        later()
        ring_d.close(home=False)

    pl.run_scoped(
        ending, pltpu.VMEM((4 * width, wq.shape[1]), BF), pltpu.VMEM(pr.shape, BF), pltpu.VMEM((2, PADS, width), BF)
    )


def layer(parts, tok, cot, bias, wq, wo, wu, wd):
    width, hw, ff, nq = tok.shape[2], wo.shape[1], wu.shape[1], wq.shape[1]
    full, heads, nh = 4 * width, hw // HD, nq // 2
    others = max(parts - 1, 1)
    peers = lax.axis_size("dp") - 1
    piece, slab = width // parts, hw // parts
    low = lambda *d: (d, BF)
    wide = lambda *d: (d, F32)
    tall, rows4 = low(PADS, full), low(4, PADS, width)
    hbm = dict(
        gq=low(4, width, nq), go=low(4, width, hw), gu=low(4, width, ff), gd=low(4, width, ff),
        xb=tall, dyb=tall, f1b=rows4, qh=low(3 * heads, PADS, 128), oh=low(heads, PADS, 128), hflat=low(PADS, hw),
        lse=wide(heads, PADS), residual=wide(PADS, full), f2b=rows4, hidden=low(PADS, ff), slope=low(PADS, ff),
        dd=low(4, width, ff), tbuf=rows4, cbuf=rows4, rd=low(5, width, ff), outb=low(2, PADS, width),
        du=low(4, width, ff), dbr=tall, dbrb=rows4, rowv=wide(8, full), dbu=wide(1, ff),
        zsd=low(parts, piece, ff), ru=low(5, width, ff), zsu=low(parts, piece, ff),
        ro=low(5, hw, width), zso=low(parts, slab, width),
        ra=low(5, width, nh), zsa=low(parts, piece, nh), rb=low(5, width, nh), zsb=low(parts, piece, nh),
        zrd=low(others, piece, ff), zru=low(others, piece, ff), zro=low(others, slab, width),
        zra=low(others, piece, nh), zrb=low(others, piece, nh), gin=low(2, PADS, width),
    )
    small = [(piece, ff), (piece, ff), (slab, width), (piece, nh), (piece, nh)]
    vmem_out = dict(
        zip(("td", "tu", "to", "ta", "tb"), [wide(*d) if parts > 1 else wide(8, 128) for d in small]),
        rowt=wide(8, width), colt=wide(2, ff),
    )
    kept = dict(
        bv=low(*bias.shape), precv_f=tall, precv_m=tall, orecv=low(2, PADS, width), theirs=low(2, PADS, width),
        pr=tall, sbd=low(width, ff), rowb=wide(4, 8, width), colv=wide(2, ff), rr=wide(3, 8, width), cr=wide(4, 2, ff),
        rsum=wide(8, width), csum=wide(2, ff), rz=wide(peers, 8, width), cz=wide(peers, 2, ff),
    )
    sems = dict(
        ssem=(8,), rsem=(8,), csem=(3,), lsem=(4,), wsend=(4, 4), wrecv=(4, 4), msem_f=(12,),
        ssd=(4,), rsd=(6,), lsd=(6,), lsem_m=(2, 4), ps_m=(3,), pr_m=(3,), cs_m=(), msem_m=(11,),
        ssu=(4,), rsu=(6,), lsu=(6,), sso=(4,), rso=(6,), lso=(6,), ssa=(4,), rsa=(6,), lsa=(6,), ssb=(4,), rsb=(6,), lsb=(6,),
        lsem_b=(2, 4), zss=(5, others), zrs=(5, others), zls=(5, others + 1), es=(), er=(), hs=(), hr=(), cs=(),
        vs=(7,), vr=(7,), ws=(2, peers), wr=(2, peers), msem_b=(10,),
    )
    names = ["tok", "cot", "bias", "wq", "wo", "wu", "wd", *hbm, *vmem_out, *kept, *sems]

    def scoped(fn, shapes):
        pl.run_scoped(fn, *[pltpu.VMEM(d, t) for d, t in shapes])

    def kernel(*refs):
        r = types.SimpleNamespace(**dict(zip(names, refs)))
        x, k, y = spot = place()
        size, me = lax.axis_size("dp"), lax.axis_index("dp")
        plane = [at(1 - x, k, y), at(x, k, 1 - y), at(1 - x, k, 1 - y), at(x, 1 - k, y)]
        plane += [at(1 - x, 1 - k, y), at(x, 1 - k, 1 - y), at(1 - x, 1 - k, 1 - y)]
        greet(plane + [{"dp": lax.rem(me + o, size)} for o in range(1, size)])

        def first_ring():
            Scatter(r.dd, r.rd, None, None, r.sbd, None, r.ssd, r.rsd, r.lsd, spot).first()

        def second_ring():
            Scatter(r.du, r.ru, None, None, None, None, r.ssu, r.rsu, r.lsu, spot).first()

        scoped(
            lambda *v: forward_phase(
                r.tok, r.cot, r.bias, r.wq, r.wo, r.wu, r.wd,
                r.gq, r.go, r.gu, r.gd, r.xb, r.dyb, r.f1b, r.qh, r.oh, r.hflat, r.lse, r.residual, r.f2b,
                r.hidden, r.slope, r.dd, r.tbuf, r.cbuf, r.bv, r.precv_f,
                r.ssem, r.rsem, r.csem, r.lsem, r.wsend, r.wrecv, r.msem_f, spot, first_ring, *v,
            ),
            [hbm[n] for n in ("xb", "dyb", "f1b", "qh", "oh", "hflat", "lse", "residual", "f2b", "hidden", "slope", "dd")]
            + [rows4, low(full, nq), low(full, hw), low(full, ff), tall, tall],
        )

        def later():
            far = at(1 - x, k, y)
            pltpu.make_async_copy(r.theirs.at[0], r.outb.at[x], r.cs_m).wait()
            remote(r.theirs.at[1], r.outb.at[1 - x], r.ps_m.at[2], r.pr_m.at[2], far).wait_recv()
            remote(r.theirs.at[1], r.outb.at[x], r.ps_m.at[2], r.pr_m.at[2], far).wait_send()

        scoped(
            lambda *v: middle_phase(
                r.dd, r.gd, r.wd, r.gu, r.wu, r.xb, r.dyb, r.residual, r.f2b, r.hidden, r.slope,
                r.rd, r.outb, r.du, r.dbr, r.dbrb, r.rowv, r.dbu, r.precv_m, r.orecv, r.theirs, r.sbd,
                r.ssd, r.rsd, r.lsd, r.lsem_m, r.ps_m, r.pr_m, r.cs_m, r.msem_m, spot, second_ring, *v,
            ),
            [hbm[n] for n in ("xb", "dyb", "residual", "f2b", "hidden", "slope", "du", "dbr", "dbrb", "rowv", "dbu")]
            + [wide(4, 8, full), tall, low(full, ff), low(full, ff), low(PADS, ff), low(2, PADS, width), wide(PADS, full),
               low(3, width, ff)],
        )
        scoped(
            lambda *v: backward_phase(
                r.du, r.dd, r.rd, r.go, r.wo, r.gq, r.wq, r.xb, r.f1b, r.hflat, r.qh, r.oh, r.lse, r.dbr, r.dbrb, r.rowv, r.dbu,
                r.zsd, r.ru, r.zsu, r.ro, r.zso, r.ra, r.zsa, r.rb, r.zsb, r.zrd, r.zru, r.zro, r.zra, r.zrb, r.gin,
                r.td, r.tu, r.to, r.ta, r.tb, r.rowt, r.colt,
                r.pr, r.sbd, r.rowb, r.colv, r.rr, r.cr, r.rsum, r.csum, r.rz, r.cz,
                r.ssu, r.rsu, r.lsu, r.sso, r.rso, r.lso, r.ssa, r.rsa, r.lsa, r.ssb, r.rsb, r.lsb, r.ssd, r.rsd,
                r.lsem_b, r.zss, r.zrs, r.zls, r.es, r.er, r.hs, r.hr, r.cs, r.vs, r.vr, r.ws, r.wr, r.msem_b,
                spot, later, *v,
            ),
            [hbm[n] for n in ("xb", "f1b", "hflat", "dbr", "dbrb", "rowv", "dbu")]
            + [wide(2, 8, full), low(full, hw), low(PADS, nq), low(4, hw, width), low(2, 4, width, nh)]
            + [low(3, width, ff), low(width, ff), low(2, parts, piece, ff)]
            + [low(3, hw, width), low(hw, width), low(2, parts, slab, width)]
            + [low(3, width, nh), low(width, nh), low(2, parts, piece, nh), low(width, nh), low(2, parts, piece, nh)],
        )

    anyspec = pl.BlockSpec(memory_space=pl.ANY)
    outs = pl.pallas_call(
        kernel,
        out_shape=[jax.ShapeDtypeStruct(*v) for v in (*hbm.values(), *vmem_out.values())],
        in_specs=[anyspec] * 7,
        out_specs=[anyspec] * len(hbm) + [pl.BlockSpec(memory_space=pltpu.VMEM)] * len(vmem_out),
        scratch_shapes=[pltpu.VMEM(*v) for v in kept.values()] + [pltpu.SemaphoreType.DMA(v) for v in sems.values()],
        compiler_params=pltpu.CompilerParams(collective_id=0, has_side_effects=True, vmem_limit_bytes=VMEM_CAP),
        name="layer",
    )(tok, cot, bias, wq, wo, wu, wd)
    return types.SimpleNamespace(**dict(zip((*hbm, *vmem_out), outs)))


def shards(tokens, ln_gain, ln_bias, w_qkv, b_qv, w_out, b_out, w_up, b_up, w_down, b_down, cotangent):
    width = tokens.shape[1]
    hw = b_qv.shape[1]

    extra = jnp.concatenate(
        [ln_gain, ln_bias, b_out[None], b_down[None], jnp.zeros((1, width), BF)], axis=0
    )
    images = tokens.shape[0] // SEQ
    blank = jnp.zeros((PADS - SEQ, width), BF)

    def with_rows(a, tail):
        return jnp.stack([jnp.concatenate([a[i * SEQ : (i + 1) * SEQ], tail]) for i in range(images)])

    tok2, cot2 = with_rows(tokens, extra), with_rows(cotangent, blank)
    ff = b_up.shape[0]
    nq, hh = padded(hw), hw // 2
    gap = jnp.zeros((nq // 2 - 3 * hh,), BF)
    nil = jnp.zeros((hh,), BF)
    bqkv = jnp.concatenate(
        [b_qv[0, :hh], nil, b_qv[1, :hh], gap, b_qv[0, hh:], nil, b_qv[1, hh:], gap, jnp.zeros((ff - nq,), BF)]
    )
    bias = jnp.concatenate([bqkv[None], b_up[None], jnp.zeros((14, ff), BF)])
    side = jnp.zeros((width, gap.shape[0]), BF)
    qblock = jnp.concatenate(
        [w_qkv[:, p, i * hh : (i + 1) * hh] if p < 3 else side for i in range(2) for p in range(4)], axis=1
    )
    wot, wdt = w_out.T, w_down.T
    dp_size = lax.axis_size("dp")
    parts = dp_size if width % dp_size == 0 and (width // dp_size) % 8 == 0 else 1
    r = layer(parts, tok2, cot2, bias, qblock, wot, w_up, wdt)
    output = jnp.concatenate([r.outb[i, :SEQ] for i in range(images)])
    input_grad = jnp.concatenate([r.gin[i, :SEQ] for i in range(images)])
    td, tu, to, ta, tb, rowt, colt = r.td, r.tu, r.to, r.ta, r.tb, r.rowt, r.colt
    if parts == 1:

        def over_dp(a):
            return lax.psum_scatter(a[0], "dp", scatter_dimension=0, tiled=True).astype(F32)

        td, tu, to, ta, tb = (over_dp(a) for a in (r.zsd, r.zsu, r.zso, r.zsa, r.zsb))

    return (
        output,
        input_grad,
        rowt[0:2],
        rowt[2:4],
        jnp.concatenate([a[:, : 3 * hh].reshape(-1, 3, hh) for a in (ta, tb)], axis=2),
        jnp.stack(
            [jnp.concatenate([colt[0, i * nq // 2 + p * hh :][:hh] for i in range(2)]) for p in (0, 2)]
        ),
        to,
        rowt[4],
        tu,
        colt[1],
        td.T,
        rowt[5],
    )


def solution(mesh):
    placed = (
        P(("dp", "col"), "row"),
        P(None, "row"),
        P(None, "row"),
        P("row", None, "col"),
        P(None, "col"),
        P("col", "row"),
        P("row"),
        P("row", "col"),
        P("col"),
        P("col", "row"),
        P("row"),
        P(("dp", "col"), "row"),
    )
    return jax.shard_map(
        shards,
        mesh=mesh,
        in_specs=placed,
        out_specs=(
            P(("dp", "col"), "row"),
            P(("dp", "col"), "row"),
            P(None, "row"),
            P(None, "row"),
            P(("row", "dp"), None, "col"),
            P(None, "col"),
            P(("col", "dp"), "row"),
            P("row"),
            P(("row", "dp"), "col"),
            P("col"),
            P("col", ("row", "dp")),
            P("row"),
        ),
        check_vma=False,
    )
```

```python
import types

import jax
import jax.numpy as jnp
from jax import lax
from jax.experimental import pallas as pl
from jax.experimental.pallas import tpu as pltpu
from jax.sharding import PartitionSpec as P

HD = 72
SEQ = 729
EPS = 1e-06
BF = jnp.bfloat16
F32 = jnp.float32


def nn(a, b):
    return jnp.dot(a, b, preferred_element_type=F32)


def nt(a, b):
    return lax.dot_general(a, b, (((1,), (1,)), ((), ())), preferred_element_type=F32)


def tn(a, b):
    return lax.dot_general(a, b, (((0,), (0,)), ((), ())), preferred_element_type=F32)


def gelu_parts(u):
    t = jnp.tanh(0.7978845608028654 * (u + 0.044715 * u * u * u))
    value = 0.5 * u * (1.0 + t)
    slope = 0.5 * (1.0 + t) + 0.5 * u * (1.0 - t * t) * 0.7978845608028654 * (1.0 + 3 * 0.044715 * u * u)
    return value, slope


MESH = pl.DeviceIdType.MESH
PADS = 736
VMEM_CAP = 66_000_000


def place():
    row, col = lax.axis_index("row"), lax.axis_index("col")
    return row // 2, lax.rem(row, 2), col


def at(x, k, y):
    return {"row": 2 * x + k, "col": y}


def greet(peers):
    barrier = pltpu.get_barrier_semaphore()
    for peer in peers:
        pl.semaphore_signal(barrier, inc=1, device_id=peer, device_id_type=MESH)
    pl.semaphore_wait(barrier, len(peers))


def chunks(total, step, body):
    whole = total // step
    if whole > 0:
        lax.fori_loop(0, whole, lambda i, c: (body(pl.multiple_of(i * step, step), step), c)[1], 0)
    if total % step:
        body(whole * step, total % step)


def column(part, head, hw):
    half, left = divmod(head, hw // HD // 2)
    return half * (padded(hw) // 2) + part * (hw // 2) + left * HD


def padded(hw):
    return 2 * (-(-3 * hw // 2 // 128) * 128)


class Moves:
    def __init__(self, sems):
        self.sems, self.open = sems, {}

    def start(self, src, dst):
        c = pltpu.make_async_copy(src, dst, self.sems.at[len(self.open)])
        c.start()
        self.open[len(self.open)] = c
        return c

    def finish(self):
        for c in self.open.values():
            c.wait()


def forward_phase(
    tok, cot, bias, wq, wo, wu, wd,
    gq, go, gu, gd, xb_h, dyb_h, f1b_h, qh_h, oh_h, hflat_h, lse_h, residual_h, f2b_h, hidden_h, slope_h, dd_h,
    tbuf, cbuf, bv, precv, ssem, rsem, csem, lsem, wsend, wrecv, msem, spot, after,
    xb, dyb, f1b, qh, oh, hflat, lse, residual, f2b, hidden, slope, dd, tb, gqv, gov, guv, f1, psend,
):
    x, k, y = spot
    is_a, is_b = k == y, k != y
    hw = hflat.shape[1]
    heads = hw // HD
    width = tok.shape[2]
    blocks, wholes = (wq, wo, wu, wd), (gq, go, gu, gd)
    out = Moves(msem)
    over_y = (1,)

    def own_sends(w):
        b, g = blocks[w], wholes[w]
        a = [
            remote(b, g.at[2 + k], wsend.at[w, 0], wrecv.at[w, 2 + k], at(1 - x, k, y)),
            remote(b, g.at[k], wsend.at[w, 1], wrecv.at[w, k], at(x, k, 1 - y)),
        ]
        bb = [
            remote(b, g.at[2 + k], wsend.at[w, 0], wrecv.at[w, 2 + k], at(1 - x, 1 - k, y)),
            remote(b, g.at[k], wsend.at[w, 1], wrecv.at[w, k], at(x, 1 - k, 1 - y)),
            remote(b, g.at[k], wsend.at[w, 2], wrecv.at[w, k], at(x, 1 - k, y)),
        ]
        return a, bb

    def relays(w):
        g = wholes[w]
        return (
            remote(g.at[2], g.at[2], wsend.at[w, 3], wrecv.at[w, 2], at(x, k, 1 - y)),
            remote(g.at[1], g.at[3], wsend.at[w, 3], wrecv.at[w, 3], at(1 - x, k, y)),
            remote(g.at[3], g.at[3], wsend.at[w, 2], wrecv.at[w, 3], at(x, k, 1 - y)),
        )

    def both(fa, fb):
        pl.when(is_a)(fa)
        pl.when(is_b)(fb)

    def start_own(w):
        a, b = own_sends(w)
        both(lambda: [c.start() for c in a] and None, lambda: [c.start() for c in b] and None)

    def arrived(w, j):
        remote(blocks[w], wholes[w].at[j], wsend.at[w, 0], wrecv.at[w, j], at(x, 1 - k, y)).wait_recv()

    def start_relay(w):
        ra, rb, rc = relays(w)

        def fa():
            arrived(w, 2)
            ra.start()
            if w in over_y:
                arrived(w, 3)
                rc.start()

        def fb():
            arrived(w, 1)
            rb.start()

        pl.when(is_a)(fa)
        if w not in over_y:
            pl.when(is_b)(fb)

    def wait_rest(w):
        pl.when(is_b | (k == 1))(lambda: arrived(w, 0))
        pl.when(is_a & (k == 0))(lambda: arrived(w, 1))
        pl.when(is_b)(lambda: arrived(w, 2))
        if w in over_y:
            pl.when(is_b)(lambda: (arrived(w, 1), arrived(w, 3)) and None)
        else:
            arrived(w, 3)

    def finish_sends(w):
        a, b = own_sends(w)
        ra, rb, rc = relays(w)
        a, b = (a + [ra, rc], b) if w in over_y else (a + [ra], b + [rb])
        both(
            lambda: [c.wait_send() for c in a] and None,
            lambda: [c.wait_send() for c in b] and None,
        )

    def load(w, dst):
        b, g = blocks[w], wholes[w]
        for j in range(4):
            rows = pl.ds(j * width, width)
            local = is_a & (k == j) if j < 2 else None
            if local is None:
                pltpu.make_async_copy(g.at[j], dst.at[rows], lsem.at[j]).start()
            else:
                pl.when(local)(lambda: pltpu.make_async_copy(b, dst.at[rows], lsem.at[j]).start())
                pl.when(jnp.logical_not(local))(
                    lambda: pltpu.make_async_copy(g.at[j], dst.at[rows], lsem.at[j]).start()
                )
        for j in range(4):
            pltpu.make_async_copy(g.at[j], dst.at[pl.ds(j * width, width)], lsem.at[j]).wait()

    tx = remote(tok.at[1 - x], tbuf.at[2 + k], ssem.at[0], rsem.at[0], at(1 - x, k, y))
    cx = remote(cot.at[1 - x], cbuf.at[2 + k], ssem.at[1], rsem.at[1], at(1 - x, k, y))
    t1 = remote(tok.at[x], tbuf.at[k], ssem.at[2], rsem.at[2], at(x, 1 - k, y))
    c1 = remote(cot.at[x], cbuf.at[k], ssem.at[3], rsem.at[3], at(x, 1 - k, y))
    t2 = remote(tbuf.at[2 + k], tbuf.at[2 + k], ssem.at[4], rsem.at[4], at(x, 1 - k, y))
    c2 = remote(cbuf.at[2 + k], cbuf.at[2 + k], ssem.at[5], rsem.at[5], at(x, 1 - k, y))
    bs = remote(bias, bv, ssem.at[6], rsem.at[6], at(x, k, 1 - y))
    pe = remote(psend, precv, ssem.at[7], rsem.at[7], at(x, 1 - k, y))

    def collect(src, buf, wide):
        parts = [(src.at[x], k), (buf.at[1 - k], 1 - k), (buf.at[2], 2), (buf.at[3], 3)]
        copies = [pltpu.make_async_copy(a, tb.at[j], lsem.at[i]) for i, (a, j) in enumerate(parts)]
        for c in copies:
            c.start()
        for c in copies:
            c.wait()
        for j in range(4):
            wide[:, j * width : (j + 1) * width] = tb[j]

    bl = pltpu.make_async_copy(bias, bv, csem.at[2])

    tx.start()
    t1.start()
    start_own(0)
    both(lambda: (bl.start(), bs.start()) and None, lambda: None)
    c1.start()

    tx.wait_recv()
    t2.start()
    t1.wait_recv()
    t2.wait_recv()
    collect(tok, tbuf, xb)
    vecs = xb[SEQ - 1 : PADS, :].astype(F32)
    g1, g2, s1, s2, bo = (vecs[j : j + 1] for j in range(1, 6))

    def stats(v):
        mean = jnp.mean(v, axis=1, keepdims=True)
        c = v - mean
        return c * lax.rsqrt(jnp.mean(c * c, axis=1, keepdims=True) + EPS)

    def norm1(r, n):
        f1[pl.ds(r, n), :] = (stats(xb[pl.ds(r, n), :].astype(F32)) * g1 + s1).astype(BF)

    chunks(PADS, 128, norm1)
    f2 = f1
    start_relay(0)
    start_own(1)
    both(bl.wait, bs.wait_recv)
    wait_rest(0)
    load(0, gqv)

    def project(c, n):
        cols = pl.ds(c, n)
        hidden[:, cols] = (nn(f1[...], gqv[:, cols]) + bv[0:1, cols].astype(F32)).astype(BF)

    chunks(gqv.shape[1], 256, project)
    start_relay(1)
    start_own(2)
    for j in range(4):
        f1b[j] = f1[:, j * width : (j + 1) * width]
    qh[...] = jnp.zeros_like(qh)
    for p in range(3):
        for h in range(heads):
            lo = column(p, h, hw)
            qh[p * heads + h, :, 0:HD] = hidden[:, lo : lo + HD]
    out.start(xb, xb_h)
    out.start(f1b, f1b_h)
    out.start(qh, qh_h)
    keymask = jnp.where(lax.broadcasted_iota(jnp.int32, (PADS, 1), 0) < SEQ, 0.0, -1e30)

    def attend(h, carry):
        st = nt(qh[heads + h], qh[h]) + keymask
        top = jnp.max(st, axis=0, keepdims=True)
        e = jnp.exp((st - top) * HD ** (-0.5))
        tot = jnp.sum(e, axis=0, keepdims=True)
        lse[pl.ds(h, 1), :] = top * HD ** (-0.5) + jnp.log(tot)
        out = tn(qh[2 * heads + h], e.astype(BF)) / tot
        oh[h] = out.T.astype(BF)
        return carry

    lax.fori_loop(0, heads, attend, 0)
    for h in range(heads):
        hflat[:, h * HD : (h + 1) * HD] = oh[h, :, 0:HD]
    out.start(oh, oh_h)
    out.start(hflat, hflat_h)
    out.start(lse, lse_h)
    wait_rest(1)
    load(1, gov)

    def out_project(c, n):
        cols = pl.ds(c, n)
        part = nt(hflat[...], gov[cols, :])
        psend[:, cols] = part.astype(BF)
        residual[:, cols] = part

    chunks(4 * width, 384, out_project)
    pe.start()
    pe.wait_recv()

    def norm2(r, n):
        rows = pl.ds(r, n)
        v = xb[rows, :].astype(F32) + bo + residual[rows, :] + precv[rows, :].astype(F32)
        residual[rows, :] = v
        f2[rows, :] = (stats(v) * g2 + s2).astype(BF)

    chunks(PADS, 128, norm2)
    start_relay(2)
    cx.start()
    start_own(3)
    wait_rest(2)
    load(2, guv)
    for j in range(4):
        f2b[j] = f2[:, j * width : (j + 1) * width]
    out.start(residual, residual_h)
    out.start(f2b, f2b_h)

    def expand(c, n):
        cols = pl.ds(c, n)
        u = nn(f2[...], guv[:, cols]) + bv[1:2, cols].astype(F32)
        value, grad = gelu_parts(u)
        hidden[:, cols] = value.astype(BF)
        slope[:, cols] = grad.astype(BF)

    chunks(hidden.shape[1], 256, expand)
    out.start(hidden, hidden_h)
    out.start(slope, slope_h)
    cx.wait_recv()
    c2.start()
    c1.wait_recv()
    c2.wait_recv()
    collect(cot, cbuf, dyb)

    def down_grad(j, carry):
        dd[j] = tn(tb[j], hidden[...]).astype(BF)
        return carry

    out.start(dyb, dyb_h)
    start_relay(3)
    lax.fori_loop(0, 4, down_grad, 0)
    out.start(dd, dd_h)
    out.finish()
    wait_rest(3)
    after()
    for c in (tx, cx, t1, c1, t2, c2, pe):
        c.wait_send()
    both(bs.wait_send, lambda: None)
    for w in range(4):
        finish_sends(w)


def load_weight(b, g, dst, sem, k, is_a):
    width = b.shape[0]
    for j in range(4):
        rows = pl.ds(j * width, width)
        if j < 2:
            local = is_a & (k == j)
            pl.when(local)(lambda: pltpu.make_async_copy(b, dst.at[rows], sem.at[j]).start())
            pl.when(jnp.logical_not(local))(lambda: pltpu.make_async_copy(g.at[j], dst.at[rows], sem.at[j]).start())
        else:
            pltpu.make_async_copy(g.at[j], dst.at[rows], sem.at[j]).start()

    def wait():
        for j in range(4):
            pltpu.make_async_copy(g.at[j], dst.at[pl.ds(j * width, width)], sem.at[j]).wait()

    return wait


def remote(src, dst, s, r, dest):
    return pltpu.make_async_remote_copy(
        src_ref=src, dst_ref=dst, send_sem=s, recv_sem=r, device_id=dest, device_id_type=MESH
    )


class Scatter:
    def __init__(self, d, r, zs, st, sb, cv, ss, rs, ls, spot):
        self.d, self.r, self.zs, self.st, self.sb, self.cv, self.ls, self.spot = d, r, zs, st, sb, cv, ls, spot
        x, k, y = spot
        self.is_a, self.is_b, self.k = k == y, k != y, k
        across, over, mate = at(1 - x, k, y), at(x, k, 1 - y), at(x, 1 - k, y)
        self.x1 = remote(d.at[2], r.at[0], ss.at[0], rs.at[0], across)
        self.y1 = remote(d.at[3], r.at[1], ss.at[1], rs.at[1], over)
        self.y1b = remote(d.at[1], r.at[2], ss.at[2], rs.at[2], over)
        if sb is not None:
            self.x2 = remote(sb, r.at[3], ss.at[1], rs.at[3], across)
            self.y2 = remote(sb, r.at[4], ss.at[3], rs.at[4], over)
        if zs is not None:
            self.home = remote(cv.at[1], zs, ss.at[2], rs.at[5], mate)

    def first(self):
        self.x1.start()

        def b():
            self.y1.start()
            self.y1b.start()

        pl.when(self.is_b)(b)

    def copy_in(self, pairs):
        for i, src in pairs:
            pltpu.make_async_copy(src, self.st.at[i], self.ls.at[i]).start()
        for i, src in pairs:
            pltpu.make_async_copy(src, self.st.at[i], self.ls.at[i]).wait()

    def second(self):
        st, sb = self.st, self.sb

        def fetch_a():
            self.y1.wait_recv()
            self.copy_in([(0, self.d.at[3]), (1, self.r.at[1])])

        def fetch_b():
            self.x1.wait_recv()
            self.copy_in([(0, self.d.at[0]), (1, self.r.at[0])])

        pl.when(self.is_a)(fetch_a)
        pl.when(self.is_b)(fetch_b)

        def add(c, n):
            cols = pl.ds(c, n)
            sb[:, cols] = (st[0, :, cols].astype(F32) + st[1, :, cols].astype(F32)).astype(BF)

        chunks(sb.shape[1], 128, add)
        pl.when(self.is_a)(self.x2.start)
        pl.when(self.is_b)(self.y2.start)

    def settle(self):
        def a():
            self.x1.wait_recv()
            self.y1b.wait_recv()
            self.x2.wait_recv()
            self.y2.wait_recv()

        pl.when(self.is_a)(a)

    def third(self):
        self.settle()
        st, cv = self.st, self.cv
        parts, piece = cv.shape[1], cv.shape[2]

        def a():
            d, r = self.d, self.r
            for which, trio in ((self.k, (d.at[0], r.at[0], r.at[4])), (1 - self.k, (d.at[1], r.at[2], r.at[3]))):
                self.copy_in(list(enumerate(trio)))

                def add(c, n):
                    cols = pl.ds(c, n)
                    total = sum(st[i, :, cols].astype(F32) for i in range(3))
                    for q in range(parts):
                        cv[which, q, :, cols] = total[q * piece : (q + 1) * piece].astype(BF)

                chunks(cv.shape[3], 128, add)
            self.home.start()
            keep = pltpu.make_async_copy(cv.at[0], self.zs, self.ls.at[0])
            keep.start()
            keep.wait()

        pl.when(self.is_a)(a)

    def fourth(self):
        pl.when(self.is_b)(self.home.wait_recv)

    def home_sent(self):
        pl.when(self.is_a)(self.home.wait_send)

    def close(self, home=True):
        self.x1.wait_send()
        pl.when(self.is_a)(self.x2.wait_send)
        if home:
            self.home_sent()

        def b():
            self.y1.wait_send()
            self.y1b.wait_send()
            self.y2.wait_send()

        pl.when(self.is_b)(b)

    @staticmethod
    def peers(spot):
        x, k, y = spot
        return [at(1 - x, k, y), at(x, k, 1 - y), at(x, 1 - k, y)]


def norm_back_rows(values, mine, theirs, gain):
    mean = jnp.mean(values, axis=1, keepdims=True)
    center = values - mean
    scale = lax.rsqrt(jnp.mean(center * center, axis=1, keepdims=True) + EPS)
    normed = center * scale
    incoming = mine.astype(F32) + theirs.astype(F32)
    e = incoming * gain
    back = scale * (e - jnp.mean(e, axis=1, keepdims=True) - normed * jnp.mean(e * normed, axis=1, keepdims=True))
    return back, normed, incoming


def fold(acc, i, rows):
    acc[i] += sum(rows[8 * j : 8 * j + 8] for j in range(rows.shape[0] // 8))


def middle_phase(
    dd, gd, wd, gu, wu, xb_h, dyb_h, residual_h, f2b_h, hidden_h, slope_h,
    rd, outb, du_h, dbr_h, dbrb_h, rowv_h, dbu_h,
    precv, orecv, theirs, sb, ss, rs, ls, lsem, ps, pr, cs, msem, spot, after,
    xb, dyb, residual, f2b, hidden, slope, du, dbr, dbrb, rowv, dbu,
    acc, psend, gdv, guv, dup, osend, full, st,
):
    x, k, y = spot
    is_a = k == y
    width = wd.shape[0]
    ring = Scatter(dd, rd, None, st, sb, None, ss, rs, ls, spot)
    got_d = load_weight(wd, gd, gdv, lsem.at[0], k, is_a)
    moves = Moves(msem)
    got = [moves.start(a, b) for a, b in ((dyb_h, dyb), (slope_h, slope))]
    got_u = load_weight(wu, gu, guv, lsem.at[1], k, is_a)
    more = [
        moves.start(a, b) for a, b in ((hidden_h, hidden), (f2b_h, f2b), (residual_h, residual), (xb_h, xb))
    ]
    got_d()
    for c in got:
        c.wait()

    def contract(c, n):
        cols = pl.ds(c, n)
        grad = (nn(dyb[...], gdv[:, cols]) * slope[:, cols].astype(F32)).astype(BF)
        dup[:, cols] = grad
        dbu[:, cols] = jnp.sum(grad.astype(F32), axis=0, keepdims=True)

    chunks(slope.shape[1], 256, contract)
    got_u()
    for c in more:
        c.wait()
    tail = [pltpu.make_async_copy(a, b, msem.at[6 + i]) for i, (a, b) in enumerate(
        ((du, du_h), (dbr, dbr_h), (dbrb, dbrb_h), (rowv, rowv_h), (dbu, dbu_h)))]

    def up_grad(j, carry):
        du[j] = tn(f2b[j], dup[...]).astype(BF)
        return carry

    lax.fori_loop(0, 4, up_grad, 0)
    tail[0].start()

    def second_grad(c, n):
        rows = pl.ds(c, n)
        psend[:, rows] = nt(dup[...], guv[rows, :]).astype(BF)

    chunks(psend.shape[1], 384, second_grad)
    exchange = remote(psend, precv, ps.at[0], pr.at[0], at(x, 1 - k, y))
    exchange.start()
    tail[0].wait()
    ring.second()
    after()
    low = k == 0
    bd = xb[SEQ - 1 : PADS, :].astype(F32)[6:7]

    def side(a, i):
        lo = 2 * i * width
        return jnp.where(low, a[:, lo : lo + width], a[:, lo + width : lo + 2 * width])

    def down(c, n):
        rows = pl.ds(c, n)
        full[:, rows] = nt(hidden[...], gdv[rows, :])

    chunks(4 * width, 384, down)

    def far(a, i):
        lo = 2 * i * width
        return jnp.where(low, a[:, lo + width : lo + 2 * width], a[:, lo : lo + width])

    for i in range(2):
        osend[i] = far(full, i).astype(BF)
    outs = remote(osend, orecv, ps.at[1], pr.at[1], at(x, 1 - k, y))
    outs.start()
    outs.wait_recv()
    for i in range(2):
        theirs[i] = (side(full, i) + side(residual, i) + side(bd, i) + orecv[i].astype(F32)).astype(BF)
    mine = pltpu.make_async_copy(theirs.at[0], outb.at[x], cs)
    mine.start()
    away = remote(theirs.at[1], outb.at[x], ps.at[2], pr.at[2], at(1 - x, k, y))
    away.start()

    exchange.wait_recv()
    g2 = xb[SEQ - 1 : PADS, :].astype(F32)[2:3]
    acc[...] = jnp.zeros_like(acc)

    def norm2(r, n):
        rows = pl.ds(r, n)
        back, normed, incoming = norm_back_rows(residual[rows, :], psend[rows, :], precv[rows, :], g2)
        dyr = dyb[rows, :].astype(F32)
        low = (dyr + back).astype(BF)
        dbr[rows, :] = low
        fold(acc, 0, incoming * normed)
        fold(acc, 1, incoming)
        fold(acc, 2, low.astype(F32))
        fold(acc, 3, dyr)

    chunks(PADS, 128, norm2)
    rowv[...] = jnp.concatenate(
        [jnp.sum(acc[i], axis=0, keepdims=True) for i in range(4)] + [jnp.zeros((4, 4 * width), F32)], axis=0
    )
    for j in range(4):
        dbrb[j] = dbr[:, j * width : (j + 1) * width]
    for c in tail[1:]:
        c.start()
    exchange.wait_send()
    outs.wait_send()
    for c in tail[1:]:
        c.wait()


class DpSum:
    def __init__(self, zs, zr, buf, out, ss, rs, ls):
        self.zs, self.zr, self.buf, self.out, self.ls = zs, zr, buf, out, ls
        size = lax.axis_size("dp")
        self.me = lax.axis_index("dp")
        self.copies = []
        for o in range(1, size):
            dest = lax.rem(self.me + o, size)
            self.copies.append(remote(zs.at[dest], zr.at[o - 1], ss.at[o - 1], rs.at[o - 1], {"dp": dest}))

    def start(self):
        for c in self.copies:
            c.start()

    def finish(self):
        for c in self.copies:
            c.wait_recv()
        sources = [self.zs.at[self.me]] + [self.zr.at[i] for i in range(len(self.copies))]
        for i, src in enumerate(sources):
            pltpu.make_async_copy(src, self.buf.at[i], self.ls.at[i]).start()
        for i, src in enumerate(sources):
            pltpu.make_async_copy(src, self.buf.at[i], self.ls.at[i]).wait()
        buf, out = self.buf, self.out

        def add(c, n):
            cols = pl.ds(c, n)
            out[:, cols] = sum(buf[i, :, cols].astype(F32) for i in range(len(sources)))

        chunks(out.shape[1], 128, add)

    def close(self):
        for c in self.copies:
            c.wait_send()


def backward_phase(
    du, dd, rd, go, wo, gq, wq, xb_h, f1b_h, hflat_h, qh_h, oh_h, lse_h, dbr_h, dbrb_h, vec2_h, dbu_h,
    zsd, ru, zsu, ro, zso, ra, zsa, rb, zsb, zrd, zru, zro, zra, zrb, gin,
    td, tu, to, ta, tb, rowt, colt,
    pr, sbd, rowb, colv, rr, cr, rsum, csum, rz, cz,
    ssu, rsu, lsu, sso, rso, lso, ssa, rsa, lsa, ssb, rsb, lsb, ssd, rsd,
    lsem, zss, zrs, zls, es, er, hs, hr, cs, vs, vr, ws, wr, msem, spot, later,
    xb, f1b, hflat, dbr, dbrb, vec2, dbu,
    acc, gov, dqkv, do, dq,
    stu, sbu, cvu, sto, sbo, cvo, sta, sba, cva, sbb, cvb,
):
    x, k, y = spot
    is_a, is_b = k == y, k != y
    width, hw = xb.shape[1] // 4, hflat.shape[1]
    heads = hw // HD
    size, me = lax.axis_size("dp"), lax.axis_index("dp")
    summed = cvu.shape[1] > 1
    plane = [at(1 - x, k, y), at(x, k, 1 - y), at(1 - x, k, 1 - y)]
    side = jnp.where(is_a, 0, 1)
    row_sends = [
        remote(rowb.at[k if i == 1 else 2 + k], rr.at[i], vs.at[i], vr.at[i], plane[i]) for i in range(3)
    ]
    col_sends = [
        remote(colv, cr.at[side], vs.at[3], vr.at[3 + side], at(x, 1 - k, k)),
        remote(colv, cr.at[2 + side], vs.at[4], vr.at[5 + side], at(1 - x, k, k)),
        remote(colv, cr.at[2 + side], vs.at[5], vr.at[5 + side], at(1 - x, 1 - k, k)),
    ]
    col_extra = remote(colv, cr.at[1], vs.at[6], vr.at[4], at(x, k, k))
    dp_sends = []
    for o in range(1, size):
        dest = {"dp": lax.rem(me + o, size)}
        dp_sends.append(remote(rsum, rz.at[o - 1], ws.at[0, o - 1], wr.at[0, o - 1], dest))
        dp_sends.append(remote(csum, cz.at[o - 1], ws.at[1, o - 1], wr.at[1, o - 1], dest))
    ring_u = Scatter(du, ru, zsu, stu, sbu, cvu, ssu, rsu, lsu, spot)
    moves = Moves(msem)
    got = [moves.start(a, b) for a, b in ((dbr_h, dbr), (hflat_h, hflat), (dbrb_h, dbrb))]
    got_o = load_weight(wo, go, gov, lsem.at[0], k, is_a)
    more = [moves.start(a, b) for a, b in ((f1b_h, f1b), (xb_h, xb), (vec2_h, vec2), (dbu_h, dbu))]
    ring_d = Scatter(dd, rd, zsd, stu, sbd, cvu, ssd, rsd, lsu, spot)
    ring_o = Scatter(do, ro, zso, sto, sbo, cvo, sso, rso, lso, spot)
    ring_a = Scatter(dq.at[0], ra, zsa, sta, sba, cva, ssa, rsa, lsa, spot)
    ring_b = Scatter(dq.at[1], rb, zsb, sta, sbb, cvb, ssb, rsb, lsb, spot)
    if summed:
        sums = [
            DpSum(zs, zr, cv.at[0], t, zss.at[i], zrs.at[i], zls.at[i])
            for i, (zs, zr, cv, t) in enumerate(
                ((zsd, zrd, cvu, td), (zsu, zru, cvu, tu), (zso, zro, cvo, to), (zsa, zra, cva, ta), (zsb, zrb, cvb, tb))
            )
        ]
    def attention(qh, oh, lse, dh, dqh):
        inner = [moves.start(a, b) for a, b in ((qh_h, qh), (oh_h, oh), (lse_h, lse))]
        ring_d.third()
        dh[...] = jnp.zeros_like(dh)
        for c in got:
            c.wait()
        got_o()
        dqkv[:, 0:hw] = nn(dbr[...], gov[...]).astype(BF)
        for h in range(heads):
            dh[h, :, 0:HD] = dqkv[:, h * HD : (h + 1) * HD]

        def out_grad(j, carry):
            do[j] = tn(hflat[...], dbrb[j]).astype(BF)
            return carry

        lax.fori_loop(0, 4, out_grad, 0)
        ring_d.fourth()
        if summed:
            sums[0].start()
        for c in more + inner:
            c.wait()
        keymask = jnp.where(lax.broadcasted_iota(jnp.int32, (PADS, 1), 0) < SEQ, 0.0, -1e30)
        ones = jnp.ones((8, 128), F32)

        def attend(h, carry):
            q, kk, v, g = qh[h], qh[heads + h], qh[2 * heads + h], dh[h]
            p = jnp.exp(nt(kk, q) * HD ** (-0.5) + keymask - lse[pl.ds(h, 1), :])
            delta = lax.dot_general(
                ones, g.astype(F32) * oh[h].astype(F32), (((1,), (1,)), ((), ())),
                precision=lax.Precision.HIGHEST, preferred_element_type=F32,
            )[0:1]
            ds = (p * (nt(v, g) - delta)).astype(BF)
            dqh[2 * heads + h] = nn(p.astype(BF), g).astype(BF)
            dqh[heads + h] = (nn(ds, q) * HD ** (-0.5)).astype(BF)
            dqh[h] = (tn(kk, ds) * HD ** (-0.5)).T.astype(BF)
            return carry

        half_cols, group = dq.shape[3], heads // 2

        def one_half(half, carry):
            lax.fori_loop(half * group, (half + 1) * group, attend, 0)
            cols = pl.ds(pl.multiple_of(half * half_cols, 128), half_cols)
            block = dqkv.at[:, cols]
            for p in range(3):
                for i in range(group):
                    lo = (p * group + i) * HD
                    block[:, lo : lo + HD] = dqh[p * heads + half * group + i, :, 0:HD]
            block[:, 3 * group * HD :] = jnp.zeros((PADS, half_cols - 3 * group * HD), BF)

            def qkv_grad(j, c):
                dq[half, j] = tn(f1b[j], block[...]).astype(BF)
                return c

            lax.fori_loop(0, 4, qkv_grad, 0)

            @pl.when(half == 0)
            def _():
                ring_u.second()
                ring_o.first()
                ring_a.first()

            return carry

        lax.fori_loop(0, 2, one_half, 0)

    pl.run_scoped(
        attention,
        pltpu.VMEM(qh_h.shape, BF), pltpu.VMEM(oh_h.shape, BF), pltpu.VMEM(lse_h.shape, F32),
        pltpu.VMEM((heads,) + qh_h.shape[1:], BF), pltpu.VMEM(qh_h.shape, BF),
    )
    ring_b.first()

    def ending(gqv, ps, home):
        got_q = load_weight(wq, gq, gqv, lsem.at[1], k, is_a)
        ring_d.home_sent()
        ring_u.third()
        ring_u.fourth()
        if summed:
            sums[1].start()
        ring_o.second()
        got_q()

        def first_grad(c, n):
            rows = pl.ds(c, n)
            ps[:, rows] = nt(dqkv[...], gqv[rows, :]).astype(BF)

        chunks(ps.shape[1], 384, first_grad)
        exchange = remote(ps, pr, es, er, at(x, 1 - k, y))
        exchange.start()
        ring_a.second()

        def bias_grad(c, n):
            cols = pl.ds(c, n)
            colv[0:1, cols] = jnp.sum(dqkv[:, cols].astype(F32), axis=0, keepdims=True)

        chunks(dqkv.shape[1], 128, bias_grad)
        colv[1:2, :] = dbu[...]
        exchange.wait_recv()
        exchange.wait_send()
        g1 = xb[SEQ - 1 : PADS, :].astype(F32)[1:2]
        acc[...] = jnp.zeros_like(acc)

        def norm1(r, n):
            rows = pl.ds(r, n)
            back, normed, incoming = norm_back_rows(xb[rows, :].astype(F32), ps[rows, :], pr[rows, :], g1)
            ps[rows, :] = (dbr[rows, :].astype(F32) + back).astype(BF)
            fold(acc, 0, incoming * normed)
            fold(acc, 1, incoming)

        chunks(PADS, 128, norm1)
        gain, shift = (jnp.sum(acc[i], axis=0, keepdims=True) for i in range(2))
        rows6 = jnp.concatenate(
            [gain, vec2[0:1], shift, vec2[1:2], vec2[2:3], vec2[3:4], jnp.zeros((2, 4 * width), F32)], axis=0
        )
        for j in range(4):
            rowb[j] = rows6[:, j * width : (j + 1) * width]
        for c in row_sends + col_sends:
            c.start()
        pl.when(is_b)(col_extra.start)
        low = k == 0
        for i in range(2):
            lo = 2 * i * width
            home[i] = jnp.where(low, ps[:, lo : lo + width], ps[:, lo + width : lo + 2 * width])
        mine = pltpu.make_async_copy(home.at[0], gin.at[x], cs)
        mine.start()
        away = remote(home.at[1], gin.at[x], hs, hr, at(1 - x, k, y))
        away.start()
        ring_b.second()
        ring_o.third()
        ring_o.fourth()
        if summed:
            sums[0].finish()
            sums[2].start()
        ring_a.third()
        ring_a.fourth()
        if summed:
            sums[3].start()
        for c in row_sends:
            c.wait_recv()
        for i in range(1, 4):
            remote(colv, cr.at[i], vs.at[3], vr.at[3 + i], at(x, 1 - k, k)).wait_recv()
        pl.when(is_b)(lambda: remote(colv, cr.at[0], vs.at[3], vr.at[3], at(x, 1 - k, k)).wait_recv())
        rsum[...] = rowb[k] + rr[0] + rr[1] + rr[2]

        @pl.when(is_a)
        def _():
            csum[...] = colv[...] + cr[1] + cr[2] + cr[3]

        @pl.when(is_b)
        def _():
            csum[...] = cr[0] + cr[1] + cr[2] + cr[3]

        for c in dp_sends:
            c.start()
        ring_b.third()
        ring_b.fourth()
        if summed:
            sums[4].start()
            sums[1].finish()
        mine.wait()
        remote(home.at[1], gin.at[1 - x], hs, hr, at(1 - x, k, y)).wait_recv()
        away.wait_send()
        for ring in (ring_u, ring_o, ring_a, ring_b):
            ring.close()
        for c in row_sends + col_sends:
            c.wait_send()
        pl.when(is_b)(col_extra.wait_send)
        for c in dp_sends:
            c.wait_recv()
            c.wait_send()
        rowt[...] = rsum[...] + sum(rz[o] for o in range(size - 1))
        colt[...] = csum[...] + sum(cz[o] for o in range(size - 1))
        if summed:
            for total in sums[2:]:
                total.finish()
            for total in sums:
                total.close()

        later()
        ring_d.close(home=False)

    pl.run_scoped(
        ending, pltpu.VMEM((4 * width, wq.shape[1]), BF), pltpu.VMEM(pr.shape, BF), pltpu.VMEM((2, PADS, width), BF)
    )


def layer(parts, tok, cot, bias, wq, wo, wu, wd):
    width, hw, ff, nq = tok.shape[2], wo.shape[1], wu.shape[1], wq.shape[1]
    full, heads, nh = 4 * width, hw // HD, nq // 2
    others = max(parts - 1, 1)
    peers = lax.axis_size("dp") - 1
    piece, slab = width // parts, hw // parts
    low = lambda *d: (d, BF)
    wide = lambda *d: (d, F32)
    tall, rows4 = low(PADS, full), low(4, PADS, width)
    hbm = dict(
        gq=low(4, width, nq), go=low(4, width, hw), gu=low(4, width, ff), gd=low(4, width, ff),
        xb=tall, dyb=tall, f1b=rows4, qh=low(3 * heads, PADS, 128), oh=low(heads, PADS, 128), hflat=low(PADS, hw),
        lse=wide(heads, PADS), residual=wide(PADS, full), f2b=rows4, hidden=low(PADS, ff), slope=low(PADS, ff),
        dd=low(4, width, ff), tbuf=rows4, cbuf=rows4, rd=low(5, width, ff), outb=low(2, PADS, width),
        du=low(4, width, ff), dbr=tall, dbrb=rows4, rowv=wide(8, full), dbu=wide(1, ff),
        zsd=low(parts, piece, ff), ru=low(5, width, ff), zsu=low(parts, piece, ff),
        ro=low(5, hw, width), zso=low(parts, slab, width),
        ra=low(5, width, nh), zsa=low(parts, piece, nh), rb=low(5, width, nh), zsb=low(parts, piece, nh),
        zrd=low(others, piece, ff), zru=low(others, piece, ff), zro=low(others, slab, width),
        zra=low(others, piece, nh), zrb=low(others, piece, nh), gin=low(2, PADS, width),
    )
    small = [(piece, ff), (piece, ff), (slab, width), (piece, nh), (piece, nh)]
    vmem_out = dict(
        zip(("td", "tu", "to", "ta", "tb"), [wide(*d) if parts > 1 else wide(8, 128) for d in small]),
        rowt=wide(8, width), colt=wide(2, ff),
    )
    kept = dict(
        bv=low(*bias.shape), precv_f=tall, precv_m=tall, orecv=low(2, PADS, width), theirs=low(2, PADS, width),
        pr=tall, sbd=low(width, ff), rowb=wide(4, 8, width), colv=wide(2, ff), rr=wide(3, 8, width), cr=wide(4, 2, ff),
        rsum=wide(8, width), csum=wide(2, ff), rz=wide(peers, 8, width), cz=wide(peers, 2, ff),
    )
    sems = dict(
        ssem=(8,), rsem=(8,), csem=(3,), lsem=(4,), wsend=(4, 4), wrecv=(4, 4), msem_f=(12,),
        ssd=(4,), rsd=(6,), lsd=(6,), lsem_m=(2, 4), ps_m=(3,), pr_m=(3,), cs_m=(), msem_m=(11,),
        ssu=(4,), rsu=(6,), lsu=(6,), sso=(4,), rso=(6,), lso=(6,), ssa=(4,), rsa=(6,), lsa=(6,), ssb=(4,), rsb=(6,), lsb=(6,),
        lsem_b=(2, 4), zss=(5, others), zrs=(5, others), zls=(5, others + 1), es=(), er=(), hs=(), hr=(), cs=(),
        vs=(7,), vr=(7,), ws=(2, peers), wr=(2, peers), msem_b=(10,),
    )
    names = ["tok", "cot", "bias", "wq", "wo", "wu", "wd", *hbm, *vmem_out, *kept, *sems]

    def scoped(fn, shapes):
        pl.run_scoped(fn, *[pltpu.VMEM(d, t) for d, t in shapes])

    def kernel(*refs):
        r = types.SimpleNamespace(**dict(zip(names, refs)))
        x, k, y = spot = place()
        size, me = lax.axis_size("dp"), lax.axis_index("dp")
        plane = [at(1 - x, k, y), at(x, k, 1 - y), at(1 - x, k, 1 - y), at(x, 1 - k, y)]
        plane += [at(1 - x, 1 - k, y), at(x, 1 - k, 1 - y), at(1 - x, 1 - k, 1 - y)]
        greet(plane + [{"dp": lax.rem(me + o, size)} for o in range(1, size)])

        def first_ring():
            Scatter(r.dd, r.rd, None, None, r.sbd, None, r.ssd, r.rsd, r.lsd, spot).first()

        def second_ring():
            Scatter(r.du, r.ru, None, None, None, None, r.ssu, r.rsu, r.lsu, spot).first()

        scoped(
            lambda *v: forward_phase(
                r.tok, r.cot, r.bias, r.wq, r.wo, r.wu, r.wd,
                r.gq, r.go, r.gu, r.gd, r.xb, r.dyb, r.f1b, r.qh, r.oh, r.hflat, r.lse, r.residual, r.f2b,
                r.hidden, r.slope, r.dd, r.tbuf, r.cbuf, r.bv, r.precv_f,
                r.ssem, r.rsem, r.csem, r.lsem, r.wsend, r.wrecv, r.msem_f, spot, first_ring, *v,
            ),
            [hbm[n] for n in ("xb", "dyb", "f1b", "qh", "oh", "hflat", "lse", "residual", "f2b", "hidden", "slope", "dd")]
            + [rows4, low(full, nq), low(full, hw), low(full, ff), tall, tall],
        )

        def later():
            far = at(1 - x, k, y)
            pltpu.make_async_copy(r.theirs.at[0], r.outb.at[x], r.cs_m).wait()
            remote(r.theirs.at[1], r.outb.at[1 - x], r.ps_m.at[2], r.pr_m.at[2], far).wait_recv()
            remote(r.theirs.at[1], r.outb.at[x], r.ps_m.at[2], r.pr_m.at[2], far).wait_send()

        scoped(
            lambda *v: middle_phase(
                r.dd, r.gd, r.wd, r.gu, r.wu, r.xb, r.dyb, r.residual, r.f2b, r.hidden, r.slope,
                r.rd, r.outb, r.du, r.dbr, r.dbrb, r.rowv, r.dbu, r.precv_m, r.orecv, r.theirs, r.sbd,
                r.ssd, r.rsd, r.lsd, r.lsem_m, r.ps_m, r.pr_m, r.cs_m, r.msem_m, spot, second_ring, *v,
            ),
            [hbm[n] for n in ("xb", "dyb", "residual", "f2b", "hidden", "slope", "du", "dbr", "dbrb", "rowv", "dbu")]
            + [wide(4, 8, full), tall, low(full, ff), low(full, ff), low(PADS, ff), low(2, PADS, width), wide(PADS, full),
               low(3, width, ff)],
        )
        scoped(
            lambda *v: backward_phase(
                r.du, r.dd, r.rd, r.go, r.wo, r.gq, r.wq, r.xb, r.f1b, r.hflat, r.qh, r.oh, r.lse, r.dbr, r.dbrb, r.rowv, r.dbu,
                r.zsd, r.ru, r.zsu, r.ro, r.zso, r.ra, r.zsa, r.rb, r.zsb, r.zrd, r.zru, r.zro, r.zra, r.zrb, r.gin,
                r.td, r.tu, r.to, r.ta, r.tb, r.rowt, r.colt,
                r.pr, r.sbd, r.rowb, r.colv, r.rr, r.cr, r.rsum, r.csum, r.rz, r.cz,
                r.ssu, r.rsu, r.lsu, r.sso, r.rso, r.lso, r.ssa, r.rsa, r.lsa, r.ssb, r.rsb, r.lsb, r.ssd, r.rsd,
                r.lsem_b, r.zss, r.zrs, r.zls, r.es, r.er, r.hs, r.hr, r.cs, r.vs, r.vr, r.ws, r.wr, r.msem_b,
                spot, later, *v,
            ),
            [hbm[n] for n in ("xb", "f1b", "hflat", "dbr", "dbrb", "rowv", "dbu")]
            + [wide(2, 8, full), low(full, hw), low(PADS, nq), low(4, hw, width), low(2, 4, width, nh)]
            + [low(3, width, ff), low(width, ff), low(2, parts, piece, ff)]
            + [low(3, hw, width), low(hw, width), low(2, parts, slab, width)]
            + [low(3, width, nh), low(width, nh), low(2, parts, piece, nh), low(width, nh), low(2, parts, piece, nh)],
        )

    anyspec = pl.BlockSpec(memory_space=pl.ANY)
    outs = pl.pallas_call(
        kernel,
        out_shape=[jax.ShapeDtypeStruct(*v) for v in (*hbm.values(), *vmem_out.values())],
        in_specs=[anyspec] * 7,
        out_specs=[anyspec] * len(hbm) + [pl.BlockSpec(memory_space=pltpu.VMEM)] * len(vmem_out),
        scratch_shapes=[pltpu.VMEM(*v) for v in kept.values()] + [pltpu.SemaphoreType.DMA(v) for v in sems.values()],
        compiler_params=pltpu.CompilerParams(collective_id=0, has_side_effects=True, vmem_limit_bytes=VMEM_CAP),
        name="layer",
    )(tok, cot, bias, wq, wo, wu, wd)
    return types.SimpleNamespace(**dict(zip((*hbm, *vmem_out), outs)))


def shards(tokens, ln_gain, ln_bias, w_qkv, b_qv, w_out, b_out, w_up, b_up, w_down, b_down, cotangent):
    width = tokens.shape[1]
    hw = b_qv.shape[1]

    images = tokens.shape[0] // SEQ
    ff = b_up.shape[0]
    nq, hh = padded(hw), hw // 2

    def put(a, shape, *spot):
        a = a.reshape((1,) * (len(shape) - a.ndim) + a.shape)
        return jnp.pad(a, [(lo, n - m - lo) for lo, n, m in zip(spot, shape, a.shape)])

    wide = (images, PADS, width)
    vectors = sum(
        put(v, (PADS, width), SEQ + i, 0) for i, v in enumerate((ln_gain[0], ln_gain[1], ln_bias[0], ln_bias[1], b_out, b_down))
    )

    def halves(a):
        return sum(put(a[i * SEQ : (i + 1) * SEQ], wide, i, 0, 0) for i in range(images))

    tok2, cot2 = halves(tokens) + vectors[None], halves(cotangent)
    bias = put(b_up, (16, ff), 1, 0)
    for i in range(2):
        for p in (0, 2):
            bias += put(b_qv[p // 2, i * hh : (i + 1) * hh], (16, ff), 0, i * nq // 2 + p * hh)
    gap = jnp.zeros((nq // 2 - 3 * hh,), BF)
    side = jnp.zeros((width, gap.shape[0]), BF)
    qblock = jnp.concatenate(
        [w_qkv[:, p, i * hh : (i + 1) * hh] if p < 3 else side for i in range(2) for p in range(4)], axis=1
    )
    wot, wdt = w_out.T, w_down.T
    dp_size = lax.axis_size("dp")
    parts = dp_size if width % dp_size == 0 and (width // dp_size) % 8 == 0 else 1
    r = layer(parts, tok2, cot2, bias, qblock, wot, w_up, wdt)
    output = jnp.concatenate([r.outb[i, :SEQ] for i in range(images)])
    input_grad = jnp.concatenate([r.gin[i, :SEQ] for i in range(images)])
    td, tu, to, ta, tb, rowt, colt = r.td, r.tu, r.to, r.ta, r.tb, r.rowt, r.colt
    if parts == 1:

        def over_dp(a):
            return lax.psum_scatter(a[0], "dp", scatter_dimension=0, tiled=True).astype(F32)

        td, tu, to, ta, tb = (over_dp(a) for a in (r.zsd, r.zsu, r.zso, r.zsa, r.zsb))

    return (
        output,
        input_grad,
        rowt[0:2],
        rowt[2:4],
        jnp.concatenate([a[:, : 3 * hh].reshape(-1, 3, hh) for a in (ta, tb)], axis=2),
        jnp.stack(
            [jnp.concatenate([colt[0, i * nq // 2 + p * hh :][:hh] for i in range(2)]) for p in (0, 2)]
        ),
        to,
        rowt[4],
        tu,
        colt[1],
        td.T,
        rowt[5],
    )


def solution(mesh):
    placed = (
        P(("dp", "col"), "row"),
        P(None, "row"),
        P(None, "row"),
        P("row", None, "col"),
        P(None, "col"),
        P("col", "row"),
        P("row"),
        P("row", "col"),
        P("col"),
        P("col", "row"),
        P("row"),
        P(("dp", "col"), "row"),
    )
    return jax.shard_map(
        shards,
        mesh=mesh,
        in_specs=placed,
        out_specs=(
            P(("dp", "col"), "row"),
            P(("dp", "col"), "row"),
            P(None, "row"),
            P(None, "row"),
            P(("row", "dp"), None, "col"),
            P(None, "col"),
            P(("col", "dp"), "row"),
            P("row"),
            P(("row", "dp"), "col"),
            P("col"),
            P("col", ("row", "dp")),
            P("row"),
        ),
        check_vma=False,
    )
```

```python
import types

import jax
import jax.numpy as jnp
from jax import lax
from jax.experimental import pallas as pl
from jax.experimental.pallas import tpu as pltpu
from jax.sharding import PartitionSpec as P

HD = 72
SEQ = 729
EPS = 1e-06
BF = jnp.bfloat16
F32 = jnp.float32


def nn(a, b):
    return jnp.dot(a, b, preferred_element_type=F32)


def nt(a, b):
    return lax.dot_general(a, b, (((1,), (1,)), ((), ())), preferred_element_type=F32)


def tn(a, b):
    return lax.dot_general(a, b, (((0,), (0,)), ((), ())), preferred_element_type=F32)


def gelu_parts(u):
    t = jnp.tanh(0.7978845608028654 * (u + 0.044715 * u * u * u))
    value = 0.5 * u * (1.0 + t)
    slope = 0.5 * (1.0 + t) + 0.5 * u * (1.0 - t * t) * 0.7978845608028654 * (1.0 + 3 * 0.044715 * u * u)
    return value, slope


MESH = pl.DeviceIdType.MESH
PADS = 736
VMEM_CAP = 66_000_000


def place():
    row, col = lax.axis_index("row"), lax.axis_index("col")
    return row // 2, lax.rem(row, 2), col


def at(x, k, y):
    return {"row": 2 * x + k, "col": y}


def greet(peers):
    barrier = pltpu.get_barrier_semaphore()
    for peer in peers:
        pl.semaphore_signal(barrier, inc=1, device_id=peer, device_id_type=MESH)
    pl.semaphore_wait(barrier, len(peers))


def chunks(total, step, body):
    whole = total // step
    if whole > 0:
        lax.fori_loop(0, whole, lambda i, c: (body(pl.multiple_of(i * step, step), step), c)[1], 0)
    if total % step:
        body(whole * step, total % step)


def column(part, head, hw):
    half, left = divmod(head, hw // HD // 2)
    return half * (padded(hw) // 2) + part * (hw // 2) + left * HD


def padded(hw):
    return 2 * (-(-3 * hw // 2 // 128) * 128)


class Moves:
    def __init__(self, sems):
        self.sems, self.open = sems, {}

    def start(self, src, dst):
        c = pltpu.make_async_copy(src, dst, self.sems.at[len(self.open)])
        c.start()
        self.open[len(self.open)] = c
        return c

    def finish(self):
        for c in self.open.values():
            c.wait()


def forward_phase(
    tok, cot, bias, wq, wo, wu, wd,
    gq, go, gu, gd, xb_h, dyb_h, f1b_h, qh_h, oh_h, hflat_h, lse_h, residual_h, f2b_h, hidden_h, slope_h, dd_h,
    tbuf, cbuf, bv, precv, ssem, rsem, csem, lsem, wsend, wrecv, msem, spot, after,
    xb, dyb, f1b, qh, oh, hflat, lse, residual, f2b, hidden, slope, dd, tb, gqv, gov, guv, f1, psend,
):
    x, k, y = spot
    is_a, is_b = k == y, k != y
    hw = hflat.shape[1]
    heads = hw // HD
    width = tok.shape[2]
    blocks, wholes = (wq, wo, wu, wd), (gq, go, gu, gd)
    out = Moves(msem)
    over_y = (1,)

    def own_sends(w):
        b, g = blocks[w], wholes[w]
        a = [
            remote(b, g.at[2 + k], wsend.at[w, 0], wrecv.at[w, 2 + k], at(1 - x, k, y)),
            remote(b, g.at[k], wsend.at[w, 1], wrecv.at[w, k], at(x, k, 1 - y)),
        ]
        bb = [
            remote(b, g.at[2 + k], wsend.at[w, 0], wrecv.at[w, 2 + k], at(1 - x, 1 - k, y)),
            remote(b, g.at[k], wsend.at[w, 1], wrecv.at[w, k], at(x, 1 - k, 1 - y)),
            remote(b, g.at[k], wsend.at[w, 2], wrecv.at[w, k], at(x, 1 - k, y)),
        ]
        return a, bb

    def relays(w):
        g = wholes[w]
        return (
            remote(g.at[2], g.at[2], wsend.at[w, 3], wrecv.at[w, 2], at(x, k, 1 - y)),
            remote(g.at[1], g.at[3], wsend.at[w, 3], wrecv.at[w, 3], at(1 - x, k, y)),
            remote(g.at[3], g.at[3], wsend.at[w, 2], wrecv.at[w, 3], at(x, k, 1 - y)),
        )

    def both(fa, fb):
        pl.when(is_a)(fa)
        pl.when(is_b)(fb)

    def start_own(w):
        a, b = own_sends(w)
        both(lambda: [c.start() for c in a] and None, lambda: [c.start() for c in b] and None)

    def arrived(w, j):
        remote(blocks[w], wholes[w].at[j], wsend.at[w, 0], wrecv.at[w, j], at(x, 1 - k, y)).wait_recv()

    def start_relay(w):
        ra, rb, rc = relays(w)

        def fa():
            arrived(w, 2)
            ra.start()
            if w in over_y:
                arrived(w, 3)
                rc.start()

        def fb():
            arrived(w, 1)
            rb.start()

        pl.when(is_a)(fa)
        if w not in over_y:
            pl.when(is_b)(fb)

    def wait_rest(w):
        pl.when(is_b | (k == 1))(lambda: arrived(w, 0))
        pl.when(is_a & (k == 0))(lambda: arrived(w, 1))
        pl.when(is_b)(lambda: arrived(w, 2))
        if w in over_y:
            pl.when(is_b)(lambda: (arrived(w, 1), arrived(w, 3)) and None)
        else:
            arrived(w, 3)

    def finish_sends(w):
        a, b = own_sends(w)
        ra, rb, rc = relays(w)
        a, b = (a + [ra, rc], b) if w in over_y else (a + [ra], b + [rb])
        both(
            lambda: [c.wait_send() for c in a] and None,
            lambda: [c.wait_send() for c in b] and None,
        )

    def load(w, dst):
        b, g = blocks[w], wholes[w]
        for j in range(4):
            rows = pl.ds(j * width, width)
            local = is_a & (k == j) if j < 2 else None
            if local is None:
                pltpu.make_async_copy(g.at[j], dst.at[rows], lsem.at[j]).start()
            else:
                pl.when(local)(lambda: pltpu.make_async_copy(b, dst.at[rows], lsem.at[j]).start())
                pl.when(jnp.logical_not(local))(
                    lambda: pltpu.make_async_copy(g.at[j], dst.at[rows], lsem.at[j]).start()
                )
        for j in range(4):
            pltpu.make_async_copy(g.at[j], dst.at[pl.ds(j * width, width)], lsem.at[j]).wait()

    tx = remote(tok.at[1 - x], tbuf.at[2 + k], ssem.at[0], rsem.at[0], at(1 - x, k, y))
    cx = remote(cot.at[1 - x], cbuf.at[2 + k], ssem.at[1], rsem.at[1], at(1 - x, k, y))
    t1 = remote(tok.at[x], tbuf.at[k], ssem.at[2], rsem.at[2], at(x, 1 - k, y))
    c1 = remote(cot.at[x], cbuf.at[k], ssem.at[3], rsem.at[3], at(x, 1 - k, y))
    t2 = remote(tbuf.at[2 + k], tbuf.at[2 + k], ssem.at[4], rsem.at[4], at(x, 1 - k, y))
    c2 = remote(cbuf.at[2 + k], cbuf.at[2 + k], ssem.at[5], rsem.at[5], at(x, 1 - k, y))
    bs = remote(bias, bv, ssem.at[6], rsem.at[6], at(x, k, 1 - y))
    pe = remote(psend, precv, ssem.at[7], rsem.at[7], at(x, 1 - k, y))

    def collect(src, buf, wide):
        parts = [(src.at[x], k), (buf.at[1 - k], 1 - k), (buf.at[2], 2), (buf.at[3], 3)]
        copies = [pltpu.make_async_copy(a, tb.at[j], lsem.at[i]) for i, (a, j) in enumerate(parts)]
        for c in copies:
            c.start()
        for c in copies:
            c.wait()
        for j in range(4):
            wide[:, j * width : (j + 1) * width] = tb[j]

    bl = pltpu.make_async_copy(bias, bv, csem.at[2])

    tx.start()
    t1.start()
    start_own(0)
    both(lambda: (bl.start(), bs.start()) and None, lambda: None)
    c1.start()

    tx.wait_recv()
    t2.start()
    t1.wait_recv()
    t2.wait_recv()
    collect(tok, tbuf, xb)
    vecs = xb[SEQ - 1 : PADS, :].astype(F32)
    g1, g2, s1, s2, bo = (vecs[j : j + 1] for j in range(1, 6))

    def stats(v):
        mean = jnp.mean(v, axis=1, keepdims=True)
        c = v - mean
        return c * lax.rsqrt(jnp.mean(c * c, axis=1, keepdims=True) + EPS)

    def norm1(r, n):
        f1[pl.ds(r, n), :] = (stats(xb[pl.ds(r, n), :].astype(F32)) * g1 + s1).astype(BF)

    chunks(PADS, 128, norm1)
    f2 = f1
    start_relay(0)
    start_own(1)
    both(bl.wait, bs.wait_recv)
    wait_rest(0)
    load(0, gqv)

    def project(c, n):
        cols = pl.ds(c, n)
        hidden[:, cols] = (nn(f1[...], gqv[:, cols]) + bv[0:1, cols].astype(F32)).astype(BF)

    chunks(gqv.shape[1], 256, project)
    start_relay(1)
    start_own(2)
    for j in range(4):
        f1b[j] = f1[:, j * width : (j + 1) * width]
    qh[...] = jnp.zeros_like(qh)
    for p in range(3):
        for h in range(heads):
            lo = column(p, h, hw)
            qh[p * heads + h, :, 0:HD] = hidden[:, lo : lo + HD]
    out.start(xb, xb_h)
    out.start(f1b, f1b_h)
    out.start(qh, qh_h)
    keymask = jnp.where(lax.broadcasted_iota(jnp.int32, (PADS, 1), 0) < SEQ, 0.0, -1e30)

    def attend(h, carry):
        st = nt(qh[heads + h], qh[h]) + keymask
        top = jnp.max(st, axis=0, keepdims=True)
        e = jnp.exp((st - top) * HD ** (-0.5))
        tot = jnp.sum(e, axis=0, keepdims=True)
        lse[pl.ds(h, 1), :] = top * HD ** (-0.5) + jnp.log(tot)
        out = tn(qh[2 * heads + h], e.astype(BF)) / tot
        oh[h] = out.T.astype(BF)
        return carry

    lax.fori_loop(0, heads, attend, 0)
    for h in range(heads):
        hflat[:, h * HD : (h + 1) * HD] = oh[h, :, 0:HD]
    out.start(oh, oh_h)
    out.start(hflat, hflat_h)
    out.start(lse, lse_h)
    wait_rest(1)
    load(1, gov)

    def out_project(c, n):
        cols = pl.ds(c, n)
        part = nt(hflat[...], gov[cols, :])
        psend[:, cols] = part.astype(BF)
        residual[:, cols] = part

    chunks(4 * width, 384, out_project)
    pe.start()
    pe.wait_recv()

    def norm2(r, n):
        rows = pl.ds(r, n)
        v = xb[rows, :].astype(F32) + bo + residual[rows, :] + precv[rows, :].astype(F32)
        residual[rows, :] = v
        f2[rows, :] = (stats(v) * g2 + s2).astype(BF)

    chunks(PADS, 128, norm2)
    start_relay(2)
    cx.start()
    start_own(3)
    wait_rest(2)
    load(2, guv)
    for j in range(4):
        f2b[j] = f2[:, j * width : (j + 1) * width]
    out.start(residual, residual_h)
    out.start(f2b, f2b_h)

    def expand(c, n):
        cols = pl.ds(c, n)
        u = nn(f2[...], guv[:, cols]) + bv[1:2, cols].astype(F32)
        value, grad = gelu_parts(u)
        hidden[:, cols] = value.astype(BF)
        slope[:, cols] = grad.astype(BF)

    chunks(hidden.shape[1], 256, expand)
    out.start(hidden, hidden_h)
    out.start(slope, slope_h)
    cx.wait_recv()
    c2.start()
    c1.wait_recv()
    c2.wait_recv()
    collect(cot, cbuf, dyb)

    def down_grad(j, carry):
        dd[j] = tn(tb[j], hidden[...]).astype(BF)
        return carry

    out.start(dyb, dyb_h)
    start_relay(3)
    lax.fori_loop(0, 4, down_grad, 0)
    out.start(dd, dd_h)
    out.finish()
    wait_rest(3)
    after()
    for c in (tx, cx, t1, c1, t2, c2, pe):
        c.wait_send()
    both(bs.wait_send, lambda: None)
    for w in range(4):
        finish_sends(w)


def load_weight(b, g, dst, sem, k, is_a):
    width = b.shape[0]
    for j in range(4):
        rows = pl.ds(j * width, width)
        if j < 2:
            local = is_a & (k == j)
            pl.when(local)(lambda: pltpu.make_async_copy(b, dst.at[rows], sem.at[j]).start())
            pl.when(jnp.logical_not(local))(lambda: pltpu.make_async_copy(g.at[j], dst.at[rows], sem.at[j]).start())
        else:
            pltpu.make_async_copy(g.at[j], dst.at[rows], sem.at[j]).start()

    def wait():
        for j in range(4):
            pltpu.make_async_copy(g.at[j], dst.at[pl.ds(j * width, width)], sem.at[j]).wait()

    return wait


def remote(src, dst, s, r, dest):
    return pltpu.make_async_remote_copy(
        src_ref=src, dst_ref=dst, send_sem=s, recv_sem=r, device_id=dest, device_id_type=MESH
    )


class Scatter:
    def __init__(self, d, r, zs, st, sb, cv, ss, rs, ls, spot):
        self.d, self.r, self.zs, self.st, self.sb, self.cv, self.ls, self.spot = d, r, zs, st, sb, cv, ls, spot
        x, k, y = spot
        self.is_a, self.is_b, self.k = k == y, k != y, k
        across, over, mate = at(1 - x, k, y), at(x, k, 1 - y), at(x, 1 - k, y)
        self.x1 = remote(d.at[2], r.at[0], ss.at[0], rs.at[0], across)
        self.y1 = remote(d.at[3], r.at[1], ss.at[1], rs.at[1], over)
        self.y1b = remote(d.at[1], r.at[2], ss.at[2], rs.at[2], over)
        if sb is not None:
            self.x2 = remote(sb, r.at[3], ss.at[1], rs.at[3], across)
            self.y2 = remote(sb, r.at[4], ss.at[3], rs.at[4], over)
        if zs is not None:
            self.home = remote(cv.at[1], zs, ss.at[2], rs.at[5], mate)

    def first(self):
        self.x1.start()

        def b():
            self.y1.start()
            self.y1b.start()

        pl.when(self.is_b)(b)

    def copy_in(self, pairs):
        for i, src in pairs:
            pltpu.make_async_copy(src, self.st.at[i], self.ls.at[i]).start()
        for i, src in pairs:
            pltpu.make_async_copy(src, self.st.at[i], self.ls.at[i]).wait()

    def second(self):
        st, sb = self.st, self.sb

        def fetch_a():
            self.y1.wait_recv()
            self.copy_in([(0, self.d.at[3]), (1, self.r.at[1])])

        def fetch_b():
            self.x1.wait_recv()
            self.copy_in([(0, self.d.at[0]), (1, self.r.at[0])])

        pl.when(self.is_a)(fetch_a)
        pl.when(self.is_b)(fetch_b)

        def add(c, n):
            cols = pl.ds(c, n)
            sb[:, cols] = (st[0, :, cols].astype(F32) + st[1, :, cols].astype(F32)).astype(BF)

        chunks(sb.shape[1], 128, add)
        pl.when(self.is_a)(self.x2.start)
        pl.when(self.is_b)(self.y2.start)

    def settle(self):
        def a():
            self.x1.wait_recv()
            self.y1b.wait_recv()
            self.x2.wait_recv()
            self.y2.wait_recv()

        pl.when(self.is_a)(a)

    def third(self):
        self.settle()
        st, cv = self.st, self.cv
        parts, piece = cv.shape[1], cv.shape[2]

        def a():
            d, r = self.d, self.r
            for which, trio in ((self.k, (d.at[0], r.at[0], r.at[4])), (1 - self.k, (d.at[1], r.at[2], r.at[3]))):
                self.copy_in(list(enumerate(trio)))

                def add(c, n):
                    cols = pl.ds(c, n)
                    total = sum(st[i, :, cols].astype(F32) for i in range(3))
                    for q in range(parts):
                        cv[which, q, :, cols] = total[q * piece : (q + 1) * piece].astype(BF)

                chunks(cv.shape[3], 128, add)
            self.home.start()
            keep = pltpu.make_async_copy(cv.at[0], self.zs, self.ls.at[0])
            keep.start()
            keep.wait()

        pl.when(self.is_a)(a)

    def fourth(self):
        pl.when(self.is_b)(self.home.wait_recv)

    def home_sent(self):
        pl.when(self.is_a)(self.home.wait_send)

    def close(self, home=True):
        self.x1.wait_send()
        pl.when(self.is_a)(self.x2.wait_send)
        if home:
            self.home_sent()

        def b():
            self.y1.wait_send()
            self.y1b.wait_send()
            self.y2.wait_send()

        pl.when(self.is_b)(b)

    @staticmethod
    def peers(spot):
        x, k, y = spot
        return [at(1 - x, k, y), at(x, k, 1 - y), at(x, 1 - k, y)]


def norm_back_rows(values, mine, theirs, gain):
    mean = jnp.mean(values, axis=1, keepdims=True)
    center = values - mean
    scale = lax.rsqrt(jnp.mean(center * center, axis=1, keepdims=True) + EPS)
    normed = center * scale
    incoming = mine.astype(F32) + theirs.astype(F32)
    e = incoming * gain
    back = scale * (e - jnp.mean(e, axis=1, keepdims=True) - normed * jnp.mean(e * normed, axis=1, keepdims=True))
    return back, normed, incoming


def fold(acc, i, rows):
    acc[i] += sum(rows[8 * j : 8 * j + 8] for j in range(rows.shape[0] // 8))


def middle_phase(
    dd, gd, wd, gu, wu, xb_h, dyb_h, residual_h, f2b_h, hidden_h, slope_h,
    rd, outb, du_h, dbr_h, dbrb_h, rowv_h, dbu_h,
    precv, orecv, theirs, sb, ss, rs, ls, lsem, ps, pr, cs, msem, spot, after,
    xb, dyb, residual, f2b, hidden, slope, du, dbr, dbrb, rowv, dbu,
    acc, psend, gdv, guv, dup, osend, full, st,
):
    x, k, y = spot
    is_a = k == y
    width = wd.shape[0]
    ring = Scatter(dd, rd, None, st, sb, None, ss, rs, ls, spot)
    got_d = load_weight(wd, gd, gdv, lsem.at[0], k, is_a)
    moves = Moves(msem)
    got = [moves.start(a, b) for a, b in ((dyb_h, dyb), (slope_h, slope))]
    got_u = load_weight(wu, gu, guv, lsem.at[1], k, is_a)
    more = [
        moves.start(a, b) for a, b in ((hidden_h, hidden), (f2b_h, f2b), (residual_h, residual), (xb_h, xb))
    ]
    got_d()
    for c in got:
        c.wait()

    def contract(c, n):
        cols = pl.ds(c, n)
        grad = (nn(dyb[...], gdv[:, cols]) * slope[:, cols].astype(F32)).astype(BF)
        dup[:, cols] = grad
        dbu[:, cols] = jnp.sum(grad.astype(F32), axis=0, keepdims=True)

    chunks(slope.shape[1], 256, contract)
    got_u()
    for c in more:
        c.wait()
    tail = [pltpu.make_async_copy(a, b, msem.at[6 + i]) for i, (a, b) in enumerate(
        ((du, du_h), (dbr, dbr_h), (dbrb, dbrb_h), (rowv, rowv_h), (dbu, dbu_h)))]

    def up_grad(j, carry):
        du[j] = tn(f2b[j], dup[...]).astype(BF)
        return carry

    lax.fori_loop(0, 4, up_grad, 0)
    tail[0].start()

    def second_grad(c, n):
        rows = pl.ds(c, n)
        psend[:, rows] = nt(dup[...], guv[rows, :]).astype(BF)

    chunks(psend.shape[1], 384, second_grad)
    exchange = remote(psend, precv, ps.at[0], pr.at[0], at(x, 1 - k, y))
    exchange.start()
    tail[0].wait()
    ring.second()
    after()
    low = k == 0
    bd = xb[SEQ - 1 : PADS, :].astype(F32)[6:7]

    def side(a, i):
        lo = 2 * i * width
        return jnp.where(low, a[:, lo : lo + width], a[:, lo + width : lo + 2 * width])

    def down(c, n):
        rows = pl.ds(c, n)
        full[:, rows] = nt(hidden[...], gdv[rows, :])

    chunks(4 * width, 384, down)

    def far(a, i):
        lo = 2 * i * width
        return jnp.where(low, a[:, lo + width : lo + 2 * width], a[:, lo : lo + width])

    for i in range(2):
        osend[i] = far(full, i).astype(BF)
    outs = remote(osend, orecv, ps.at[1], pr.at[1], at(x, 1 - k, y))
    outs.start()
    outs.wait_recv()
    for i in range(2):
        theirs[i] = (side(full, i) + side(residual, i) + side(bd, i) + orecv[i].astype(F32)).astype(BF)
    mine = pltpu.make_async_copy(theirs.at[0], outb.at[x], cs)
    mine.start()

    exchange.wait_recv()
    g2 = xb[SEQ - 1 : PADS, :].astype(F32)[2:3]
    acc[...] = jnp.zeros_like(acc)

    def norm2(r, n):
        rows = pl.ds(r, n)
        back, normed, incoming = norm_back_rows(residual[rows, :], psend[rows, :], precv[rows, :], g2)
        dyr = dyb[rows, :].astype(F32)
        low = (dyr + back).astype(BF)
        dbr[rows, :] = low
        fold(acc, 0, incoming * normed)
        fold(acc, 1, incoming)
        fold(acc, 2, low.astype(F32))
        fold(acc, 3, dyr)

    chunks(PADS, 128, norm2)
    rowv[...] = jnp.concatenate(
        [jnp.sum(acc[i], axis=0, keepdims=True) for i in range(4)] + [jnp.zeros((4, 4 * width), F32)], axis=0
    )
    for j in range(4):
        dbrb[j] = dbr[:, j * width : (j + 1) * width]
    for c in tail[1:]:
        c.start()
    exchange.wait_send()
    outs.wait_send()
    for c in tail[1:]:
        c.wait()


class DpSum:
    def __init__(self, zs, zr, buf, out, ss, rs, ls):
        self.zs, self.zr, self.buf, self.out, self.ls = zs, zr, buf, out, ls
        size = lax.axis_size("dp")
        self.me = lax.axis_index("dp")
        self.copies = []
        for o in range(1, size):
            dest = lax.rem(self.me + o, size)
            self.copies.append(remote(zs.at[dest], zr.at[o - 1], ss.at[o - 1], rs.at[o - 1], {"dp": dest}))

    def start(self):
        for c in self.copies:
            c.start()

    def finish(self):
        for c in self.copies:
            c.wait_recv()
        sources = [self.zs.at[self.me]] + [self.zr.at[i] for i in range(len(self.copies))]
        for i, src in enumerate(sources):
            pltpu.make_async_copy(src, self.buf.at[i], self.ls.at[i]).start()
        for i, src in enumerate(sources):
            pltpu.make_async_copy(src, self.buf.at[i], self.ls.at[i]).wait()
        buf, out = self.buf, self.out

        def add(c, n):
            cols = pl.ds(c, n)
            out[:, cols] = sum(buf[i, :, cols].astype(F32) for i in range(len(sources)))

        chunks(out.shape[1], 128, add)

    def close(self):
        for c in self.copies:
            c.wait_send()


def backward_phase(
    du, dd, rd, go, wo, gq, wq, xb_h, f1b_h, hflat_h, qh_h, oh_h, lse_h, dbr_h, dbrb_h, vec2_h, dbu_h,
    zsd, ru, zsu, ro, zso, ra, zsa, rb, zsb, zrd, zru, zro, zra, zrb, gin,
    td, tu, to, ta, tb, rowt, colt,
    pr, sbd, rowb, colv, rr, cr, rsum, csum, rz, cz,
    ssu, rsu, lsu, sso, rso, lso, ssa, rsa, lsa, ssb, rsb, lsb, ssd, rsd,
    lsem, zss, zrs, zls, es, er, hs, hr, cs, vs, vr, ws, wr, msem, spot, later, far_start,
    xb, f1b, hflat, dbr, dbrb, vec2, dbu,
    acc, gov, dqkv, do, dq,
    stu, sbu, cvu, sto, sbo, cvo, sta, sba, cva, sbb, cvb,
):
    x, k, y = spot
    is_a, is_b = k == y, k != y
    width, hw = xb.shape[1] // 4, hflat.shape[1]
    heads = hw // HD
    size, me = lax.axis_size("dp"), lax.axis_index("dp")
    summed = cvu.shape[1] > 1
    plane = [at(1 - x, k, y), at(x, k, 1 - y), at(1 - x, k, 1 - y)]
    side = jnp.where(is_a, 0, 1)
    row_sends = [
        remote(rowb.at[k if i == 1 else 2 + k], rr.at[i], vs.at[i], vr.at[i], plane[i]) for i in range(3)
    ]
    col_sends = [
        remote(colv, cr.at[side], vs.at[3], vr.at[3 + side], at(x, 1 - k, k)),
        remote(colv, cr.at[2 + side], vs.at[4], vr.at[5 + side], at(1 - x, k, k)),
        remote(colv, cr.at[2 + side], vs.at[5], vr.at[5 + side], at(1 - x, 1 - k, k)),
    ]
    col_extra = remote(colv, cr.at[1], vs.at[6], vr.at[4], at(x, k, k))
    dp_sends = []
    for o in range(1, size):
        dest = {"dp": lax.rem(me + o, size)}
        dp_sends.append(remote(rsum, rz.at[o - 1], ws.at[0, o - 1], wr.at[0, o - 1], dest))
        dp_sends.append(remote(csum, cz.at[o - 1], ws.at[1, o - 1], wr.at[1, o - 1], dest))
    ring_u = Scatter(du, ru, zsu, stu, sbu, cvu, ssu, rsu, lsu, spot)
    moves = Moves(msem)
    got = [moves.start(a, b) for a, b in ((dbr_h, dbr), (hflat_h, hflat), (dbrb_h, dbrb))]
    got_o = load_weight(wo, go, gov, lsem.at[0], k, is_a)
    more = [moves.start(a, b) for a, b in ((f1b_h, f1b), (xb_h, xb), (vec2_h, vec2), (dbu_h, dbu))]
    ring_d = Scatter(dd, rd, zsd, stu, sbd, cvu, ssd, rsd, lsu, spot)
    ring_o = Scatter(do, ro, zso, sto, sbo, cvo, sso, rso, lso, spot)
    ring_a = Scatter(dq.at[0], ra, zsa, sta, sba, cva, ssa, rsa, lsa, spot)
    ring_b = Scatter(dq.at[1], rb, zsb, sta, sbb, cvb, ssb, rsb, lsb, spot)
    if summed:
        sums = [
            DpSum(zs, zr, cv.at[0], t, zss.at[i], zrs.at[i], zls.at[i])
            for i, (zs, zr, cv, t) in enumerate(
                ((zsd, zrd, cvu, td), (zsu, zru, cvu, tu), (zso, zro, cvo, to), (zsa, zra, cva, ta), (zsb, zrb, cvb, tb))
            )
        ]
    def attention(qh, oh, lse, dh, dqh):
        inner = [moves.start(a, b) for a, b in ((qh_h, qh), (oh_h, oh), (lse_h, lse))]
        ring_d.third()
        dh[...] = jnp.zeros_like(dh)
        for c in got:
            c.wait()
        got_o()
        dqkv[:, 0:hw] = nn(dbr[...], gov[...]).astype(BF)
        for h in range(heads):
            dh[h, :, 0:HD] = dqkv[:, h * HD : (h + 1) * HD]

        def out_grad(j, carry):
            do[j] = tn(hflat[...], dbrb[j]).astype(BF)
            return carry

        lax.fori_loop(0, 4, out_grad, 0)
        ring_d.fourth()
        if summed:
            sums[0].start()
        for c in more + inner:
            c.wait()
        keymask = jnp.where(lax.broadcasted_iota(jnp.int32, (PADS, 1), 0) < SEQ, 0.0, -1e30)
        ones = jnp.ones((8, 128), F32)

        def attend(h, carry):
            q, kk, v, g = qh[h], qh[heads + h], qh[2 * heads + h], dh[h]
            p = jnp.exp(nt(kk, q) * HD ** (-0.5) + keymask - lse[pl.ds(h, 1), :])
            delta = lax.dot_general(
                ones, g.astype(F32) * oh[h].astype(F32), (((1,), (1,)), ((), ())),
                precision=lax.Precision.HIGHEST, preferred_element_type=F32,
            )[0:1]
            ds = (p * (nt(v, g) - delta)).astype(BF)
            dqh[2 * heads + h] = nn(p.astype(BF), g).astype(BF)
            dqh[heads + h] = (nn(ds, q) * HD ** (-0.5)).astype(BF)
            dqh[h] = (tn(kk, ds) * HD ** (-0.5)).T.astype(BF)
            return carry

        half_cols, group = dq.shape[3], heads // 2

        def one_half(half, carry):
            lax.fori_loop(half * group, (half + 1) * group, attend, 0)
            cols = pl.ds(pl.multiple_of(half * half_cols, 128), half_cols)
            block = dqkv.at[:, cols]
            for p in range(3):
                for i in range(group):
                    lo = (p * group + i) * HD
                    block[:, lo : lo + HD] = dqh[p * heads + half * group + i, :, 0:HD]
            block[:, 3 * group * HD :] = jnp.zeros((PADS, half_cols - 3 * group * HD), BF)

            def qkv_grad(j, c):
                dq[half, j] = tn(f1b[j], block[...]).astype(BF)
                return c

            lax.fori_loop(0, 4, qkv_grad, 0)

            @pl.when(half == 0)
            def _():
                ring_u.second()
                ring_o.first()
                ring_a.first()

            return carry

        lax.fori_loop(0, 2, one_half, 0)

    pl.run_scoped(
        attention,
        pltpu.VMEM(qh_h.shape, BF), pltpu.VMEM(oh_h.shape, BF), pltpu.VMEM(lse_h.shape, F32),
        pltpu.VMEM((heads,) + qh_h.shape[1:], BF), pltpu.VMEM(qh_h.shape, BF),
    )
    ring_b.first()

    def ending(gqv, ps, home):
        got_q = load_weight(wq, gq, gqv, lsem.at[1], k, is_a)
        ring_d.home_sent()
        ring_u.third()
        ring_u.fourth()
        if summed:
            sums[1].start()
        ring_o.second()
        got_q()

        def first_grad(c, n):
            rows = pl.ds(c, n)
            ps[:, rows] = nt(dqkv[...], gqv[rows, :]).astype(BF)

        chunks(ps.shape[1], 384, first_grad)
        exchange = remote(ps, pr, es, er, at(x, 1 - k, y))
        exchange.start()
        ring_a.second()

        def bias_grad(c, n):
            cols = pl.ds(c, n)
            colv[0:1, cols] = jnp.sum(dqkv[:, cols].astype(F32), axis=0, keepdims=True)

        chunks(dqkv.shape[1], 128, bias_grad)
        colv[1:2, :] = dbu[...]
        exchange.wait_recv()
        exchange.wait_send()
        g1 = xb[SEQ - 1 : PADS, :].astype(F32)[1:2]
        acc[...] = jnp.zeros_like(acc)

        def norm1(r, n):
            rows = pl.ds(r, n)
            back, normed, incoming = norm_back_rows(xb[rows, :].astype(F32), ps[rows, :], pr[rows, :], g1)
            ps[rows, :] = (dbr[rows, :].astype(F32) + back).astype(BF)
            fold(acc, 0, incoming * normed)
            fold(acc, 1, incoming)

        chunks(PADS, 128, norm1)
        gain, shift = (jnp.sum(acc[i], axis=0, keepdims=True) for i in range(2))
        rows6 = jnp.concatenate(
            [gain, vec2[0:1], shift, vec2[1:2], vec2[2:3], vec2[3:4], jnp.zeros((2, 4 * width), F32)], axis=0
        )
        for j in range(4):
            rowb[j] = rows6[:, j * width : (j + 1) * width]
        for c in row_sends + col_sends:
            c.start()
        pl.when(is_b)(col_extra.start)
        low = k == 0
        for i in range(2):
            lo = 2 * i * width
            home[i] = jnp.where(low, ps[:, lo : lo + width], ps[:, lo + width : lo + 2 * width])
        mine = pltpu.make_async_copy(home.at[0], gin.at[x], cs)
        mine.start()
        away = remote(home.at[1], gin.at[x], hs, hr, at(1 - x, k, y))
        ring_b.second()
        away.start()
        far_start()
        ring_o.third()
        ring_o.fourth()
        if summed:
            sums[0].finish()
            sums[2].start()
        ring_a.third()
        ring_a.fourth()
        if summed:
            sums[3].start()
        for c in row_sends:
            c.wait_recv()
        for i in range(1, 4):
            remote(colv, cr.at[i], vs.at[3], vr.at[3 + i], at(x, 1 - k, k)).wait_recv()
        pl.when(is_b)(lambda: remote(colv, cr.at[0], vs.at[3], vr.at[3], at(x, 1 - k, k)).wait_recv())
        rsum[...] = rowb[k] + rr[0] + rr[1] + rr[2]

        @pl.when(is_a)
        def _():
            csum[...] = colv[...] + cr[1] + cr[2] + cr[3]

        @pl.when(is_b)
        def _():
            csum[...] = cr[0] + cr[1] + cr[2] + cr[3]

        for c in dp_sends:
            c.start()
        ring_b.third()
        ring_b.fourth()
        if summed:
            sums[4].start()
            sums[1].finish()
        mine.wait()
        remote(home.at[1], gin.at[1 - x], hs, hr, at(1 - x, k, y)).wait_recv()
        away.wait_send()
        for ring in (ring_u, ring_o, ring_a, ring_b):
            ring.close()
        for c in row_sends + col_sends:
            c.wait_send()
        pl.when(is_b)(col_extra.wait_send)
        for c in dp_sends:
            c.wait_recv()
            c.wait_send()
        rowt[...] = rsum[...] + sum(rz[o] for o in range(size - 1))
        colt[...] = csum[...] + sum(cz[o] for o in range(size - 1))
        if summed:
            for total in sums[2:]:
                total.finish()
            for total in sums:
                total.close()

        later()
        ring_d.close(home=False)

    pl.run_scoped(
        ending, pltpu.VMEM((4 * width, wq.shape[1]), BF), pltpu.VMEM(pr.shape, BF), pltpu.VMEM((2, PADS, width), BF)
    )


def layer(parts, tok, cot, bias, wq, wo, wu, wd):
    width, hw, ff, nq = tok.shape[2], wo.shape[1], wu.shape[1], wq.shape[1]
    full, heads, nh = 4 * width, hw // HD, nq // 2
    others = max(parts - 1, 1)
    peers = lax.axis_size("dp") - 1
    piece, slab = width // parts, hw // parts
    low = lambda *d: (d, BF)
    wide = lambda *d: (d, F32)
    tall, rows4 = low(PADS, full), low(4, PADS, width)
    hbm = dict(
        gq=low(4, width, nq), go=low(4, width, hw), gu=low(4, width, ff), gd=low(4, width, ff),
        xb=tall, dyb=tall, f1b=rows4, qh=low(3 * heads, PADS, 128), oh=low(heads, PADS, 128), hflat=low(PADS, hw),
        lse=wide(heads, PADS), residual=wide(PADS, full), f2b=rows4, hidden=low(PADS, ff), slope=low(PADS, ff),
        dd=low(4, width, ff), tbuf=rows4, cbuf=rows4, rd=low(5, width, ff), outb=low(2, PADS, width),
        du=low(4, width, ff), dbr=tall, dbrb=rows4, rowv=wide(8, full), dbu=wide(1, ff),
        zsd=low(parts, piece, ff), ru=low(5, width, ff), zsu=low(parts, piece, ff),
        ro=low(5, hw, width), zso=low(parts, slab, width),
        ra=low(5, width, nh), zsa=low(parts, piece, nh), rb=low(5, width, nh), zsb=low(parts, piece, nh),
        zrd=low(others, piece, ff), zru=low(others, piece, ff), zro=low(others, slab, width),
        zra=low(others, piece, nh), zrb=low(others, piece, nh), gin=low(2, PADS, width),
    )
    small = [(piece, ff), (piece, ff), (slab, width), (piece, nh), (piece, nh)]
    vmem_out = dict(
        zip(("td", "tu", "to", "ta", "tb"), [wide(*d) if parts > 1 else wide(8, 128) for d in small]),
        rowt=wide(8, width), colt=wide(2, ff),
    )
    kept = dict(
        bv=low(*bias.shape), precv_f=tall, precv_m=tall, orecv=low(2, PADS, width), theirs=low(2, PADS, width),
        pr=tall, sbd=low(width, ff), rowb=wide(4, 8, width), colv=wide(2, ff), rr=wide(3, 8, width), cr=wide(4, 2, ff),
        rsum=wide(8, width), csum=wide(2, ff), rz=wide(peers, 8, width), cz=wide(peers, 2, ff),
    )
    sems = dict(
        ssem=(8,), rsem=(8,), csem=(3,), lsem=(4,), wsend=(4, 4), wrecv=(4, 4), msem_f=(12,),
        ssd=(4,), rsd=(6,), lsd=(6,), lsem_m=(2, 4), ps_m=(3,), pr_m=(3,), cs_m=(), msem_m=(11,),
        ssu=(4,), rsu=(6,), lsu=(6,), sso=(4,), rso=(6,), lso=(6,), ssa=(4,), rsa=(6,), lsa=(6,), ssb=(4,), rsb=(6,), lsb=(6,),
        lsem_b=(2, 4), zss=(5, others), zrs=(5, others), zls=(5, others + 1), es=(), er=(), hs=(), hr=(), cs=(),
        vs=(7,), vr=(7,), ws=(2, peers), wr=(2, peers), msem_b=(10,),
    )
    names = ["tok", "cot", "bias", "wq", "wo", "wu", "wd", *hbm, *vmem_out, *kept, *sems]

    def scoped(fn, shapes):
        pl.run_scoped(fn, *[pltpu.VMEM(d, t) for d, t in shapes])

    def kernel(*refs):
        r = types.SimpleNamespace(**dict(zip(names, refs)))
        x, k, y = spot = place()
        size, me = lax.axis_size("dp"), lax.axis_index("dp")
        plane = [at(1 - x, k, y), at(x, k, 1 - y), at(1 - x, k, 1 - y), at(x, 1 - k, y)]
        plane += [at(1 - x, 1 - k, y), at(x, 1 - k, 1 - y), at(1 - x, 1 - k, 1 - y)]
        greet(plane + [{"dp": lax.rem(me + o, size)} for o in range(1, size)])

        def first_ring():
            Scatter(r.dd, r.rd, None, None, r.sbd, None, r.ssd, r.rsd, r.lsd, spot).first()

        def second_ring():
            Scatter(r.du, r.ru, None, None, None, None, r.ssu, r.rsu, r.lsu, spot).first()

        scoped(
            lambda *v: forward_phase(
                r.tok, r.cot, r.bias, r.wq, r.wo, r.wu, r.wd,
                r.gq, r.go, r.gu, r.gd, r.xb, r.dyb, r.f1b, r.qh, r.oh, r.hflat, r.lse, r.residual, r.f2b,
                r.hidden, r.slope, r.dd, r.tbuf, r.cbuf, r.bv, r.precv_f,
                r.ssem, r.rsem, r.csem, r.lsem, r.wsend, r.wrecv, r.msem_f, spot, first_ring, *v,
            ),
            [hbm[n] for n in ("xb", "dyb", "f1b", "qh", "oh", "hflat", "lse", "residual", "f2b", "hidden", "slope", "dd")]
            + [rows4, low(full, nq), low(full, hw), low(full, ff), tall, tall],
        )

        def far_start():
            remote(r.theirs.at[1], r.outb.at[x], r.ps_m.at[2], r.pr_m.at[2], at(1 - x, k, y)).start()

        def later():
            far = at(1 - x, k, y)
            pltpu.make_async_copy(r.theirs.at[0], r.outb.at[x], r.cs_m).wait()
            remote(r.theirs.at[1], r.outb.at[1 - x], r.ps_m.at[2], r.pr_m.at[2], far).wait_recv()
            remote(r.theirs.at[1], r.outb.at[x], r.ps_m.at[2], r.pr_m.at[2], far).wait_send()

        scoped(
            lambda *v: middle_phase(
                r.dd, r.gd, r.wd, r.gu, r.wu, r.xb, r.dyb, r.residual, r.f2b, r.hidden, r.slope,
                r.rd, r.outb, r.du, r.dbr, r.dbrb, r.rowv, r.dbu, r.precv_m, r.orecv, r.theirs, r.sbd,
                r.ssd, r.rsd, r.lsd, r.lsem_m, r.ps_m, r.pr_m, r.cs_m, r.msem_m, spot, second_ring, *v,
            ),
            [hbm[n] for n in ("xb", "dyb", "residual", "f2b", "hidden", "slope", "du", "dbr", "dbrb", "rowv", "dbu")]
            + [wide(4, 8, full), tall, low(full, ff), low(full, ff), low(PADS, ff), low(2, PADS, width), wide(PADS, full),
               low(3, width, ff)],
        )
        scoped(
            lambda *v: backward_phase(
                r.du, r.dd, r.rd, r.go, r.wo, r.gq, r.wq, r.xb, r.f1b, r.hflat, r.qh, r.oh, r.lse, r.dbr, r.dbrb, r.rowv, r.dbu,
                r.zsd, r.ru, r.zsu, r.ro, r.zso, r.ra, r.zsa, r.rb, r.zsb, r.zrd, r.zru, r.zro, r.zra, r.zrb, r.gin,
                r.td, r.tu, r.to, r.ta, r.tb, r.rowt, r.colt,
                r.pr, r.sbd, r.rowb, r.colv, r.rr, r.cr, r.rsum, r.csum, r.rz, r.cz,
                r.ssu, r.rsu, r.lsu, r.sso, r.rso, r.lso, r.ssa, r.rsa, r.lsa, r.ssb, r.rsb, r.lsb, r.ssd, r.rsd,
                r.lsem_b, r.zss, r.zrs, r.zls, r.es, r.er, r.hs, r.hr, r.cs, r.vs, r.vr, r.ws, r.wr, r.msem_b,
                spot, later, far_start, *v,
            ),
            [hbm[n] for n in ("xb", "f1b", "hflat", "dbr", "dbrb", "rowv", "dbu")]
            + [wide(2, 8, full), low(full, hw), low(PADS, nq), low(4, hw, width), low(2, 4, width, nh)]
            + [low(3, width, ff), low(width, ff), low(2, parts, piece, ff)]
            + [low(3, hw, width), low(hw, width), low(2, parts, slab, width)]
            + [low(3, width, nh), low(width, nh), low(2, parts, piece, nh), low(width, nh), low(2, parts, piece, nh)],
        )

    anyspec = pl.BlockSpec(memory_space=pl.ANY)
    outs = pl.pallas_call(
        kernel,
        out_shape=[jax.ShapeDtypeStruct(*v) for v in (*hbm.values(), *vmem_out.values())],
        in_specs=[anyspec] * 7,
        out_specs=[anyspec] * len(hbm) + [pl.BlockSpec(memory_space=pltpu.VMEM)] * len(vmem_out),
        scratch_shapes=[pltpu.VMEM(*v) for v in kept.values()] + [pltpu.SemaphoreType.DMA(v) for v in sems.values()],
        compiler_params=pltpu.CompilerParams(collective_id=0, has_side_effects=True, vmem_limit_bytes=VMEM_CAP),
        name="layer",
    )(tok, cot, bias, wq, wo, wu, wd)
    return types.SimpleNamespace(**dict(zip((*hbm, *vmem_out), outs)))


def shards(tokens, ln_gain, ln_bias, w_qkv, b_qv, w_out, b_out, w_up, b_up, w_down, b_down, cotangent):
    width = tokens.shape[1]
    hw = b_qv.shape[1]

    images = tokens.shape[0] // SEQ
    ff = b_up.shape[0]
    nq, hh = padded(hw), hw // 2

    def put(a, shape, *spot):
        a = a.reshape((1,) * (len(shape) - a.ndim) + a.shape)
        return jnp.pad(a, [(lo, n - m - lo) for lo, n, m in zip(spot, shape, a.shape)])

    wide = (images, PADS, width)
    vectors = sum(
        put(v, (PADS, width), SEQ + i, 0) for i, v in enumerate((ln_gain[0], ln_gain[1], ln_bias[0], ln_bias[1], b_out, b_down))
    )

    def halves(a):
        return sum(put(a[i * SEQ : (i + 1) * SEQ], wide, i, 0, 0) for i in range(images))

    tok2, cot2 = halves(tokens) + vectors[None], halves(cotangent)
    bias = put(b_up, (16, ff), 1, 0)
    for i in range(2):
        for p in (0, 2):
            bias += put(b_qv[p // 2, i * hh : (i + 1) * hh], (16, ff), 0, i * nq // 2 + p * hh)
    gap = jnp.zeros((nq // 2 - 3 * hh,), BF)
    side = jnp.zeros((width, gap.shape[0]), BF)
    qblock = jnp.concatenate(
        [w_qkv[:, p, i * hh : (i + 1) * hh] if p < 3 else side for i in range(2) for p in range(4)], axis=1
    )
    wot, wdt = w_out.T, w_down.T
    dp_size = lax.axis_size("dp")
    parts = dp_size if width % dp_size == 0 and (width // dp_size) % 8 == 0 else 1
    r = layer(parts, tok2, cot2, bias, qblock, wot, w_up, wdt)
    output = jnp.concatenate([r.outb[i, :SEQ] for i in range(images)])
    input_grad = jnp.concatenate([r.gin[i, :SEQ] for i in range(images)])
    td, tu, to, ta, tb, rowt, colt = r.td, r.tu, r.to, r.ta, r.tb, r.rowt, r.colt
    if parts == 1:

        def over_dp(a):
            return lax.psum_scatter(a[0], "dp", scatter_dimension=0, tiled=True).astype(F32)

        td, tu, to, ta, tb = (over_dp(a) for a in (r.zsd, r.zsu, r.zso, r.zsa, r.zsb))

    return (
        output,
        input_grad,
        rowt[0:2],
        rowt[2:4],
        jnp.concatenate([a[:, : 3 * hh].reshape(-1, 3, hh) for a in (ta, tb)], axis=2),
        jnp.stack(
            [jnp.concatenate([colt[0, i * nq // 2 + p * hh :][:hh] for i in range(2)]) for p in (0, 2)]
        ),
        to,
        rowt[4],
        tu,
        colt[1],
        td.T,
        rowt[5],
    )


def solution(mesh):
    placed = (
        P(("dp", "col"), "row"),
        P(None, "row"),
        P(None, "row"),
        P("row", None, "col"),
        P(None, "col"),
        P("col", "row"),
        P("row"),
        P("row", "col"),
        P("col"),
        P("col", "row"),
        P("row"),
        P(("dp", "col"), "row"),
    )
    return jax.shard_map(
        shards,
        mesh=mesh,
        in_specs=placed,
        out_specs=(
            P(("dp", "col"), "row"),
            P(("dp", "col"), "row"),
            P(None, "row"),
            P(None, "row"),
            P(("row", "dp"), None, "col"),
            P(None, "col"),
            P(("col", "dp"), "row"),
            P("row"),
            P(("row", "dp"), "col"),
            P("col"),
            P("col", ("row", "dp")),
            P("row"),
        ),
        check_vma=False,
    )
```
